32 devices in a mesh: dp: 8 (over y, x, core), tensor: 4 (over z).
Axes of the slice: x: 2, y: 2, z: 4, core: 2. Of those that a mesh axis runs over, the one named last changes fastest.
Arguments:
- tokens: bfloat16 [8192, 2048], P(('dp', 'tensor')), may hold values from -40 to 40
- cotangent: bfloat16 [8192, 2048], P(('dp', 'tensor')), may hold values from -6 to 6
- norm1_gain: bfloat16 [2048], replicated, may hold values from 0.5 to 1.5
- w_query: bfloat16 [2048, 2048], P(None, 'tensor'), may hold values from -0.125 to 0.125
- w_key: bfloat16 [2048, 512], P(None, 'tensor'), may hold values from -0.125 to 0.125
- w_value: bfloat16 [2048, 512], P(None, 'tensor'), may hold values from -0.125 to 0.125
- w_output: bfloat16 [2048, 2048], P('tensor'), may hold values from -1 to 1
- norm2_gain: bfloat16 [2048], replicated, may hold values from 0.5 to 1.5
- w_gate: bfloat16 [2048, 8192], P(None, 'tensor'), may hold values from -0.125 to 0.125
- w_up: bfloat16 [2048, 8192], P(None, 'tensor'), may hold values from -0.125 to 0.125
- w_down: bfloat16 [8192, 2048], P('tensor'), may hold values from -0.0625 to 0.0625
Outputs:
- output: bfloat16 [8192, 2048], P(('dp', 'tensor'))
- input_grad: bfloat16 [8192, 2048], P(('dp', 'tensor'))
- grad_norm1: float32 [2048], replicated
- grad_query: float32 [2048, 2048], P(None, 'tensor')
- grad_key: float32 [2048, 512], P(None, 'tensor')
- grad_value: float32 [2048, 512], P(None, 'tensor')
- grad_output: float32 [2048, 2048], P('tensor')
- grad_norm2: float32 [2048], replicated
- grad_gate: float32 [2048, 8192], P(None, 'tensor')
- grad_up: float32 [2048, 8192], P(None, 'tensor')
- grad_down: float32 [8192, 2048], P('tensor')
The draws below stay inside these ranges and needn't reach their ends.
All inputs are finite; a program needn't handle non-finite values.
Results may differ from the reference program's by a relative error of at most 0.022.
Values may be sent and summed in bfloat16 or wider, within the bound.
No kernel may reach another device: no remote copies, remote signals or barrier semaphores. Data moves between devices by JAX's collectives and lax.ppermute only.
A program may use at most 384 MiB of HBM per device.

```python
import jax
import jax.numpy as jnp
from jax import lax

D = 2048
HQ = 32
KV = 8
HD = 64
FF = 8192
SEQLEN = 512
SEQ_DEV = 2
TOKENS = 8192
N_DP = 8
N_TENSOR = 4


def draw_tokens(key, part):
    key_base, key_rows, key_cols = jax.random.split(key, 3)
    base_draw = jnp.clip(jax.random.normal(key_base, (TOKENS, D), jnp.float32), -4.0, 4.0)
    row_scale = jnp.exp(jax.random.uniform(key_rows, (TOKENS, 1), jnp.float32, -1.15, 1.15))
    col_scale = jnp.exp(jax.random.uniform(key_cols, (1, D), jnp.float32, -1.15, 1.15))
    return (base_draw * row_scale * col_scale).astype(jnp.bfloat16)


def levels(stream_key, extent, cuts, least, largest):
    gain, own = 1.0, jax.random.fold_in(stream_key, 6)
    for axis_at, blocks in cuts:
        heights = jnp.exp(jax.random.uniform(jax.random.fold_in(own, axis_at), (blocks,), jnp.float32, least / len(cuts), largest / len(cuts)))
        gain = gain * jnp.repeat(heights, extent[axis_at] // blocks).reshape([-1 if axis == axis_at else 1 for axis in range(len(extent))])
    return gain


def bell_draw(own_key, shape, deviation, limit, cuts=(), held_as=jnp.bfloat16):
    gain = levels(own_key, shape, cuts, -0.22, 0.18) if cuts else 1.0
    array = jax.random.normal(own_key, shape, jnp.float32) * deviation * gain
    return jnp.minimum(jnp.maximum(array, -limit), limit).astype(held_as)


def setup_inputs(seed: int = 0) -> dict:
    key_list = jax.random.split(jax.random.key(seed), 12)
    tokens = draw_tokens(jax.random.fold_in(key_list[11], 71), 0)
    cotangent = bell_draw(key_list[1], (TOKENS, D), 1.0, 6.0, ((0, 32),))
    norm1_gain = jnp.clip(1.0 + 0.1 * jax.random.normal(key_list[2], (D,), jnp.float32), 0.5, 1.5).astype(jnp.bfloat16)
    w_query = bell_draw(key_list[3], (D, HQ * HD), D ** -0.5, 0.125, ((1, 4),))
    w_key = bell_draw(key_list[4], (D, KV * HD), D ** -0.5, 0.125, ((1, 4),))
    w_value = bell_draw(key_list[5], (D, KV * HD), D ** -0.5, 0.125, ((1, 4),))
    w_output = bell_draw(key_list[6], (HQ * HD, D), (HQ * HD // 64) ** -0.5, 1.0, ((0, 4),))
    norm2_gain = jnp.clip(1.0 + 0.1 * jax.random.normal(key_list[7], (D,), jnp.float32), 0.5, 1.5).astype(jnp.bfloat16)
    w_gate = bell_draw(key_list[8], (D, FF), D ** -0.5, 0.125, ((1, 4),))
    w_up = bell_draw(key_list[9], (D, FF), D ** -0.5, 0.125, ((1, 4),))
    w_down = bell_draw(key_list[10], (FF, D), FF ** -0.5, 0.0625, ((0, 4),))
    return {"tokens": tokens, "cotangent": cotangent, "norm1_gain": norm1_gain, "w_query": w_query, "w_key": w_key, "w_value": w_value, "w_output": w_output, "norm2_gain": norm2_gain, "w_gate": w_gate, "w_up": w_up, "w_down": w_down}


@jax.custom_vjp
def low(v):
    return lax.optimization_barrier(v.astype(jnp.bfloat16)).astype(jnp.float32)

@jax.custom_vjp
def low_back(v):
    return v

def low_keep(v):
    return (low(v), None)

def low_pass(kept, grad):
    return (grad,)

def back_keep(v):
    return (v, None)

def back_low(kept, grad):
    return (low(grad),)
low.defvjp(low_keep, low_pass)
low_back.defvjp(back_keep, back_low)
EPS = 1e-05
ROPE_BASE = 500000.0
HIGHEST = lax.Precision.HIGHEST
MASKED = -1e+30

def rope_tables(length, columns):
    half_width = columns // 2
    frequency = ROPE_BASE ** (-(jnp.arange(half_width, dtype=jnp.float32) * 2.0 / columns))
    angles = jnp.arange(length, dtype=jnp.float32)[:, None] * frequency[None, :]
    return (jnp.cos(angles), jnp.sin(angles))

def rotate(values, cos_table, sin_table):
    half_width = values.shape[-1] // 2
    table_shape = (cos_table.shape[0],) + (1,) * (values.ndim - 3) + (half_width,)
    cos_table = cos_table.reshape(table_shape)
    sin_table = sin_table.reshape(table_shape)
    first_half = values[..., :half_width]
    second_half = values[..., half_width:]
    return jnp.concatenate([first_half * cos_table - second_half * sin_table, second_half * cos_table + first_half * sin_table], axis=-1)

def rms_norm(values, gain_vec):
    row_scale = lax.rsqrt(lax.optimization_barrier(jnp.mean(values * values, axis=-1, keepdims=True)) + EPS)
    return values * row_scale * gain_vec

def shard_project(copies, weight):
    shards = copies.shape[0]
    columns = weight.shape[1] // shards
    split_weight = weight.reshape(weight.shape[0], shards, columns)
    product = jnp.einsum('kgd,dkc->gkc', copies, split_weight, precision=HIGHEST)
    return product.reshape(copies.shape[1], shards * columns)

def shard_reduce(inputs, weight):
    shards = N_TENSOR
    per_shard = inputs.shape[1] // shards
    pieces = inputs.reshape(inputs.shape[0], shards, per_shard)
    split_weight = weight.reshape(shards, per_shard, weight.shape[1])
    partial_sums = low(low_back(jnp.einsum('gkc,kcd->kgd', pieces, split_weight, precision=HIGHEST)))
    return lax.optimization_barrier(jnp.sum(partial_sums, axis=0))

def block_forward(tokens, norm1_gain, w_query, w_key, w_value, w_output, norm2_gain, w_gate, w_up, w_down):
    all_rows = tokens.shape[0]
    seq_count = all_rows // SEQLEN
    group_size = HQ // KV
    normed1 = low(rms_norm(tokens, norm1_gain))
    copies1 = low_back(jnp.broadcast_to(normed1[None], (N_TENSOR, all_rows, D)))
    query_pre = low_back(shard_project(copies1, w_query)).reshape(seq_count, SEQLEN, HQ, HD)
    key_pre = low_back(shard_project(copies1, w_key)).reshape(seq_count, SEQLEN, KV, HD)
    value_all = low(low_back(shard_project(copies1, w_value))).reshape(seq_count, SEQLEN, KV, HD)
    cos_table, sin_table = rope_tables(SEQLEN, HD)
    query_rot = low(rotate(query_pre, cos_table, sin_table)).reshape(seq_count, SEQLEN, KV, group_size, HD)
    key_rot = low(rotate(key_pre, cos_table, sin_table))
    scores = low_back(jnp.einsum('sqhgd,skhd->shgqk', query_rot, key_rot, precision=HIGHEST) * HD ** (-0.5))
    positions = jnp.arange(SEQLEN)
    causal = positions[:, None] >= positions[None, :]
    scores = jnp.where(causal, scores, MASKED)
    attn_probs = jax.nn.softmax(scores, axis=-1)
    mixed_heads = jnp.einsum('shgqk,skhd->sqhgd', low(attn_probs), value_all, precision=HIGHEST)
    heads_out = low(low_back(mixed_heads)).reshape(all_rows, HQ * HD)
    hidden_state = tokens + shard_reduce(heads_out, w_output)
    normed2 = low(rms_norm(hidden_state, norm2_gain))
    copies2 = low_back(jnp.broadcast_to(normed2[None], (N_TENSOR, all_rows, D)))
    gate_proj = low_back(shard_project(copies2, w_gate))
    up_proj = low_back(shard_project(copies2, w_up))
    activated = low(jax.nn.silu(gate_proj) * up_proj)
    return low(hidden_state + shard_reduce(activated, w_down))

def reference(tokens, cotangent, norm1_gain, w_query, w_key, w_value, w_output, norm2_gain, w_gate, w_up, w_down):
    weights = tuple((member.astype(jnp.float32) for member in (norm1_gain, w_query, w_key, w_value, w_output, norm2_gain, w_gate, w_up, w_down)))
    group_rows = SEQ_DEV * SEQLEN
    token_groups = tokens.astype(jnp.float32).reshape(N_DP, group_rows, D)
    cot_groups = cotangent.astype(jnp.float32).reshape(N_DP, group_rows, D)

    def group_step(running, batch_pair):
        token_block, cot_block = batch_pair
        result, pull_back = jax.vjp(block_forward, token_block, *weights)
        gradients = pull_back(cot_block)
        running = tuple((accum + fresh for accum, fresh in zip(running, gradients[1:])))
        return (running, (result, gradients[0]))
    starting = tuple((jnp.zeros_like(member) for member in weights))
    totals, (outputs, input_grads) = lax.scan(group_step, starting, (token_groups, cot_groups))
    return (outputs.reshape(TOKENS, D).astype(jnp.bfloat16), input_grads.reshape(TOKENS, D).astype(jnp.bfloat16), totals[0], totals[1], totals[2], totals[3], totals[4], totals[5], totals[6], totals[7], totals[8])
```

```python
import jax
import jax.numpy as jnp
from jax import lax
from jax.experimental import pallas as pl
from jax.experimental.pallas import tpu as pltpu
from jax.sharding import PartitionSpec as P

HQ = 32
KV = 8
HD = 64
SEQLEN = 512


EPS = 1e-05
ROPE_BASE = 500000.0
MASKED = -1e30


def rope_tables(length, columns):
    half_width = columns // 2
    frequency = ROPE_BASE ** (-(jnp.arange(half_width, dtype=jnp.float32) * 2.0 / columns))
    angles = jnp.arange(length, dtype=jnp.float32)[:, None] * frequency[None, :]
    return (jnp.cos(angles), jnp.sin(angles))


def rotate(values, cos_table, sin_table):
    half_width = values.shape[-1] // 2
    table_shape = (cos_table.shape[0],) + (1,) * (values.ndim - 3) + (half_width,)
    cos_table = cos_table.reshape(table_shape)
    sin_table = sin_table.reshape(table_shape)
    first_half = values[..., :half_width]
    second_half = values[..., half_width:]
    return jnp.concatenate(
        [
            first_half * cos_table - second_half * sin_table,
            second_half * cos_table + first_half * sin_table,
        ],
        axis=-1,
    )


def rms_norm(values, gain_vec):
    row_scale = lax.rsqrt(jnp.mean(values * values, axis=-1, keepdims=True) + EPS)
    return values * row_scale * gain_vec


def norm_backward(values, gain_vec, upstream):
    _, pull_back = jax.vjp(lambda inner_values: rms_norm(inner_values, gain_vec), values)
    return pull_back(upstream)[0]


def gain_gradient(values, upstream):
    row_scale = lax.rsqrt(jnp.mean(values * values, axis=-1, keepdims=True) + EPS)
    return jnp.sum(upstream * values * row_scale, axis=0)


def contract_rows(left_side, right_side):
    return lax.dot_general(
        left_side, right_side, (((0,), (0,)), ((), ())), preferred_element_type=jnp.float32
    )


def contract_cols(left_side, right_side):
    return lax.dot_general(
        left_side, right_side, (((1,), (1,)), ((), ())), preferred_element_type=jnp.float32
    )


def gated_unit(gate_in, up_in):
    return jax.nn.silu(gate_in) * up_in


def line_reduce(partial, axis):
    n = lax.axis_size(axis)
    me = lax.axis_index(axis)
    rows = partial.shape[0] // n

    def block(index):
        return lax.dynamic_slice_in_dim(partial, jnp.clip(index, 0, n - 1) * rows, rows, 0)

    up = down = None
    for step in range(1, n):
        up_term = block(me + n - step)
        down_term = block(me - n + step)
        if up is not None:
            up_term = (up.astype(jnp.float32) + up_term.astype(jnp.float32)).astype(jnp.bfloat16)
            down_term = (down.astype(jnp.float32) + down_term.astype(jnp.float32)).astype(
                jnp.bfloat16
            )
        up = lax.ppermute(up_term, axis, [(i, i + 1) for i in range(min(step, n - 1))])
        down = lax.ppermute(down_term, axis, [(i, i - 1) for i in range(max(n - step, 1), n)])
    own = block(me).astype(jnp.float32)
    return own + up.astype(jnp.float32) + down.astype(jnp.float32)


def cube_share(piece, axis):
    n = lax.axis_size(axis)
    bits = [1 << b for b in range(n.bit_length() - 1)]
    outer, inner = bits[1:], bits[:1]

    def spread(block, order):
        have = {0: block}
        for bit in order:
            pairs = [(i, i ^ bit) for i in range(n)]
            have.update({k | bit: lax.ppermute(v, axis, pairs) for k, v in list(have.items())})
        return have

    half = piece.shape[1] // 2
    first = spread(piece[:, :half], outer + inner)
    second = spread(piece[:, half:], outer[::-1] + inner)
    return first, second


def place_blocks(shared, axis):
    n = lax.axis_size(axis)
    me = lax.axis_index(axis)
    first, second = shared
    rows, half = first[0].shape
    columns = 2 * half
    tile = min(rows, 128)
    steps = rows // tile

    def kernel(me_ref, *refs):
        out_ref = refs[-1]
        k = pl.program_id(0)
        for j in range(n):

            @pl.when(k == j)
            def _():
                out_ref[:, :half] = refs[2 * j][...].astype(jnp.float32)
                out_ref[:, half:] = refs[2 * j + 1][...].astype(jnp.float32)

    def source(j):
        def index(k, t, me_ref):
            return (jnp.where(k == j, t, jnp.where(k < j, 0, steps - 1)), 0)

        return pl.BlockSpec((tile, half), index)

    operands = []
    for j in range(n):
        operands += [first[j], second[j]]
    return pl.pallas_call(
        kernel,
        grid_spec=pltpu.PrefetchScalarGridSpec(
            num_scalar_prefetch=1,
            grid=(n, steps),
            in_specs=[source(j // 2) for j in range(2 * n)],
            out_specs=pl.BlockSpec(
                (tile, columns), lambda k, t, me_ref: ((me_ref[0] ^ k) * steps + t, 0)
            ),
        ),
        out_shape=jax.ShapeDtypeStruct((n * rows, columns), jnp.float32),
        cost_estimate=pl.CostEstimate(
            flops=0, transcendentals=0, bytes_accessed=6 * n * rows * columns
        ),
        name="place_blocks",
    )(me.reshape(1), *operands)


def scatter_sum(grad):
    return lax.psum_scatter(grad, "dp", scatter_dimension=0, tiled=True)


def cube_sum(vector, axes):
    for axis in axes:
        n = lax.axis_size(axis)
        bit = 1
        while bit < n:
            vector = vector + lax.ppermute(vector, axis, [(i, i ^ bit) for i in range(n)])
            bit *= 2
    return vector


def on_device(
    tokens,
    cotangent,
    norm1_gain,
    w_query,
    w_key,
    w_value,
    w_output,
    norm2_gain,
    w_gate,
    w_up,
    w_down,
):
    all_tokens, all_cot = (
        lax.all_gather(tokens, "tensor", axis=0, tiled=True),
        lax.all_gather(cotangent, "tensor", axis=0, tiled=True),
    )
    all_rows = all_tokens.shape[0]
    seq_count = all_rows // SEQLEN
    kv_heads = w_key.shape[1] // HD
    group_size = HQ // KV
    score_scale = HD ** (-0.5)
    gain_one = norm1_gain.astype(jnp.float32)
    gain_two = norm2_gain.astype(jnp.float32)
    token_values = all_tokens.astype(jnp.float32)
    own_tokens = tokens.astype(jnp.float32)
    normed1 = rms_norm(token_values, gain_one).astype(jnp.bfloat16)
    query_pre = jnp.dot(normed1, w_query, preferred_element_type=jnp.float32).reshape(
        seq_count, SEQLEN, kv_heads, group_size, HD
    )
    key_pre = jnp.dot(normed1, w_key, preferred_element_type=jnp.float32).reshape(
        seq_count, SEQLEN, kv_heads, HD
    )
    value_all = (
        jnp.dot(normed1, w_value, preferred_element_type=jnp.float32)
        .astype(jnp.bfloat16)
        .reshape(seq_count, SEQLEN, kv_heads, HD)
    )
    cos_table, sin_table = rope_tables(SEQLEN, HD)
    query_rot = rotate(query_pre, cos_table, sin_table).astype(jnp.bfloat16)
    key_rot = rotate(key_pre, cos_table, sin_table).astype(jnp.bfloat16)
    positions = jnp.arange(SEQLEN)
    causal = positions[:, None] >= positions[None, :]

    def masked_scores():
        raw_scores = (
            jnp.einsum("sqhgd,skhd->shgqk", query_rot, key_rot, preferred_element_type=jnp.float32)
            * score_scale
        )
        return jnp.where(causal, raw_scores, MASKED)

    scores = masked_scores()
    row_max = jnp.max(scores, axis=-1, keepdims=True)
    exp_scores = jnp.exp(scores - row_max)
    row_total = jnp.sum(exp_scores, axis=-1, keepdims=True)
    attn_probs = exp_scores / row_total
    log_total = row_max + jnp.log(row_total)
    mixed_heads = jnp.einsum(
        "shgqk,skhd->sqhgd",
        attn_probs.astype(jnp.bfloat16),
        value_all,
        preferred_element_type=jnp.float32,
    )
    heads_out = mixed_heads.astype(jnp.bfloat16).reshape(all_rows, kv_heads * group_size * HD)
    attn_part = jnp.dot(heads_out, w_output, preferred_element_type=jnp.float32)
    hidden_state = own_tokens + line_reduce(attn_part.astype(jnp.bfloat16), "tensor")
    normed2 = lax.all_gather(
        rms_norm(hidden_state, gain_two).astype(jnp.bfloat16), "tensor", axis=0, tiled=True
    )
    gate_proj = jnp.dot(normed2, w_gate, preferred_element_type=jnp.float32)
    up_proj = jnp.dot(normed2, w_up, preferred_element_type=jnp.float32)
    activated = gated_unit(gate_proj, up_proj).astype(jnp.bfloat16)
    mlp_part = jnp.dot(activated, w_down, preferred_element_type=jnp.float32)
    output = (hidden_state + line_reduce(mlp_part.astype(jnp.bfloat16), "tensor")).astype(
        jnp.bfloat16
    )
    grad_down = contract_rows(activated, all_cot).astype(jnp.bfloat16)
    d_activated = contract_cols(all_cot, w_down)
    _, pull_gated = jax.vjp(gated_unit, gate_proj, up_proj)
    d_gate, d_up = pull_gated(d_activated)
    d_gate = d_gate.astype(jnp.bfloat16)
    d_up = d_up.astype(jnp.bfloat16)
    grad_gate = contract_rows(normed2, d_gate).astype(jnp.bfloat16)
    grad_up = contract_rows(normed2, d_up).astype(jnp.bfloat16)
    dn2_part = contract_cols(d_gate, w_gate) + contract_cols(d_up, w_up)
    d_normed2 = line_reduce(dn2_part.astype(jnp.bfloat16), "tensor")
    d_state = cotangent.astype(jnp.float32) + norm_backward(hidden_state, gain_two, d_normed2)
    d_state_low = lax.all_gather(d_state.astype(jnp.bfloat16), "tensor", axis=0, tiled=True)
    grad_gain2 = gain_gradient(hidden_state, d_normed2)
    grad_output = contract_rows(heads_out, d_state_low)
    d_heads = (
        contract_cols(d_state_low, w_output)
        .astype(jnp.bfloat16)
        .reshape(seq_count, SEQLEN, kv_heads, group_size, HD)
    )
    probs_again = jnp.exp(masked_scores() - log_total)
    probs_low = probs_again.astype(jnp.bfloat16)
    d_value = (
        jnp.einsum("shgqk,sqhgd->skhd", probs_low, d_heads, preferred_element_type=jnp.float32)
        .astype(jnp.bfloat16)
        .reshape(all_rows, kv_heads * HD)
    )
    d_probs = jnp.einsum(
        "sqhgd,skhd->shgqk", d_heads, value_all, preferred_element_type=jnp.float32
    )
    d_scores = (
        probs_again * (d_probs - jnp.sum(probs_again * d_probs, axis=-1, keepdims=True))
    ).astype(jnp.bfloat16)
    d_query = (
        jnp.einsum("shgqk,skhd->sqhgd", d_scores, key_rot, preferred_element_type=jnp.float32)
        * score_scale
    )
    d_key = (
        jnp.einsum("shgqk,sqhgd->skhd", d_scores, query_rot, preferred_element_type=jnp.float32)
        * score_scale
    )
    d_query = (
        rotate(d_query, cos_table, -sin_table)
        .astype(jnp.bfloat16)
        .reshape(all_rows, kv_heads * group_size * HD)
    )
    d_key = (
        rotate(d_key, cos_table, -sin_table).astype(jnp.bfloat16).reshape(all_rows, kv_heads * HD)
    )
    grad_query = contract_rows(normed1, d_query)
    grad_key = contract_rows(normed1, d_key)
    grad_value = contract_rows(normed1, d_value)
    dn1_part = (
        contract_cols(d_query, w_query)
        + contract_cols(d_key, w_key)
        + contract_cols(d_value, w_value)
    )
    d_normed1 = line_reduce(dn1_part.astype(jnp.bfloat16), "tensor")
    input_grad = (d_state + norm_backward(own_tokens, gain_one, d_normed1)).astype(jnp.bfloat16)
    grad_gain1 = gain_gradient(own_tokens, d_normed1)
    gain_two_sum = cube_sum(grad_gain2, ("dp", "tensor"))
    gain_one_sum = cube_sum(grad_gain1, ("dp", "tensor"))

    def total(grad):
        return place_blocks(cube_share(scatter_sum(grad), "dp"), "dp")

    full_down = total(grad_down)
    gate_up = scatter_sum(jnp.concatenate([grad_gate, grad_up], axis=1))
    ff_columns = grad_gate.shape[1]
    full_gate = place_blocks(cube_share(gate_up[:, :ff_columns], "dp"), "dp")
    full_up = place_blocks(cube_share(gate_up[:, ff_columns:], "dp"), "dp")
    q_columns, k_columns = w_query.shape[1], w_key.shape[1]
    low_qkv = jnp.concatenate([grad_query, grad_key, grad_value], axis=1).astype(jnp.bfloat16)
    full_qkv = total(low_qkv)
    full_query = full_qkv[:, :q_columns]
    full_key = full_qkv[:, q_columns : q_columns + k_columns]
    full_value = full_qkv[:, q_columns + k_columns :]
    full_output = total(grad_output.astype(jnp.bfloat16))
    return (
        output,
        input_grad,
        gain_one_sum,
        full_query,
        full_key,
        full_value,
        full_output,
        gain_two_sum,
        full_gate,
        full_up,
        full_down,
    )


def solution(mesh):
    return jax.shard_map(
        on_device,
        mesh=mesh,
        in_specs=(
            P(("dp", "tensor"), None),
            P(("dp", "tensor"), None),
            P(),
            P(None, "tensor"),
            P(None, "tensor"),
            P(None, "tensor"),
            P("tensor", None),
            P(),
            P(None, "tensor"),
            P(None, "tensor"),
            P("tensor", None),
        ),
        out_specs=(
            P(("dp", "tensor"), None),
            P(("dp", "tensor"), None),
            P(),
            P(None, "tensor"),
            P(None, "tensor"),
            P(None, "tensor"),
            P("tensor", None),
            P(),
            P(None, "tensor"),
            P(None, "tensor"),
            P("tensor", None),
        ),
        check_vma=False,
    )
```

```python
import jax
import jax.numpy as jnp
from jax import lax
from jax.experimental import pallas as pl
from jax.experimental.pallas import tpu as pltpu
from jax.experimental.layout import Layout, with_layout_constraint
from jax.sharding import PartitionSpec as P


HQ = 32
KV = 8
HD = 64
SEQLEN = 512


EPS = 1e-05
ROPE_BASE = 500000.0
MASKED = -1e30


def rope_tables(length, columns):
    half_width = columns // 2
    frequency = ROPE_BASE ** (-(jnp.arange(half_width, dtype=jnp.float32) * 2.0 / columns))
    angles = jnp.arange(length, dtype=jnp.float32)[:, None] * frequency[None, :]
    return (jnp.cos(angles), jnp.sin(angles))


def rotate(values, cos_table, sin_table):
    half_width = values.shape[-1] // 2
    table_shape = (cos_table.shape[0],) + (1,) * (values.ndim - 3) + (half_width,)
    cos_table = cos_table.reshape(table_shape)
    sin_table = sin_table.reshape(table_shape)
    first_half = values[..., :half_width]
    second_half = values[..., half_width:]
    return jnp.concatenate(
        [
            first_half * cos_table - second_half * sin_table,
            second_half * cos_table + first_half * sin_table,
        ],
        axis=-1,
    )


def rms_norm(values, gain_vec):
    row_scale = lax.rsqrt(jnp.mean(values * values, axis=-1, keepdims=True) + EPS)
    return values * row_scale * gain_vec


def norm_backward(values, gain_vec, upstream):
    _, pull_back = jax.vjp(lambda inner_values: rms_norm(inner_values, gain_vec), values)
    return pull_back(upstream)[0]


def gain_gradient(values, upstream):
    row_scale = lax.rsqrt(jnp.mean(values * values, axis=-1, keepdims=True) + EPS)
    return jnp.sum(upstream * values * row_scale, axis=0)


def contract_rows(left_side, right_side):
    return lax.dot_general(
        left_side, right_side, (((0,), (0,)), ((), ())), preferred_element_type=jnp.float32
    )


def contract_cols(left_side, right_side):
    return lax.dot_general(
        left_side, right_side, (((1,), (1,)), ((), ())), preferred_element_type=jnp.float32
    )


def gated_unit(gate_in, up_in):
    return jax.nn.silu(gate_in) * up_in


def gather_rows(block, axis):
    return lax.all_gather(block, axis, axis=0, tiled=True)


def scatter_sum(partial, axis):
    return lax.psum_scatter(partial, axis, scatter_dimension=0, tiled=True)


def exchange_sum(partial, axis):
    n = lax.axis_size(axis)
    me = lax.axis_index(axis)
    rows = partial.shape[0] // n

    def block(index):
        return lax.dynamic_slice_in_dim(partial, index * rows, rows, 0)

    total = block(me).astype(jnp.float32)
    for hop in range(1, n):
        moved = lax.ppermute(block((me + hop) % n), axis, [(i, (i + hop) % n) for i in range(n)])
        total += moved.astype(jnp.float32)
    return total


def cube_gather(block, axis):
    n = lax.axis_size(axis)
    bits = [1 << b for b in range(n.bit_length() - 1)]
    half = block.shape[0] // 2
    halves = []
    for part, order in ((block[:half], bits[1:] + bits[:1]), (block[half:], bits[:0:-1] + bits[:1])):
        held, offsets = part[None], [0]
        for bit in order:
            moved = lax.ppermute(held, axis, [(i, i ^ bit) for i in range(n)])
            held = jnp.concatenate([held, moved], axis=0)
            offsets = offsets + [o ^ bit for o in offsets]
        halves.append((held, tuple(offsets)))
    return halves


def cube_sum(vector, axes):
    for axis in axes:
        n = lax.axis_size(axis)
        bit = 1
        while bit < n:
            vector = vector + lax.ppermute(vector, axis, [(i, i ^ bit) for i in range(n)])
            bit *= 2
    return vector


def project_and_norm(all_heads, weights, all_tokens, gain_vec):
    groups, rows, group_columns = all_heads.shape
    (first, first_offsets), (second, second_offsets) = weights
    parts, _, part_columns = first.shape
    width = all_tokens.shape[1]
    tile = rows // groups
    places = jnp.stack([lax.axis_index("tensor"), lax.axis_index("dp")])

    def kernel(
        at_ref, heads_ref, first_ref, second_ref, tokens_ref, gain_ref, hidden_ref, normed_ref, acc_ref
    ):
        step = pl.program_id(0)
        acc_ref[...] = tokens_ref[...].astype(jnp.float32)
        for half, (weight_ref, offsets) in enumerate(
            ((first_ref, first_offsets), (second_ref, second_offsets))
        ):
            for part in range(parts):
                start = (at_ref[1] ^ offsets[part]) * part_columns
                columns = pl.ds(pl.multiple_of(start, part_columns), part_columns)
                for g in range(groups // 2):
                    acc_ref[:, columns] += jnp.dot(
                        heads_ref[half * (groups // 2) + g],
                        weight_ref[part, g * group_columns : (g + 1) * group_columns, :],
                        preferred_element_type=jnp.float32,
                    )
        hidden = acc_ref[...]
        row_scale = lax.rsqrt(jnp.mean(hidden * hidden, axis=-1, keepdims=True) + EPS)
        normed_ref[...] = (hidden * row_scale * gain_ref[...].astype(jnp.float32)).astype(
            jnp.bfloat16
        )

        @pl.when(step == at_ref[0])
        def _():
            hidden_ref[...] = hidden

    return pl.pallas_call(
        kernel,
        grid_spec=pltpu.PrefetchScalarGridSpec(
            num_scalar_prefetch=1,
            grid=(groups,),
            in_specs=[
                pl.BlockSpec((groups, tile, group_columns), lambda i, at_ref: (0, i, 0)),
                pl.BlockSpec(first.shape, lambda i, at_ref: (0, 0, 0)),
                pl.BlockSpec(second.shape, lambda i, at_ref: (0, 0, 0)),
                pl.BlockSpec((tile, width), lambda i, at_ref: (i, 0)),
                pl.BlockSpec((1, width), lambda i, at_ref: (0, 0)),
            ],
            out_specs=[
                pl.BlockSpec((tile, width), lambda i, at_ref: (0, 0)),
                pl.BlockSpec((tile, width), lambda i, at_ref: (i, 0)),
            ],
            scratch_shapes=[pltpu.VMEM((tile, width), jnp.float32)],
        ),
        out_shape=[
            jax.ShapeDtypeStruct((tile, width), jnp.float32),
            jax.ShapeDtypeStruct((rows, width), jnp.bfloat16),
        ],
        cost_estimate=pl.CostEstimate(
            flops=2 * rows * width * width, transcendentals=rows, bytes_accessed=20 << 20
        ),
        name="project_and_norm",
    )(places, all_heads, first, second, all_tokens, gain_vec.reshape(1, -1))


def row_major(array):
    return with_layout_constraint(array, Layout(major_to_minor=tuple(range(array.ndim))))


def split_columns(array, parts):
    columns = array.shape[1] // parts
    return jnp.concatenate(
        [array[:, p * columns : (p + 1) * columns] for p in range(parts)], axis=0
    )


def join_columns(array, parts):
    rows = array.shape[0] // parts
    return jnp.concatenate([array[p * rows : (p + 1) * rows] for p in range(parts)], axis=1)


def block(
    tokens,
    cotangent,
    norm1_gain,
    w_query,
    w_key,
    w_value,
    w_output,
    norm2_gain,
    w_gate,
    w_up,
    w_down,
):
    low = jnp.bfloat16
    n_dp = lax.axis_size("dp")
    nothing = scatter_sum(tokens[:, :128] * 0, "dp")[0, 0]
    all_tokens = gather_rows(tokens, "tensor")
    part_columns = w_output.shape[1] // n_dp
    own_part = lax.dynamic_slice_in_dim(
        w_output, lax.axis_index("dp") * part_columns, part_columns, 1
    )
    part_output = gather_rows(own_part, "tensor")
    all_output = cube_gather(part_output, "dp")
    all_rows = all_tokens.shape[0]
    seq_count = all_rows // SEQLEN
    kv_heads = w_key.shape[1] // HD
    group_size = HQ // KV
    score_scale = HD ** (-0.5)
    gain_one = norm1_gain.astype(jnp.float32)
    gain_two = norm2_gain.astype(jnp.float32)
    token_values = all_tokens.astype(jnp.float32)
    own_tokens = tokens.astype(jnp.float32)
    normed1 = rms_norm(token_values, gain_one).astype(low)
    query_pre = jnp.dot(normed1, w_query, preferred_element_type=jnp.float32).reshape(
        seq_count, SEQLEN, kv_heads, group_size, HD
    )
    key_pre = jnp.dot(normed1, w_key, preferred_element_type=jnp.float32).reshape(
        seq_count, SEQLEN, kv_heads, HD
    )
    value_all = (
        jnp.dot(normed1, w_value, preferred_element_type=jnp.float32)
        .astype(low)
        .reshape(seq_count, SEQLEN, kv_heads, HD)
    )
    cos_table, sin_table = rope_tables(SEQLEN, HD)
    query_rot = rotate(query_pre, cos_table, sin_table).astype(low)
    key_rot = rotate(key_pre, cos_table, sin_table).astype(low)
    positions = jnp.arange(SEQLEN)
    causal = positions[:, None] >= positions[None, :]

    def masked_scores():
        raw_scores = (
            jnp.einsum("sqhgd,skhd->shgqk", query_rot, key_rot, preferred_element_type=jnp.float32)
            * score_scale
        )
        return jnp.where(causal, raw_scores, MASKED)

    scores = masked_scores()
    row_max = jnp.max(scores, axis=-1, keepdims=True)
    exp_scores = jnp.exp(scores - row_max)
    row_total = jnp.sum(exp_scores, axis=-1, keepdims=True)
    attn_probs = exp_scores / row_total
    log_total = row_max + jnp.log(row_total)
    mixed_heads = jnp.einsum(
        "shgqk,skhd->sqhgd", attn_probs.astype(low), value_all, preferred_element_type=jnp.float32
    )
    heads_out = mixed_heads.astype(low).reshape(all_rows, kv_heads * group_size * HD)
    all_heads = lax.all_gather(heads_out, "tensor", axis=0)
    all_cot = gather_rows(cotangent, "tensor")
    hidden_state, normed2 = project_and_norm(
        all_heads, all_output, all_tokens, (gain_two + nothing.astype(jnp.float32))
    )
    gate_proj = jnp.dot(normed2, w_gate, preferred_element_type=jnp.float32)
    up_proj = jnp.dot(normed2, w_up, preferred_element_type=jnp.float32)
    activated = gated_unit(gate_proj, up_proj).astype(low)
    d_activated = contract_cols(all_cot, w_down)
    _, pull_gated = jax.vjp(gated_unit, gate_proj, up_proj)
    d_gate, d_up = pull_gated(d_activated)
    d_gate = d_gate.astype(low)
    d_up = d_up.astype(low)
    ff_columns = w_gate.shape[1]
    ff_folds = w_gate.shape[0] // w_down.shape[0]
    grad_down = row_major(split_columns(contract_rows(activated, all_cot).astype(low), ff_folds))
    part_down = scatter_sum(grad_down, "dp")
    dn2_part = (contract_cols(d_gate, w_gate) + contract_cols(d_up, w_up)).astype(low)
    d_normed2 = exchange_sum(dn2_part, "tensor")
    gate_up_grads = row_major(
        jnp.concatenate(
            [contract_rows(normed2, d_gate).astype(low), contract_rows(normed2, d_up).astype(low)],
            axis=1,
        )
    )
    part_gate_up = scatter_sum(gate_up_grads, "dp")
    mlp_part = jnp.dot(activated, w_down, preferred_element_type=jnp.float32).astype(low)
    mlp_sum = exchange_sum(mlp_part, "tensor")
    output = (hidden_state + mlp_sum).astype(low)
    d_state = cotangent.astype(jnp.float32) + norm_backward(hidden_state, gain_two, d_normed2)
    d_state_low = gather_rows(d_state.astype(low), "tensor")
    gain_two_sum = cube_sum(gain_gradient(hidden_state, d_normed2), ("dp", "tensor"))
    d_heads = contract_cols(d_state_low, w_output).astype(low)
    d_heads = d_heads.reshape(seq_count, SEQLEN, kv_heads, group_size, HD)
    probs_again = jnp.exp(masked_scores() - log_total)
    probs_low = probs_again.astype(low)
    d_value = (
        jnp.einsum("shgqk,sqhgd->skhd", probs_low, d_heads, preferred_element_type=jnp.float32)
        .astype(low)
        .reshape(all_rows, kv_heads * HD)
    )
    d_probs = jnp.einsum(
        "sqhgd,skhd->shgqk", d_heads, value_all, preferred_element_type=jnp.float32
    )
    d_scores = (
        probs_again * (d_probs - jnp.sum(probs_again * d_probs, axis=-1, keepdims=True))
    ).astype(low)
    d_query = (
        jnp.einsum("shgqk,skhd->sqhgd", d_scores, key_rot, preferred_element_type=jnp.float32)
        * score_scale
    )
    d_key = (
        jnp.einsum("shgqk,sqhgd->skhd", d_scores, query_rot, preferred_element_type=jnp.float32)
        * score_scale
    )
    d_query = (
        rotate(d_query, cos_table, -sin_table)
        .astype(low)
        .reshape(all_rows, kv_heads * group_size * HD)
    )
    d_key = rotate(d_key, cos_table, -sin_table).astype(low).reshape(all_rows, kv_heads * HD)
    dn1_part = (
        contract_cols(d_query, w_query)
        + contract_cols(d_key, w_key)
        + contract_cols(d_value, w_value)
    ).astype(low)
    d_normed1 = exchange_sum(dn1_part, "tensor")
    gain_one_sum = cube_sum(
        gain_gradient(token_values, dn1_part.astype(jnp.float32)), ("dp", "tensor")
    )
    q_columns, k_columns = w_query.shape[1], w_key.shape[1]
    folds = w_query.shape[0] // w_output.shape[0]
    low_attn = row_major(
        jnp.concatenate(
            [
                contract_rows(normed1, d_query).astype(low),
                contract_rows(normed1, d_key).astype(low),
                contract_rows(normed1, d_value).astype(low),
                split_columns(contract_rows(heads_out, d_state_low).astype(low), folds),
            ],
            axis=1,
        )
    )
    part_attn = scatter_sum(low_attn, "dp")
    shared_ff = row_major(
        gather_rows(row_major(jnp.concatenate([part_gate_up, part_down], axis=1)), "dp")
    )
    shared_attn = row_major(gather_rows(part_attn, "dp"))
    input_grad = (d_state + norm_backward(own_tokens, gain_one, d_normed1)).astype(low)
    full_gate = shared_ff[:, :ff_columns].astype(jnp.float32)
    full_up = shared_ff[:, ff_columns : 2 * ff_columns].astype(jnp.float32)
    full_down = join_columns(shared_ff[:, 2 * ff_columns :], ff_folds).astype(jnp.float32)
    ends = (q_columns, q_columns + k_columns, q_columns + 2 * k_columns)
    full_query = shared_attn[:, : ends[0]].astype(jnp.float32)
    full_key = shared_attn[:, ends[0] : ends[1]].astype(jnp.float32)
    full_value = shared_attn[:, ends[1] : ends[2]].astype(jnp.float32)
    full_output = join_columns(shared_attn[:, ends[2] :], folds).astype(jnp.float32)
    return (
        output,
        input_grad,
        gain_one_sum,
        full_query,
        full_key,
        full_value,
        full_output,
        gain_two_sum,
        full_gate,
        full_up,
        full_down,
    )


def solution(mesh):
    return jax.shard_map(
        block,
        mesh=mesh,
        in_specs=(
            P(("dp", "tensor"), None),
            P(("dp", "tensor"), None),
            P(),
            P(None, "tensor"),
            P(None, "tensor"),
            P(None, "tensor"),
            P("tensor", None),
            P(),
            P(None, "tensor"),
            P(None, "tensor"),
            P("tensor", None),
        ),
        out_specs=(
            P(("dp", "tensor"), None),
            P(("dp", "tensor"), None),
            P(),
            P(None, "tensor"),
            P(None, "tensor"),
            P(None, "tensor"),
            P("tensor", None),
            P(),
            P(None, "tensor"),
            P(None, "tensor"),
            P("tensor", None),
        ),
        check_vma=False,
    )
```

```python
import functools

import jax
import jax.numpy as jnp
from jax import lax
from jax.experimental import pallas as pl
from jax.experimental.pallas import tpu as pltpu
from jax.experimental.layout import Layout, with_layout_constraint
from jax.sharding import PartitionSpec as P


HD = 64
SEQLEN = 512


EPS = 1e-05
ROPE_BASE = 500000.0
MASKED = -1e30


def rope_tables(length, columns):
    half_width = columns // 2
    frequency = ROPE_BASE ** (-(jnp.arange(half_width, dtype=jnp.float32) * 2.0 / columns))
    angles = jnp.arange(length, dtype=jnp.float32)[:, None] * frequency[None, :]
    return (jnp.cos(angles), jnp.sin(angles))


def rms_norm(values, gain_vec):
    row_scale = lax.rsqrt(jnp.mean(values * values, axis=-1, keepdims=True) + EPS)
    return values * row_scale * gain_vec


def norm_backward(values, gain_vec, upstream):
    _, pull_back = jax.vjp(lambda inner_values: rms_norm(inner_values, gain_vec), values)
    return pull_back(upstream)[0]


def gain_gradient(values, upstream):
    row_scale = lax.rsqrt(jnp.mean(values * values, axis=-1, keepdims=True) + EPS)
    return jnp.sum(upstream * values * row_scale, axis=0)


def contract_rows(left_side, right_side):
    return lax.dot_general(
        left_side, right_side, (((0,), (0,)), ((), ())), preferred_element_type=jnp.float32
    )


def contract_cols(left_side, right_side):
    return lax.dot_general(
        left_side, right_side, (((1,), (1,)), ((), ())), preferred_element_type=jnp.float32
    )


def gated_unit(gate_in, up_in):
    return jax.nn.silu(gate_in) * up_in


def gather_rows(block, axis):
    return lax.all_gather(block, axis, axis=0, tiled=True)


def scatter_sum(partial, axis):
    return lax.psum_scatter(partial, axis, scatter_dimension=0, tiled=True)


def exchange_sum(partial, axis):
    n = lax.axis_size(axis)
    me = lax.axis_index(axis)
    rows = partial.shape[0] // n

    def block(index):
        return lax.dynamic_slice_in_dim(partial, index * rows, rows, 0)

    total = block(me).astype(jnp.float32)
    for hop in range(1, n):
        moved = lax.ppermute(block((me + hop) % n), axis, [(i, (i + hop) % n) for i in range(n)])
        total += moved.astype(jnp.float32)
    return total


def cube_gather(block, axis):
    n = lax.axis_size(axis)
    bits = [1 << b for b in range(n.bit_length() - 1)]
    half = block.shape[0] // 2
    halves = []
    for part, order in ((block[:half], bits[1:] + bits[:1]), (block[half:], bits[:0:-1] + bits[:1])):
        held, offsets = part[None], [0]
        for bit in order:
            moved = lax.ppermute(held, axis, [(i, i ^ bit) for i in range(n)])
            held = jnp.concatenate([held, moved], axis=0)
            offsets = offsets + [o ^ bit for o in offsets]
        halves.append((held, tuple(offsets)))
    return halves


def cube_sum(vector, axes):
    for axis in axes:
        n = lax.axis_size(axis)
        bit = 1
        while bit < n:
            vector = vector + lax.ppermute(vector, axis, [(i, i ^ bit) for i in range(n)])
            bit *= 2
    return vector


def rotate_rows(values, cos_rows, sin_rows):
    half = HD // 2
    heads = []
    for h in range(values.shape[0] // HD):
        upper = values[h * HD : h * HD + half]
        lower = values[h * HD + half : (h + 1) * HD]
        heads.append(upper * cos_rows - lower * sin_rows)
        heads.append(lower * cos_rows + upper * sin_rows)
    return jnp.concatenate(heads, axis=0)


def dot_lanes(left_side, right_side):
    return lax.dot_general(
        left_side, right_side, (((1,), (1,)), ((), ())), preferred_element_type=jnp.float32
    )


def norm_project(all_tokens, gain_vec, weight_rows, cos_rows, sin_rows, rotated):
    rows, width = all_tokens.shape
    columns = weight_rows.shape[0]
    tile = 256

    def kernel(tokens_ref, gain_ref, weight_ref, cos_ref, sin_ref, normed_ref, out_ref):
        values = tokens_ref[...].astype(jnp.float32)
        row_scale = lax.rsqrt(jnp.mean(values * values, axis=-1, keepdims=True) + EPS)
        normed = (values * row_scale * gain_ref[...].astype(jnp.float32)).astype(jnp.bfloat16)
        normed_ref[...] = normed
        projected = dot_lanes(weight_ref[...], normed)
        out_ref[:rotated] = rotate_rows(projected[:rotated], cos_ref[...], sin_ref[...]).astype(
            jnp.bfloat16
        )
        out_ref[rotated:] = projected[rotated:].astype(jnp.bfloat16)

    half = HD // 2
    return pl.pallas_call(
        kernel,
        grid=(rows // tile,),
        in_specs=[
            pl.BlockSpec((tile, width), lambda i: (i, 0)),
            pl.BlockSpec((1, width), lambda i: (0, 0)),
            pl.BlockSpec((columns, width), lambda i: (0, 0)),
            pl.BlockSpec((half, tile), lambda i: (0, i % (SEQLEN // tile))),
            pl.BlockSpec((half, tile), lambda i: (0, i % (SEQLEN // tile))),
        ],
        out_specs=[
            pl.BlockSpec((tile, width), lambda i: (i, 0)),
            pl.BlockSpec((columns, tile), lambda i: (0, i)),
        ],
        out_shape=[
            jax.ShapeDtypeStruct((rows, width), jnp.bfloat16),
            jax.ShapeDtypeStruct((columns, rows), jnp.bfloat16),
        ],
        cost_estimate=pl.CostEstimate(
            flops=2 * rows * width * columns, transcendentals=rows, bytes_accessed=12 << 20
        ),
        name="norm_project",
    )(all_tokens, gain_vec.reshape(1, -1), weight_rows, cos_rows, sin_rows)


def key_tiles(step, tile):
    return [(t * tile, t == step) for t in range(step + 1)]


def causal_tile(tile):
    key_at = lax.broadcasted_iota(jnp.int32, (tile, tile), 0)
    query_at = lax.broadcasted_iota(jnp.int32, (tile, tile), 1)
    return key_at <= query_at


def attend(projected, q_heads, kv_heads):
    rows = projected.shape[1]
    group = q_heads // kv_heads
    wide = group * HD
    tile = 256
    score_scale = HD ** (-0.5)

    def kernel(query_ref, key_ref, value_ref, heads_ref, heads_t_ref, total_ref):
        keys = key_ref[...].astype(jnp.float32).T.astype(jnp.bfloat16)
        visible = causal_tile(tile)
        for step in range(SEQLEN // tile):
            here = slice(step * tile, (step + 1) * tile)
            for h in range(group):
                query = query_ref[h * HD : (h + 1) * HD, here]
                parts = []
                for start, masked in key_tiles(step, tile):
                    part = jnp.dot(
                        keys[start : start + tile], query, preferred_element_type=jnp.float32
                    )
                    parts.append(jnp.where(visible, part, MASKED) if masked else part)
                top = functools.reduce(
                    jnp.maximum, [jnp.max(part, axis=0, keepdims=True) for part in parts]
                )
                parts = [jnp.exp((part - top) * score_scale) for part in parts]
                total = sum(jnp.sum(part, axis=0, keepdims=True) for part in parts)
                inverse = 1.0 / total
                mixed = sum(
                    jnp.dot(
                        value_ref[:, start : start + tile],
                        (part * inverse).astype(jnp.bfloat16),
                        preferred_element_type=jnp.float32,
                    )
                    for part, (start, _) in zip(parts, key_tiles(step, tile))
                )
                heads_t_ref[h * HD : (h + 1) * HD, here] = mixed.astype(jnp.bfloat16)
                total_ref[0, h : h + 1, here] = top * score_scale + jnp.log(total)
        heads_ref[...] = heads_t_ref[...].astype(jnp.float32).T.astype(jnp.bfloat16)

    return pl.pallas_call(
        kernel,
        grid=(rows // SEQLEN, kv_heads),
        in_specs=[
            pl.BlockSpec((wide, SEQLEN), lambda s, j: (j, s)),
            pl.BlockSpec((HD, SEQLEN), lambda s, j: (q_heads + j, s)),
            pl.BlockSpec((HD, SEQLEN), lambda s, j: (q_heads + kv_heads + j, s)),
        ],
        out_specs=[
            pl.BlockSpec((SEQLEN, wide), lambda s, j: (s, j)),
            pl.BlockSpec((wide, SEQLEN), lambda s, j: (j, s)),
            pl.BlockSpec((1, group, SEQLEN), lambda s, j: (j, 0, s)),
        ],
        out_shape=[
            jax.ShapeDtypeStruct((rows, q_heads * HD), jnp.bfloat16),
            jax.ShapeDtypeStruct((q_heads * HD, rows), jnp.bfloat16),
            jax.ShapeDtypeStruct((kv_heads, group, rows), jnp.float32),
        ],
        cost_estimate=pl.CostEstimate(
            flops=4 * rows * SEQLEN * q_heads * HD,
            transcendentals=rows * SEQLEN * q_heads,
            bytes_accessed=4 << 20,
        ),
        name="attend",
    )(projected, projected, projected)


def attend_back(projected, d_heads, totals, cos_rows, sin_rows, q_heads, kv_heads):
    rows = projected.shape[1]
    group = q_heads // kv_heads
    wide = group * HD
    tile = 256
    score_scale = HD ** (-0.5)

    def kernel(
        query_ref,
        key_ref,
        value_ref,
        d_heads_ref,
        total_ref,
        cos_ref,
        sin_ref,
        d_query_ref,
        d_key_ref,
        d_value_ref,
        key_sum,
        value_sum,
    ):
        keys = key_ref[...].astype(jnp.float32).T.astype(jnp.bfloat16)
        values = value_ref[...].astype(jnp.float32).T.astype(jnp.bfloat16)
        visible = causal_tile(tile)
        key_sum[...] = jnp.zeros_like(key_sum)
        value_sum[...] = jnp.zeros_like(value_sum)
        for step in range(SEQLEN // tile):
            here = slice(step * tile, (step + 1) * tile)
            for h in range(group):
                query = query_ref[h * HD : (h + 1) * HD, here]
                d_head = d_heads_ref[h * HD : (h + 1) * HD, here]
                log_total = total_ref[0, h : h + 1, here]
                probs, d_probs = [], []
                for start, masked in key_tiles(step, tile):
                    span = slice(start, start + tile)
                    part = jnp.dot(keys[span], query, preferred_element_type=jnp.float32)
                    part = jnp.exp(part * score_scale - log_total)
                    if masked:
                        part = jnp.where(visible, part, 0.0)
                    probs.append(part)
                    value_sum[:, span] += dot_lanes(d_head, part.astype(jnp.bfloat16))
                    d_probs.append(
                        jnp.dot(values[span], d_head, preferred_element_type=jnp.float32)
                    )
                row_sum = sum(
                    jnp.sum(part * d_part, axis=0, keepdims=True)
                    for part, d_part in zip(probs, d_probs)
                )
                d_query = jnp.zeros((HD, tile), jnp.float32)
                for (start, _), part, d_part in zip(key_tiles(step, tile), probs, d_probs):
                    span = slice(start, start + tile)
                    d_scores = (part * (d_part - row_sum)).astype(jnp.bfloat16)
                    d_query += jnp.dot(
                        key_ref[:, span], d_scores, preferred_element_type=jnp.float32
                    )
                    key_sum[:, span] += dot_lanes(query, d_scores)
                d_query_ref[h * HD : (h + 1) * HD, here] = rotate_rows(
                    d_query * score_scale, cos_ref[:, here], -sin_ref[:, here]
                ).astype(jnp.bfloat16)
        d_key_ref[...] = rotate_rows(
            key_sum[...] * score_scale, cos_ref[...], -sin_ref[...]
        ).astype(jnp.bfloat16)
        d_value_ref[...] = value_sum[...].astype(jnp.bfloat16)

    half = HD // 2
    return pl.pallas_call(
        kernel,
        grid=(rows // SEQLEN, kv_heads),
        in_specs=[
            pl.BlockSpec((wide, SEQLEN), lambda s, j: (j, s)),
            pl.BlockSpec((HD, SEQLEN), lambda s, j: (q_heads + j, s)),
            pl.BlockSpec((HD, SEQLEN), lambda s, j: (q_heads + kv_heads + j, s)),
            pl.BlockSpec((wide, SEQLEN), lambda s, j: (j, s)),
            pl.BlockSpec((1, group, SEQLEN), lambda s, j: (j, 0, s)),
            pl.BlockSpec((half, SEQLEN), lambda s, j: (0, 0)),
            pl.BlockSpec((half, SEQLEN), lambda s, j: (0, 0)),
        ],
        out_specs=[
            pl.BlockSpec((wide, SEQLEN), lambda s, j: (j, s)),
            pl.BlockSpec((HD, SEQLEN), lambda s, j: (j, s)),
            pl.BlockSpec((HD, SEQLEN), lambda s, j: (j, s)),
        ],
        out_shape=[
            jax.ShapeDtypeStruct((q_heads * HD, rows), jnp.bfloat16),
            jax.ShapeDtypeStruct((kv_heads * HD, rows), jnp.bfloat16),
            jax.ShapeDtypeStruct((kv_heads * HD, rows), jnp.bfloat16),
        ],
        scratch_shapes=[
            pltpu.VMEM((HD, SEQLEN), jnp.float32),
            pltpu.VMEM((HD, SEQLEN), jnp.float32),
        ],
        cost_estimate=pl.CostEstimate(
            flops=10 * rows * SEQLEN * q_heads * HD,
            transcendentals=rows * SEQLEN * q_heads,
            bytes_accessed=6 << 20,
        ),
        name="attend_back",
    )(projected, projected, projected, d_heads, totals, cos_rows, sin_rows)


def project_and_norm(all_heads, weights, all_tokens, gain_vec):
    groups, rows, group_columns = all_heads.shape
    (first, first_offsets), (second, second_offsets) = weights
    parts, depth, part_columns = first.shape
    width = all_tokens.shape[1]
    tile = rows // groups
    places = jnp.stack([lax.axis_index("tensor"), lax.axis_index("dp")])

    def kernel(
        at_ref, heads_ref, first_ref, second_ref, tokens_ref, gain_ref, hidden_ref, normed_ref, acc_ref, wide_ref
    ):
        step = pl.program_id(0)
        for g in range(groups):
            wide_ref[:, g * group_columns : (g + 1) * group_columns] = heads_ref[g]
        acc_ref[...] = tokens_ref[...].astype(jnp.float32)
        for half, (weight_ref, offsets) in enumerate(
            ((first_ref, first_offsets), (second_ref, second_offsets))
        ):
            for part in range(parts):
                start = (at_ref[1] ^ offsets[part]) * part_columns
                columns = pl.ds(pl.multiple_of(start, part_columns), part_columns)
                acc_ref[:, columns] += jnp.dot(
                    wide_ref[:, half * depth : (half + 1) * depth],
                    weight_ref[part],
                    preferred_element_type=jnp.float32,
                )
        hidden = acc_ref[...]
        row_scale = lax.rsqrt(jnp.mean(hidden * hidden, axis=-1, keepdims=True) + EPS)
        normed_ref[...] = (hidden * row_scale * gain_ref[...].astype(jnp.float32)).astype(
            jnp.bfloat16
        )

        @pl.when(step == at_ref[0])
        def _():
            hidden_ref[...] = hidden

    return pl.pallas_call(
        kernel,
        grid_spec=pltpu.PrefetchScalarGridSpec(
            num_scalar_prefetch=1,
            grid=(groups,),
            in_specs=[
                pl.BlockSpec((groups, tile, group_columns), lambda i, at_ref: (0, i, 0)),
                pl.BlockSpec(first.shape, lambda i, at_ref: (0, 0, 0)),
                pl.BlockSpec(second.shape, lambda i, at_ref: (0, 0, 0)),
                pl.BlockSpec((tile, width), lambda i, at_ref: (i, 0)),
                pl.BlockSpec((1, width), lambda i, at_ref: (0, 0)),
            ],
            out_specs=[
                pl.BlockSpec((tile, width), lambda i, at_ref: (0, 0)),
                pl.BlockSpec((tile, width), lambda i, at_ref: (i, 0)),
            ],
            scratch_shapes=[
                pltpu.VMEM((tile, width), jnp.float32),
                pltpu.VMEM((tile, groups * group_columns), jnp.bfloat16),
            ],
        ),
        out_shape=[
            jax.ShapeDtypeStruct((tile, width), jnp.float32),
            jax.ShapeDtypeStruct((rows, width), jnp.bfloat16),
        ],
        cost_estimate=pl.CostEstimate(
            flops=2 * rows * width * width, transcendentals=rows, bytes_accessed=20 << 20
        ),
        name="project_and_norm",
    )(places, all_heads, first, second, all_tokens, gain_vec.reshape(1, -1))


def gated_up(normed, w_gate, w_up):
    rows, width = normed.shape
    columns = w_gate.shape[1]
    tile = 256

    def kernel(normed_ref, gate_w_ref, up_w_ref, gate_ref, up_ref, active_ref):
        gate = jnp.dot(normed_ref[...], gate_w_ref[...], preferred_element_type=jnp.float32)
        up = jnp.dot(normed_ref[...], up_w_ref[...], preferred_element_type=jnp.float32)
        gate_ref[...] = gate
        up_ref[...] = up
        active_ref[...] = (gate * jax.nn.sigmoid(gate) * up).astype(jnp.bfloat16)

    column_block = pl.BlockSpec((rows, tile), lambda j: (0, j))
    weight_block = pl.BlockSpec((width, tile), lambda j: (0, j))
    return pl.pallas_call(
        kernel,
        grid=(columns // tile,),
        in_specs=[pl.BlockSpec((rows, width), lambda j: (0, 0)), weight_block, weight_block],
        out_specs=[column_block] * 3,
        out_shape=[
            jax.ShapeDtypeStruct((rows, columns), jnp.float32),
            jax.ShapeDtypeStruct((rows, columns), jnp.float32),
            jax.ShapeDtypeStruct((rows, columns), jnp.bfloat16),
        ],
        cost_estimate=pl.CostEstimate(
            flops=4 * rows * width * columns,
            transcendentals=rows * columns,
            bytes_accessed=40 << 20,
        ),
        name="gated_up",
    )(normed, w_gate, w_up)


def row_major(array):
    return with_layout_constraint(array, Layout(major_to_minor=tuple(range(array.ndim))))


def split_columns(array, parts):
    if parts == 1:
        return array
    rows, columns = array.shape[0], array.shape[1] // parts
    return array.reshape(rows, parts, columns).swapaxes(0, 1).reshape(parts * rows, columns)


def join_columns(array, parts):
    if parts == 1:
        return array
    rows, columns = array.shape[0] // parts, array.shape[1]
    return array.reshape(parts, rows, columns).swapaxes(0, 1).reshape(rows, parts * columns)


def block(
    tokens,
    cotangent,
    norm1_gain,
    w_query,
    w_key,
    w_value,
    w_output,
    norm2_gain,
    w_gate,
    w_up,
    w_down,
):
    low = jnp.bfloat16
    n_dp = lax.axis_size("dp")
    nothing = scatter_sum(tokens[:, :128] * 0, "dp")[0, 0]
    all_tokens = gather_rows(tokens, "tensor")
    part_columns = w_output.shape[1] // n_dp
    own_part = lax.dynamic_slice_in_dim(
        w_output, lax.axis_index("dp") * part_columns, part_columns, 1
    )
    part_output = gather_rows(own_part, "tensor")
    all_output = cube_gather(part_output, "dp")
    q_columns, k_columns = w_query.shape[1], w_key.shape[1]
    q_heads, kv_heads = q_columns // HD, k_columns // HD
    gain_one = norm1_gain.astype(jnp.float32)
    gain_two = norm2_gain.astype(jnp.float32)
    own_tokens = tokens.astype(jnp.float32)
    cos_table, sin_table = rope_tables(SEQLEN, HD)
    cos_rows, sin_rows = cos_table.T, sin_table.T
    weight_rows = jnp.concatenate([w_query.T, w_key.T, w_value.T], axis=0)
    normed1, projected = norm_project(
        all_tokens, norm1_gain, weight_rows, cos_rows, sin_rows, q_columns + k_columns
    )
    heads_out, heads_rows, totals = attend(projected, q_heads, kv_heads)
    all_heads = lax.all_gather(heads_out, "tensor", axis=0)
    all_cot = gather_rows(cotangent, "tensor")
    hidden_state, normed2 = project_and_norm(
        all_heads, all_output, all_tokens, (gain_two + nothing.astype(jnp.float32))
    )
    gate_proj, up_proj, activated = gated_up(normed2, w_gate, w_up)
    mlp_part = jnp.dot(activated, w_down, preferred_element_type=jnp.float32).astype(low)
    d_activated = contract_cols(all_cot, w_down)
    _, pull_gated = jax.vjp(gated_unit, gate_proj, up_proj)
    d_gate, d_up = pull_gated(d_activated)
    d_gate = d_gate.astype(low)
    d_up = d_up.astype(low)
    ff_columns = w_gate.shape[1]
    ff_folds = w_gate.shape[0] // w_down.shape[0]
    grad_down = row_major(split_columns(contract_rows(activated, all_cot).astype(low), ff_folds))
    part_down = scatter_sum(grad_down, "dp")
    dn2_part = (contract_cols(d_gate, w_gate) + contract_cols(d_up, w_up)).astype(low)
    d_normed2 = exchange_sum(dn2_part, "tensor")
    gate_up_grads = row_major(
        jnp.concatenate(
            [contract_rows(normed2, d_gate).astype(low), contract_rows(normed2, d_up).astype(low)],
            axis=1,
        )
    )
    part_gate_up = scatter_sum(gate_up_grads, "dp")
    half_width = mlp_part.shape[1] // 2
    mlp_sum_a = exchange_sum(mlp_part[:, :half_width], "tensor")
    mlp_sum_b = exchange_sum(mlp_part[:, half_width:], "tensor")
    output = (hidden_state + jnp.concatenate([mlp_sum_a, mlp_sum_b], axis=1)).astype(low)
    d_state = cotangent.astype(jnp.float32) + norm_backward(hidden_state, gain_two, d_normed2)
    d_state_low = gather_rows(d_state.astype(low), "tensor")
    gain_two_sum = cube_sum(gain_gradient(hidden_state, d_normed2), ("dp", "tensor"))
    d_heads_rows = contract_cols(w_output, d_state_low).astype(low)
    d_query, d_key, d_value = attend_back(
        projected, d_heads_rows, totals, cos_rows, sin_rows, q_heads, kv_heads
    )
    d_projected = jnp.concatenate([d_query, d_key, d_value], axis=0)
    dn1_part = contract_rows(d_projected, weight_rows).astype(low)
    d_normed1 = exchange_sum(dn1_part, "tensor")
    gain_one_sum = cube_sum(
        gain_gradient(all_tokens.astype(jnp.float32), dn1_part.astype(jnp.float32)), ("dp", "tensor")
    )
    folds = w_query.shape[0] // w_output.shape[0]
    grad_qkv = lax.dot_general(
        normed1,
        d_projected,
        (((0,), (1,)), ((), ())),
        preferred_element_type=jnp.float32,
    ).astype(low)
    grad_output = jnp.dot(heads_rows, d_state_low, preferred_element_type=jnp.float32).astype(low)
    low_attn = row_major(
        jnp.concatenate([grad_qkv, split_columns(grad_output, folds)], axis=1)
    )
    part_attn = scatter_sum(low_attn, "dp")
    shared_ff = row_major(
        gather_rows(row_major(jnp.concatenate([part_gate_up, part_down], axis=1)), "dp")
    )
    shared_attn = row_major(gather_rows(part_attn, "dp"))
    input_grad = (d_state + norm_backward(own_tokens, gain_one, d_normed1)).astype(low)
    full_gate = shared_ff[:, :ff_columns].astype(jnp.float32)
    full_up = shared_ff[:, ff_columns : 2 * ff_columns].astype(jnp.float32)
    full_down = join_columns(shared_ff[:, 2 * ff_columns :], ff_folds).astype(jnp.float32)
    ends = (q_columns, q_columns + k_columns, q_columns + 2 * k_columns)
    full_query = shared_attn[:, : ends[0]].astype(jnp.float32)
    full_key = shared_attn[:, ends[0] : ends[1]].astype(jnp.float32)
    full_value = shared_attn[:, ends[1] : ends[2]].astype(jnp.float32)
    full_output = join_columns(shared_attn[:, ends[2] :], folds).astype(jnp.float32)
    return (
        output,
        input_grad,
        gain_one_sum,
        full_query,
        full_key,
        full_value,
        full_output,
        gain_two_sum,
        full_gate,
        full_up,
        full_down,
    )


def solution(mesh):
    return jax.shard_map(
        block,
        mesh=mesh,
        in_specs=(
            P(("dp", "tensor"), None),
            P(("dp", "tensor"), None),
            P(),
            P(None, "tensor"),
            P(None, "tensor"),
            P(None, "tensor"),
            P("tensor", None),
            P(),
            P(None, "tensor"),
            P(None, "tensor"),
            P("tensor", None),
        ),
        out_specs=(
            P(("dp", "tensor"), None),
            P(("dp", "tensor"), None),
            P(),
            P(None, "tensor"),
            P(None, "tensor"),
            P(None, "tensor"),
            P("tensor", None),
            P(),
            P(None, "tensor"),
            P(None, "tensor"),
            P("tensor", None),
        ),
        check_vma=False,
    )
```

```python
import functools

import jax
import jax.numpy as jnp
from jax import lax
from jax.experimental import pallas as pl
from jax.experimental.pallas import tpu as pltpu
from jax.experimental.layout import Layout, with_layout_constraint
from jax.sharding import PartitionSpec as P


HD = 64
SEQLEN = 512


EPS = 1e-05
ROPE_BASE = 500000.0
MASKED = -1e30


def rope_tables(length, columns):
    half_width = columns // 2
    frequency = ROPE_BASE ** (-(jnp.arange(half_width, dtype=jnp.float32) * 2.0 / columns))
    angles = jnp.arange(length, dtype=jnp.float32)[:, None] * frequency[None, :]
    return (jnp.cos(angles), jnp.sin(angles))


def rms_norm(values, gain_vec):
    row_scale = lax.rsqrt(jnp.mean(values * values, axis=-1, keepdims=True) + EPS)
    return values * row_scale * gain_vec


def norm_backward(values, gain_vec, upstream):
    _, pull_back = jax.vjp(lambda inner_values: rms_norm(inner_values, gain_vec), values)
    return pull_back(upstream)[0]


def gain_gradient(values, upstream):
    row_scale = lax.rsqrt(jnp.mean(values * values, axis=-1, keepdims=True) + EPS)
    return jnp.sum(upstream * values * row_scale, axis=0)


def contract_rows(left_side, right_side):
    return lax.dot_general(
        left_side, right_side, (((0,), (0,)), ((), ())), preferred_element_type=jnp.float32
    )


def contract_cols(left_side, right_side):
    return lax.dot_general(
        left_side, right_side, (((1,), (1,)), ((), ())), preferred_element_type=jnp.float32
    )


def gather_rows(block, axis):
    return lax.all_gather(block, axis, axis=0, tiled=True)


def scatter_sum(partial, axis):
    return lax.psum_scatter(partial, axis, scatter_dimension=0, tiled=True)


def exchange_sum(partial, axis):
    n = lax.axis_size(axis)
    me = lax.axis_index(axis)
    rows = partial.shape[0] // n

    def block(index):
        return lax.dynamic_slice_in_dim(partial, index * rows, rows, 0)

    total = block(me).astype(jnp.float32)
    for hop in range(1, n):
        moved = lax.ppermute(block((me + hop) % n), axis, [(i, (i + hop) % n) for i in range(n)])
        total += moved.astype(jnp.float32)
    return total


def cube_gather(blocks, axis):
    n = lax.axis_size(axis)
    bits = [1 << b for b in range(n.bit_length() - 1)]
    half = blocks.shape[-1] // 2
    halves = []
    for part, order in (
        (blocks[..., :half], bits[1:] + bits[:1]),
        (blocks[..., half:], bits[:0:-1] + bits[:1]),
    ):
        held, offsets = part[None], [0]
        for bit in order:
            moved = lax.ppermute(held, axis, [(i, i ^ bit) for i in range(n)])
            held = jnp.concatenate([held, moved], axis=0)
            offsets = offsets + [o ^ bit for o in offsets]
        halves.append((held, tuple(offsets)))
    return halves


def cube_sum(vector, axes):
    for axis in axes:
        n = lax.axis_size(axis)
        bit = 1
        while bit < n:
            vector = vector + lax.ppermute(vector, axis, [(i, i ^ bit) for i in range(n)])
            bit *= 2
    return vector


def rotate_rows(values, cos_rows, sin_rows):
    half = HD // 2
    heads = []
    for h in range(values.shape[0] // HD):
        upper = values[h * HD : h * HD + half]
        lower = values[h * HD + half : (h + 1) * HD]
        heads.append(upper * cos_rows - lower * sin_rows)
        heads.append(lower * cos_rows + upper * sin_rows)
    return jnp.concatenate(heads, axis=0)


def dot_lanes(left_side, right_side):
    return lax.dot_general(
        left_side, right_side, (((1,), (1,)), ((), ())), preferred_element_type=jnp.float32
    )


def norm_project(gathered, tile, gain_vec, weight_rows, cos_rows, sin_rows, rotated):
    groups, _, width = gathered.shape
    rows = groups * tile
    columns = weight_rows.shape[0]

    def kernel(tokens_ref, gain_ref, weight_ref, cos_ref, sin_ref, normed_ref, out_ref):
        values = tokens_ref[0].astype(jnp.float32)
        row_scale = lax.rsqrt(jnp.mean(values * values, axis=-1, keepdims=True) + EPS)
        normed = (values * row_scale * gain_ref[...].astype(jnp.float32)).astype(jnp.bfloat16)
        normed_ref[...] = normed
        projected = dot_lanes(weight_ref[...], normed)
        out_ref[:rotated] = rotate_rows(projected[:rotated], cos_ref[...], sin_ref[...]).astype(
            jnp.bfloat16
        )
        out_ref[rotated:] = projected[rotated:].astype(jnp.bfloat16)

    half = HD // 2
    return pl.pallas_call(
        kernel,
        grid=(rows // tile,),
        in_specs=[
            pl.BlockSpec((1, tile, width), lambda i: (i, 0, 0)),
            pl.BlockSpec((1, width), lambda i: (0, 0)),
            pl.BlockSpec((columns, width), lambda i: (0, 0)),
            pl.BlockSpec((half, tile), lambda i: (0, i % (SEQLEN // tile))),
            pl.BlockSpec((half, tile), lambda i: (0, i % (SEQLEN // tile))),
        ],
        out_specs=[
            pl.BlockSpec((tile, width), lambda i: (i, 0)),
            pl.BlockSpec((columns, tile), lambda i: (0, i)),
        ],
        out_shape=[
            jax.ShapeDtypeStruct((rows, width), jnp.bfloat16),
            jax.ShapeDtypeStruct((columns, rows), jnp.bfloat16),
        ],
        cost_estimate=pl.CostEstimate(
            flops=2 * rows * width * columns, transcendentals=rows, bytes_accessed=12 << 20
        ),
        name="norm_project",
    )(gathered, gain_vec.reshape(1, -1), weight_rows, cos_rows, sin_rows)


def key_tiles(step, tile):
    return [(t * tile, t == step) for t in range(step + 1)]


def causal_tile(tile):
    key_at = lax.broadcasted_iota(jnp.int32, (tile, tile), 0)
    query_at = lax.broadcasted_iota(jnp.int32, (tile, tile), 1)
    return key_at <= query_at


def attend(projected, q_heads, kv_heads):
    rows = projected.shape[1]
    group = q_heads // kv_heads
    wide = group * HD
    tile = 256
    score_scale = HD ** (-0.5)

    def kernel(query_ref, key_ref, value_ref, heads_ref, heads_t_ref, total_ref):
        keys = key_ref[...].astype(jnp.float32).T.astype(jnp.bfloat16)
        visible = causal_tile(tile)
        for step in range(SEQLEN // tile):
            here = slice(step * tile, (step + 1) * tile)
            for h in range(group):
                query = query_ref[h * HD : (h + 1) * HD, here]
                parts = []
                for start, masked in key_tiles(step, tile):
                    part = jnp.dot(
                        keys[start : start + tile], query, preferred_element_type=jnp.float32
                    )
                    parts.append(jnp.where(visible, part, MASKED) if masked else part)
                top = functools.reduce(
                    jnp.maximum, [jnp.max(part, axis=0, keepdims=True) for part in parts]
                )
                parts = [jnp.exp((part - top) * score_scale) for part in parts]
                total = sum(jnp.sum(part, axis=0, keepdims=True) for part in parts)
                inverse = 1.0 / total
                mixed = sum(
                    jnp.dot(
                        value_ref[:, start : start + tile],
                        (part * inverse).astype(jnp.bfloat16),
                        preferred_element_type=jnp.float32,
                    )
                    for part, (start, _) in zip(parts, key_tiles(step, tile))
                )
                heads_t_ref[h * HD : (h + 1) * HD, here] = mixed.astype(jnp.bfloat16)
                total_ref[0, h : h + 1, here] = top * score_scale + jnp.log(total)
        heads_ref[...] = heads_t_ref[...].astype(jnp.float32).T.astype(jnp.bfloat16)

    return pl.pallas_call(
        kernel,
        grid=(rows // SEQLEN, kv_heads),
        in_specs=[
            pl.BlockSpec((wide, SEQLEN), lambda s, j: (j, s)),
            pl.BlockSpec((HD, SEQLEN), lambda s, j: (q_heads + j, s)),
            pl.BlockSpec((HD, SEQLEN), lambda s, j: (q_heads + kv_heads + j, s)),
        ],
        out_specs=[
            pl.BlockSpec((SEQLEN, wide), lambda s, j: (s, j)),
            pl.BlockSpec((wide, SEQLEN), lambda s, j: (j, s)),
            pl.BlockSpec((1, group, SEQLEN), lambda s, j: (j, 0, s)),
        ],
        out_shape=[
            jax.ShapeDtypeStruct((rows, q_heads * HD), jnp.bfloat16),
            jax.ShapeDtypeStruct((q_heads * HD, rows), jnp.bfloat16),
            jax.ShapeDtypeStruct((kv_heads, group, rows), jnp.float32),
        ],
        cost_estimate=pl.CostEstimate(
            flops=4 * rows * SEQLEN * q_heads * HD,
            transcendentals=rows * SEQLEN * q_heads,
            bytes_accessed=4 << 20,
        ),
        name="attend",
    )(projected, projected, projected)


def attend_back(projected, d_heads, totals, cos_rows, sin_rows, q_heads, kv_heads):
    rows = projected.shape[1]
    group = q_heads // kv_heads
    wide = group * HD
    tile = 256
    score_scale = HD ** (-0.5)

    def kernel(
        query_ref,
        key_ref,
        value_ref,
        d_heads_ref,
        total_ref,
        cos_ref,
        sin_ref,
        d_query_ref,
        d_key_ref,
        d_value_ref,
        key_sum,
        value_sum,
    ):
        keys = key_ref[...].astype(jnp.float32).T.astype(jnp.bfloat16)
        values = value_ref[...].astype(jnp.float32).T.astype(jnp.bfloat16)
        visible = causal_tile(tile)
        key_sum[...] = jnp.zeros_like(key_sum)
        value_sum[...] = jnp.zeros_like(value_sum)
        for step in range(SEQLEN // tile):
            here = slice(step * tile, (step + 1) * tile)
            for h in range(group):
                query = query_ref[h * HD : (h + 1) * HD, here]
                d_head = d_heads_ref[h * HD : (h + 1) * HD, here]
                log_total = total_ref[0, h : h + 1, here]
                probs, d_probs = [], []
                for start, masked in key_tiles(step, tile):
                    span = slice(start, start + tile)
                    part = jnp.dot(keys[span], query, preferred_element_type=jnp.float32)
                    part = jnp.exp(part * score_scale - log_total)
                    if masked:
                        part = jnp.where(visible, part, 0.0)
                    probs.append(part)
                    value_sum[:, span] += dot_lanes(d_head, part.astype(jnp.bfloat16))
                    d_probs.append(
                        jnp.dot(values[span], d_head, preferred_element_type=jnp.float32)
                    )
                row_sum = sum(
                    jnp.sum(part * d_part, axis=0, keepdims=True)
                    for part, d_part in zip(probs, d_probs)
                )
                d_query = jnp.zeros((HD, tile), jnp.float32)
                for (start, _), part, d_part in zip(key_tiles(step, tile), probs, d_probs):
                    span = slice(start, start + tile)
                    d_scores = (part * (d_part - row_sum)).astype(jnp.bfloat16)
                    d_query += jnp.dot(
                        key_ref[:, span], d_scores, preferred_element_type=jnp.float32
                    )
                    key_sum[:, span] += dot_lanes(query, d_scores)
                d_query_ref[h * HD : (h + 1) * HD, here] = rotate_rows(
                    d_query * score_scale, cos_ref[:, here], -sin_ref[:, here]
                ).astype(jnp.bfloat16)
        d_key_ref[...] = rotate_rows(
            key_sum[...] * score_scale, cos_ref[...], -sin_ref[...]
        ).astype(jnp.bfloat16)
        d_value_ref[...] = value_sum[...].astype(jnp.bfloat16)

    half = HD // 2
    return pl.pallas_call(
        kernel,
        grid=(rows // SEQLEN, kv_heads),
        in_specs=[
            pl.BlockSpec((wide, SEQLEN), lambda s, j: (j, s)),
            pl.BlockSpec((HD, SEQLEN), lambda s, j: (q_heads + j, s)),
            pl.BlockSpec((HD, SEQLEN), lambda s, j: (q_heads + kv_heads + j, s)),
            pl.BlockSpec((wide, SEQLEN), lambda s, j: (j, s)),
            pl.BlockSpec((1, group, SEQLEN), lambda s, j: (j, 0, s)),
            pl.BlockSpec((half, SEQLEN), lambda s, j: (0, 0)),
            pl.BlockSpec((half, SEQLEN), lambda s, j: (0, 0)),
        ],
        out_specs=[
            pl.BlockSpec((wide, SEQLEN), lambda s, j: (j, s)),
            pl.BlockSpec((HD, SEQLEN), lambda s, j: (j, s)),
            pl.BlockSpec((HD, SEQLEN), lambda s, j: (j, s)),
        ],
        out_shape=[
            jax.ShapeDtypeStruct((q_heads * HD, rows), jnp.bfloat16),
            jax.ShapeDtypeStruct((kv_heads * HD, rows), jnp.bfloat16),
            jax.ShapeDtypeStruct((kv_heads * HD, rows), jnp.bfloat16),
        ],
        scratch_shapes=[
            pltpu.VMEM((HD, SEQLEN), jnp.float32),
            pltpu.VMEM((HD, SEQLEN), jnp.float32),
        ],
        cost_estimate=pl.CostEstimate(
            flops=10 * rows * SEQLEN * q_heads * HD,
            transcendentals=rows * SEQLEN * q_heads,
            bytes_accessed=6 << 20,
        ),
        name="attend_back",
    )(projected, projected, projected, d_heads, totals, cos_rows, sin_rows)


def project_and_norm(all_heads, weights, gathered, gain_vec):
    groups, rows, group_columns = all_heads.shape
    (first, first_offsets), (second, second_offsets) = weights
    parts, _, depth, half = first.shape
    width = 2 * half
    tile = rows // groups
    places = jnp.stack([lax.axis_index("tensor"), lax.axis_index("dp")])

    def kernel(
        at_ref,
        heads_ref,
        first_ref,
        second_ref,
        tokens_ref,
        gain_ref,
        hidden_ref,
        normed_ref,
        weight_ref,
        wide_ref,
    ):
        step = pl.program_id(0)

        @pl.when(step == 0)
        def _():
            for side, part_ref, offsets in (
                (0, first_ref, first_offsets),
                (half, second_ref, second_offsets),
            ):
                for part in range(parts):
                    for g in range(groups):
                        start = g * group_columns + (at_ref[1] ^ offsets[part]) * depth
                        at = pl.ds(pl.multiple_of(start, depth), depth)
                        weight_ref[at, side : side + half] = part_ref[part, g]

        for g in range(groups):
            wide_ref[:, g * group_columns : (g + 1) * group_columns] = heads_ref[g]
        hidden = tokens_ref[0].astype(jnp.float32) + jnp.dot(
            wide_ref[...], weight_ref[...], preferred_element_type=jnp.float32
        )
        row_scale = lax.rsqrt(jnp.mean(hidden * hidden, axis=-1, keepdims=True) + EPS)
        normed_ref[...] = (hidden * row_scale * gain_ref[...].astype(jnp.float32)).astype(
            jnp.bfloat16
        )

        @pl.when(step == at_ref[0])
        def _():
            hidden_ref[...] = hidden

    return pl.pallas_call(
        kernel,
        grid_spec=pltpu.PrefetchScalarGridSpec(
            num_scalar_prefetch=1,
            grid=(groups,),
            in_specs=[
                pl.BlockSpec((groups, tile, group_columns), lambda i, at_ref: (0, i, 0)),
                pl.BlockSpec(first.shape, lambda i, at_ref: (0, 0, 0, 0)),
                pl.BlockSpec(second.shape, lambda i, at_ref: (0, 0, 0, 0)),
                pl.BlockSpec((1, tile, width), lambda i, at_ref: (i, 0, 0)),
                pl.BlockSpec((1, width), lambda i, at_ref: (0, 0)),
            ],
            out_specs=[
                pl.BlockSpec((tile, width), lambda i, at_ref: (0, 0)),
                pl.BlockSpec((tile, width), lambda i, at_ref: (i, 0)),
            ],
            scratch_shapes=[
                pltpu.VMEM((groups * group_columns, width), jnp.bfloat16),
                pltpu.VMEM((tile, groups * group_columns), jnp.bfloat16),
            ],
        ),
        out_shape=[
            jax.ShapeDtypeStruct((tile, width), jnp.float32),
            jax.ShapeDtypeStruct((rows, width), jnp.bfloat16),
        ],
        cost_estimate=pl.CostEstimate(
            flops=2 * rows * width * width, transcendentals=rows, bytes_accessed=20 << 20
        ),
        name="project_and_norm",
    )(places, all_heads, first, second, gathered, gain_vec.reshape(1, -1))


def gated_back(all_cot, w_down, gate_proj, up_proj):
    rows, width = all_cot.shape
    columns = w_down.shape[0]
    tile = 256

    def kernel(cot_ref, weight_ref, gate_ref, up_ref, d_gate_ref, d_up_ref):
        d_active = dot_lanes(cot_ref[...], weight_ref[...])
        gate = gate_ref[...]
        chance = jax.nn.sigmoid(gate)
        smooth = gate * chance
        d_up_ref[...] = (d_active * smooth).astype(jnp.bfloat16)
        slope = chance * (1.0 + gate * (1.0 - chance))
        d_gate_ref[...] = (d_active * up_ref[...] * slope).astype(jnp.bfloat16)

    column_block = pl.BlockSpec((rows, tile), lambda j: (0, j))
    return pl.pallas_call(
        kernel,
        grid=(columns // tile,),
        in_specs=[
            pl.BlockSpec((rows, width), lambda j: (0, 0)),
            pl.BlockSpec((tile, width), lambda j: (j, 0)),
            column_block,
            column_block,
        ],
        out_specs=[column_block] * 2,
        out_shape=[jax.ShapeDtypeStruct((rows, columns), jnp.bfloat16)] * 2,
        cost_estimate=pl.CostEstimate(
            flops=2 * rows * width * columns,
            transcendentals=rows * columns,
            bytes_accessed=36 << 20,
        ),
        name="gated_back",
    )(all_cot, w_down, gate_proj, up_proj)


def pair_product(first, first_weight, second, second_weight):
    rows, depth = first.shape
    columns = first_weight.shape[0]
    tile = 256

    def kernel(first_ref, second_ref, first_w_ref, second_w_ref, out_ref):
        out_ref[...] = (
            dot_lanes(first_ref[...], first_w_ref[...])
            + dot_lanes(second_ref[...], second_w_ref[...])
        ).astype(jnp.bfloat16)

    whole = pl.BlockSpec((rows, depth), lambda j: (0, 0))
    weight_block = pl.BlockSpec((tile, depth), lambda j: (j, 0))
    return pl.pallas_call(
        kernel,
        grid=(columns // tile,),
        in_specs=[whole, whole, weight_block, weight_block],
        out_specs=pl.BlockSpec((rows, tile), lambda j: (0, j)),
        out_shape=jax.ShapeDtypeStruct((rows, columns), jnp.bfloat16),
        cost_estimate=pl.CostEstimate(
            flops=4 * rows * depth * columns, transcendentals=0, bytes_accessed=28 << 20
        ),
        name="pair_product",
    )(first, second, first_weight, second_weight)


def gated_up(normed, w_gate, w_up):
    rows, width = normed.shape
    columns = w_gate.shape[1]
    tile = 256

    def kernel(normed_ref, gate_w_ref, up_w_ref, gate_ref, up_ref, active_ref):
        gate = jnp.dot(normed_ref[...], gate_w_ref[...], preferred_element_type=jnp.float32)
        up = jnp.dot(normed_ref[...], up_w_ref[...], preferred_element_type=jnp.float32)
        gate_ref[...] = gate
        up_ref[...] = up
        active_ref[...] = (gate * jax.nn.sigmoid(gate) * up).astype(jnp.bfloat16)

    column_block = pl.BlockSpec((rows, tile), lambda j: (0, j))
    weight_block = pl.BlockSpec((width, tile), lambda j: (0, j))
    return pl.pallas_call(
        kernel,
        grid=(columns // tile,),
        in_specs=[pl.BlockSpec((rows, width), lambda j: (0, 0)), weight_block, weight_block],
        out_specs=[column_block] * 3,
        out_shape=[
            jax.ShapeDtypeStruct((rows, columns), jnp.float32),
            jax.ShapeDtypeStruct((rows, columns), jnp.float32),
            jax.ShapeDtypeStruct((rows, columns), jnp.bfloat16),
        ],
        cost_estimate=pl.CostEstimate(
            flops=4 * rows * width * columns,
            transcendentals=rows * columns,
            bytes_accessed=40 << 20,
        ),
        name="gated_up",
    )(normed, w_gate, w_up)


def row_major(array):
    return with_layout_constraint(array, Layout(major_to_minor=tuple(range(array.ndim))))


def split_columns(array, parts):
    if parts == 1:
        return array
    rows, columns = array.shape[0], array.shape[1] // parts
    return array.reshape(rows, parts, columns).swapaxes(0, 1).reshape(parts * rows, columns)


def join_columns(array, parts):
    if parts == 1:
        return array
    rows, columns = array.shape[0] // parts, array.shape[1]
    return array.reshape(parts, rows, columns).swapaxes(0, 1).reshape(rows, parts * columns)


def block(
    tokens,
    cotangent,
    norm1_gain,
    w_query,
    w_key,
    w_value,
    w_output,
    norm2_gain,
    w_gate,
    w_up,
    w_down,
):
    low = jnp.bfloat16
    n_dp = lax.axis_size("dp")
    nothing = scatter_sum(tokens[:, :128] * 0, "dp")[0, 0]
    own_rows, width = tokens.shape
    depth = w_output.shape[0] // n_dp
    own_part = lax.dynamic_slice_in_dim(w_output, lax.axis_index("dp") * depth, depth, 0)
    gathered = lax.all_gather(
        jnp.concatenate([tokens, own_part], axis=0), "tensor", axis=0
    )
    all_output = cube_gather(gathered[:, own_rows:], "dp")
    q_columns, k_columns = w_query.shape[1], w_key.shape[1]
    q_heads, kv_heads = q_columns // HD, k_columns // HD
    gain_one = norm1_gain.astype(jnp.float32)
    gain_two = norm2_gain.astype(jnp.float32)
    own_tokens = tokens.astype(jnp.float32)
    cos_table, sin_table = rope_tables(SEQLEN, HD)
    cos_rows, sin_rows = cos_table.T, sin_table.T
    weight_rows = jnp.concatenate([w_query.T, w_key.T, w_value.T], axis=0)
    normed1, projected = norm_project(
        gathered, own_rows, norm1_gain, weight_rows, cos_rows, sin_rows, q_columns + k_columns
    )
    heads_out, heads_rows, totals = attend(projected, q_heads, kv_heads)
    all_heads = lax.all_gather(heads_out, "tensor", axis=0)
    all_cot = gather_rows(cotangent, "tensor")
    hidden_state, normed2 = project_and_norm(
        all_heads, all_output, gathered, (gain_two + nothing.astype(jnp.float32))
    )
    gate_proj, up_proj, activated = gated_up(normed2, w_gate, w_up)
    mlp_part = jnp.dot(activated, w_down, preferred_element_type=jnp.float32).astype(low)
    ff_columns = w_gate.shape[1]
    ff_folds = w_gate.shape[0] // w_down.shape[0]
    grad_down = row_major(split_columns(contract_rows(activated, all_cot).astype(low), ff_folds))
    part_down = scatter_sum(grad_down, "dp")
    d_gate, d_up = gated_back(all_cot, w_down, gate_proj, up_proj)
    dn2_part = pair_product(d_gate, w_gate, d_up, w_up)
    d_normed2 = exchange_sum(dn2_part, "tensor")
    gate_up_grads = row_major(
        jnp.concatenate(
            [contract_rows(normed2, d_gate).astype(low), contract_rows(normed2, d_up).astype(low)],
            axis=1,
        )
    )
    part_gate_up = scatter_sum(gate_up_grads, "dp")
    half_width = mlp_part.shape[1] // 2
    mlp_sum_a = exchange_sum(mlp_part[:, :half_width], "tensor")
    mlp_sum_b = exchange_sum(mlp_part[:, half_width:], "tensor")
    output = (hidden_state + jnp.concatenate([mlp_sum_a, mlp_sum_b], axis=1)).astype(low)
    d_state = cotangent.astype(jnp.float32) + norm_backward(hidden_state, gain_two, d_normed2)
    d_state_low = gather_rows(d_state.astype(low), "tensor")
    gain_two_sum = cube_sum(gain_gradient(hidden_state, d_normed2), ("dp", "tensor"))
    d_heads_rows = contract_cols(w_output, d_state_low).astype(low)
    d_query, d_key, d_value = attend_back(
        projected, d_heads_rows, totals, cos_rows, sin_rows, q_heads, kv_heads
    )
    d_projected = jnp.concatenate([d_query, d_key, d_value], axis=0)
    dn1_part = contract_rows(d_projected, weight_rows).astype(low)
    d_normed1 = exchange_sum(dn1_part, "tensor")
    gain_one_sum = cube_sum(
        gain_gradient(
            gathered[:, :own_rows].reshape(-1, width).astype(jnp.float32),
            dn1_part.astype(jnp.float32),
        ), ("dp", "tensor")
    )
    folds = w_query.shape[0] // w_output.shape[0]
    grad_qkv = lax.dot_general(
        normed1,
        d_projected,
        (((0,), (1,)), ((), ())),
        preferred_element_type=jnp.float32,
    ).astype(low)
    grad_output = jnp.dot(heads_rows, d_state_low, preferred_element_type=jnp.float32).astype(low)
    low_attn = row_major(
        jnp.concatenate([grad_qkv, split_columns(grad_output, folds)], axis=1)
    )
    part_attn = scatter_sum(low_attn, "dp")
    shared_ff = row_major(
        gather_rows(row_major(jnp.concatenate([part_gate_up, part_down], axis=1)), "dp")
    )
    shared_attn = row_major(gather_rows(part_attn, "dp"))
    input_grad = (d_state + norm_backward(own_tokens, gain_one, d_normed1)).astype(low)
    full_gate = shared_ff[:, :ff_columns].astype(jnp.float32)
    full_up = shared_ff[:, ff_columns : 2 * ff_columns].astype(jnp.float32)
    full_down = join_columns(shared_ff[:, 2 * ff_columns :], ff_folds).astype(jnp.float32)
    ends = (q_columns, q_columns + k_columns, q_columns + 2 * k_columns)
    full_query = shared_attn[:, : ends[0]].astype(jnp.float32)
    full_key = shared_attn[:, ends[0] : ends[1]].astype(jnp.float32)
    full_value = shared_attn[:, ends[1] : ends[2]].astype(jnp.float32)
    full_output = join_columns(shared_attn[:, ends[2] :], folds).astype(jnp.float32)
    return (
        output,
        input_grad,
        gain_one_sum,
        full_query,
        full_key,
        full_value,
        full_output,
        gain_two_sum,
        full_gate,
        full_up,
        full_down,
    )


def solution(mesh):
    return jax.shard_map(
        block,
        mesh=mesh,
        in_specs=(
            P(("dp", "tensor"), None),
            P(("dp", "tensor"), None),
            P(),
            P(None, "tensor"),
            P(None, "tensor"),
            P(None, "tensor"),
            P("tensor", None),
            P(),
            P(None, "tensor"),
            P(None, "tensor"),
            P("tensor", None),
        ),
        out_specs=(
            P(("dp", "tensor"), None),
            P(("dp", "tensor"), None),
            P(),
            P(None, "tensor"),
            P(None, "tensor"),
            P(None, "tensor"),
            P("tensor", None),
            P(),
            P(None, "tensor"),
            P(None, "tensor"),
            P("tensor", None),
        ),
        check_vma=False,
    )
```

```python
import functools

import jax
import jax.numpy as jnp
from jax import lax
from jax.experimental import pallas as pl
from jax.experimental.pallas import tpu as pltpu
from jax.experimental.layout import Layout, with_layout_constraint
from jax.sharding import PartitionSpec as P


HD = 64
SEQLEN = 512


EPS = 1e-05
ROPE_BASE = 500000.0
MASKED = -1e30


def rope_tables(length, columns):
    half_width = columns // 2
    frequency = ROPE_BASE ** (-(jnp.arange(half_width, dtype=jnp.float32) * 2.0 / columns))
    angles = jnp.arange(length, dtype=jnp.float32)[:, None] * frequency[None, :]
    return (jnp.cos(angles), jnp.sin(angles))


def rms_norm(values, gain_vec):
    row_scale = lax.rsqrt(jnp.mean(values * values, axis=-1, keepdims=True) + EPS)
    return values * row_scale * gain_vec


def norm_backward(values, gain_vec, upstream):
    _, pull_back = jax.vjp(lambda inner_values: rms_norm(inner_values, gain_vec), values)
    return pull_back(upstream)[0]


def gain_gradient(values, upstream):
    row_scale = lax.rsqrt(jnp.mean(values * values, axis=-1, keepdims=True) + EPS)
    return jnp.sum(upstream * values * row_scale, axis=0)


def contract_rows(left_side, right_side):
    return lax.dot_general(
        left_side, right_side, (((0,), (0,)), ((), ())), preferred_element_type=jnp.float32
    )


def contract_cols(left_side, right_side):
    return lax.dot_general(
        left_side, right_side, (((1,), (1,)), ((), ())), preferred_element_type=jnp.float32
    )


def gather_rows(block, axis):
    return lax.all_gather(block, axis, axis=0, tiled=True)


def scatter_sum(partial, axis):
    return lax.psum_scatter(partial, axis, scatter_dimension=0, tiled=True)


def exchange_sum(partial, axis):
    n = lax.axis_size(axis)
    me = lax.axis_index(axis)
    rows = partial.shape[0] // n

    def block(index):
        return lax.dynamic_slice_in_dim(partial, index * rows, rows, 0)

    total = block(me).astype(jnp.float32)
    for hop in range(1, n):
        moved = lax.ppermute(block((me + hop) % n), axis, [(i, (i + hop) % n) for i in range(n)])
        total += moved.astype(jnp.float32)
    return total


def cube_gather(blocks, axis):
    n = lax.axis_size(axis)
    bits = [1 << b for b in range(n.bit_length() - 1)]
    half = blocks.shape[-1] // 2
    halves = []
    for part, order in (
        (blocks[..., :half], bits[1:] + bits[:1]),
        (blocks[..., half:], bits[:0:-1] + bits[:1]),
    ):
        held, offsets = part[None], [0]
        for bit in order:
            moved = lax.ppermute(held, axis, [(i, i ^ bit) for i in range(n)])
            held = jnp.concatenate([held, moved], axis=0)
            offsets = offsets + [o ^ bit for o in offsets]
        halves.append((held, tuple(offsets)))
    return halves


def cube_sum(vector, axes):
    for axis in axes:
        n = lax.axis_size(axis)
        bit = 1
        while bit < n:
            vector = vector + lax.ppermute(vector, axis, [(i, i ^ bit) for i in range(n)])
            bit *= 2
    return vector


def rotate_rows(values, cos_rows, sin_rows):
    half = HD // 2
    heads = []
    for h in range(values.shape[0] // HD):
        upper = values[h * HD : h * HD + half]
        lower = values[h * HD + half : (h + 1) * HD]
        heads.append(upper * cos_rows - lower * sin_rows)
        heads.append(lower * cos_rows + upper * sin_rows)
    return jnp.concatenate(heads, axis=0)


def dot_lanes(left_side, right_side):
    return lax.dot_general(
        left_side, right_side, (((1,), (1,)), ((), ())), preferred_element_type=jnp.float32
    )


def norm_project(gathered, tile, gain_vec, weight_rows, cos_rows, sin_rows, rotated):
    groups, _, width = gathered.shape
    rows = groups * tile
    columns = weight_rows.shape[0]

    def kernel(tokens_ref, gain_ref, weight_ref, cos_ref, sin_ref, normed_ref, out_ref):
        values = tokens_ref[0].astype(jnp.float32)
        row_scale = lax.rsqrt(jnp.mean(values * values, axis=-1, keepdims=True) + EPS)
        normed = (values * row_scale * gain_ref[...].astype(jnp.float32)).astype(jnp.bfloat16)
        normed_ref[...] = normed
        projected = dot_lanes(weight_ref[...], normed)
        out_ref[:rotated] = rotate_rows(projected[:rotated], cos_ref[...], sin_ref[...]).astype(
            jnp.bfloat16
        )
        out_ref[rotated:] = projected[rotated:].astype(jnp.bfloat16)

    half = HD // 2
    return pl.pallas_call(
        kernel,
        grid=(rows // tile,),
        in_specs=[
            pl.BlockSpec((1, tile, width), lambda i: (i, 0, 0)),
            pl.BlockSpec((1, width), lambda i: (0, 0)),
            pl.BlockSpec((columns, width), lambda i: (0, 0)),
            pl.BlockSpec((half, tile), lambda i: (0, i % (SEQLEN // tile))),
            pl.BlockSpec((half, tile), lambda i: (0, i % (SEQLEN // tile))),
        ],
        out_specs=[
            pl.BlockSpec((tile, width), lambda i: (i, 0)),
            pl.BlockSpec((columns, tile), lambda i: (0, i)),
        ],
        out_shape=[
            jax.ShapeDtypeStruct((rows, width), jnp.bfloat16),
            jax.ShapeDtypeStruct((columns, rows), jnp.bfloat16),
        ],
        cost_estimate=pl.CostEstimate(
            flops=2 * rows * width * columns, transcendentals=rows, bytes_accessed=12 << 20
        ),
        name="norm_project",
    )(gathered, gain_vec.reshape(1, -1), weight_rows, cos_rows, sin_rows)


def key_tiles(step, tile):
    return [(t * tile, t == step) for t in range(step + 1)]


def causal_tile(tile):
    key_at = lax.broadcasted_iota(jnp.int32, (tile, tile), 0)
    query_at = lax.broadcasted_iota(jnp.int32, (tile, tile), 1)
    return key_at <= query_at


def attend(projected, q_heads, kv_heads):
    rows = projected.shape[1]
    group = q_heads // kv_heads
    wide = group * HD
    tile = 256
    score_scale = HD ** (-0.5)

    def kernel(query_ref, key_ref, value_ref, heads_ref, heads_t_ref, total_ref):
        keys = key_ref[...].astype(jnp.float32).T.astype(jnp.bfloat16)
        visible = causal_tile(tile)
        for step in range(SEQLEN // tile):
            here = slice(step * tile, (step + 1) * tile)
            for h in range(group):
                query = query_ref[h * HD : (h + 1) * HD, here]
                parts = []
                for start, masked in key_tiles(step, tile):
                    part = jnp.dot(
                        keys[start : start + tile], query, preferred_element_type=jnp.float32
                    )
                    parts.append(jnp.where(visible, part, MASKED) if masked else part)
                top = functools.reduce(
                    jnp.maximum, [jnp.max(part, axis=0, keepdims=True) for part in parts]
                )
                parts = [jnp.exp((part - top) * score_scale) for part in parts]
                total = sum(jnp.sum(part, axis=0, keepdims=True) for part in parts)
                inverse = 1.0 / total
                mixed = sum(
                    jnp.dot(
                        value_ref[:, start : start + tile],
                        (part * inverse).astype(jnp.bfloat16),
                        preferred_element_type=jnp.float32,
                    )
                    for part, (start, _) in zip(parts, key_tiles(step, tile))
                )
                heads_t_ref[h * HD : (h + 1) * HD, here] = mixed.astype(jnp.bfloat16)
                total_ref[0, h : h + 1, here] = top * score_scale + jnp.log(total)
        heads_ref[...] = heads_t_ref[...].astype(jnp.float32).T.astype(jnp.bfloat16)

    return pl.pallas_call(
        kernel,
        grid=(rows // SEQLEN, kv_heads),
        in_specs=[
            pl.BlockSpec((wide, SEQLEN), lambda s, j: (j, s)),
            pl.BlockSpec((HD, SEQLEN), lambda s, j: (q_heads + j, s)),
            pl.BlockSpec((HD, SEQLEN), lambda s, j: (q_heads + kv_heads + j, s)),
        ],
        out_specs=[
            pl.BlockSpec((SEQLEN, wide), lambda s, j: (s, j)),
            pl.BlockSpec((wide, SEQLEN), lambda s, j: (j, s)),
            pl.BlockSpec((1, group, SEQLEN), lambda s, j: (j, 0, s)),
        ],
        out_shape=[
            jax.ShapeDtypeStruct((rows, q_heads * HD), jnp.bfloat16),
            jax.ShapeDtypeStruct((q_heads * HD, rows), jnp.bfloat16),
            jax.ShapeDtypeStruct((kv_heads, group, rows), jnp.float32),
        ],
        cost_estimate=pl.CostEstimate(
            flops=4 * rows * SEQLEN * q_heads * HD,
            transcendentals=rows * SEQLEN * q_heads,
            bytes_accessed=4 << 20,
        ),
        name="attend",
    )(projected, projected, projected)


def attend_back(projected, d_heads, totals, cos_rows, sin_rows, q_heads, kv_heads):
    rows = projected.shape[1]
    group = q_heads // kv_heads
    wide = group * HD
    tile = 256
    score_scale = HD ** (-0.5)

    def kernel(
        query_ref,
        key_ref,
        value_ref,
        d_heads_ref,
        total_ref,
        cos_ref,
        sin_ref,
        d_query_ref,
        d_key_ref,
        d_value_ref,
        key_sum,
        value_sum,
    ):
        keys = key_ref[...].astype(jnp.float32).T.astype(jnp.bfloat16)
        values = value_ref[...].astype(jnp.float32).T.astype(jnp.bfloat16)
        visible = causal_tile(tile)
        key_sum[...] = jnp.zeros_like(key_sum)
        value_sum[...] = jnp.zeros_like(value_sum)
        for step in range(SEQLEN // tile):
            here = slice(step * tile, (step + 1) * tile)
            for h in range(group):
                query = query_ref[h * HD : (h + 1) * HD, here]
                d_head = d_heads_ref[h * HD : (h + 1) * HD, here]
                log_total = total_ref[0, h : h + 1, here]
                probs, d_probs = [], []
                for start, masked in key_tiles(step, tile):
                    span = slice(start, start + tile)
                    part = jnp.dot(keys[span], query, preferred_element_type=jnp.float32)
                    part = jnp.exp(part * score_scale - log_total)
                    if masked:
                        part = jnp.where(visible, part, 0.0)
                    probs.append(part)
                    value_sum[:, span] += dot_lanes(d_head, part.astype(jnp.bfloat16))
                    d_probs.append(
                        jnp.dot(values[span], d_head, preferred_element_type=jnp.float32)
                    )
                row_sum = sum(
                    jnp.sum(part * d_part, axis=0, keepdims=True)
                    for part, d_part in zip(probs, d_probs)
                )
                d_query = jnp.zeros((HD, tile), jnp.float32)
                for (start, _), part, d_part in zip(key_tiles(step, tile), probs, d_probs):
                    span = slice(start, start + tile)
                    d_scores = (part * (d_part - row_sum)).astype(jnp.bfloat16)
                    d_query += jnp.dot(
                        key_ref[:, span], d_scores, preferred_element_type=jnp.float32
                    )
                    key_sum[:, span] += dot_lanes(query, d_scores)
                d_query_ref[h * HD : (h + 1) * HD, here] = rotate_rows(
                    d_query * score_scale, cos_ref[:, here], -sin_ref[:, here]
                ).astype(jnp.bfloat16)
        d_key_ref[...] = rotate_rows(
            key_sum[...] * score_scale, cos_ref[...], -sin_ref[...]
        ).astype(jnp.bfloat16)
        d_value_ref[...] = value_sum[...].astype(jnp.bfloat16)

    half = HD // 2
    return pl.pallas_call(
        kernel,
        grid=(rows // SEQLEN, kv_heads),
        in_specs=[
            pl.BlockSpec((wide, SEQLEN), lambda s, j: (j, s)),
            pl.BlockSpec((HD, SEQLEN), lambda s, j: (q_heads + j, s)),
            pl.BlockSpec((HD, SEQLEN), lambda s, j: (q_heads + kv_heads + j, s)),
            pl.BlockSpec((wide, SEQLEN), lambda s, j: (j, s)),
            pl.BlockSpec((1, group, SEQLEN), lambda s, j: (j, 0, s)),
            pl.BlockSpec((half, SEQLEN), lambda s, j: (0, 0)),
            pl.BlockSpec((half, SEQLEN), lambda s, j: (0, 0)),
        ],
        out_specs=[
            pl.BlockSpec((wide, SEQLEN), lambda s, j: (j, s)),
            pl.BlockSpec((HD, SEQLEN), lambda s, j: (j, s)),
            pl.BlockSpec((HD, SEQLEN), lambda s, j: (j, s)),
        ],
        out_shape=[
            jax.ShapeDtypeStruct((q_heads * HD, rows), jnp.bfloat16),
            jax.ShapeDtypeStruct((kv_heads * HD, rows), jnp.bfloat16),
            jax.ShapeDtypeStruct((kv_heads * HD, rows), jnp.bfloat16),
        ],
        scratch_shapes=[
            pltpu.VMEM((HD, SEQLEN), jnp.float32),
            pltpu.VMEM((HD, SEQLEN), jnp.float32),
        ],
        cost_estimate=pl.CostEstimate(
            flops=10 * rows * SEQLEN * q_heads * HD,
            transcendentals=rows * SEQLEN * q_heads,
            bytes_accessed=6 << 20,
        ),
        name="attend_back",
    )(projected, projected, projected, d_heads, totals, cos_rows, sin_rows)


def project_and_norm(all_heads, weights, gathered, gain_vec):
    groups, rows, group_columns = all_heads.shape
    (first, first_offsets), (second, second_offsets) = weights
    parts, _, depth, half = first.shape
    width = 2 * half
    tile = rows // groups
    places = jnp.stack([lax.axis_index("tensor"), lax.axis_index("dp")])

    def kernel(
        at_ref,
        heads_ref,
        first_ref,
        second_ref,
        tokens_ref,
        gain_ref,
        hidden_ref,
        normed_ref,
        weight_ref,
        wide_ref,
    ):
        step = pl.program_id(0)

        @pl.when(step == 0)
        def _():
            for side, part_ref, offsets in (
                (0, first_ref, first_offsets),
                (half, second_ref, second_offsets),
            ):
                for part in range(parts):
                    for g in range(groups):
                        start = g * group_columns + (at_ref[1] ^ offsets[part]) * depth
                        at = pl.ds(pl.multiple_of(start, depth), depth)
                        weight_ref[at, side : side + half] = part_ref[part, g]

        for g in range(groups):
            wide_ref[:, g * group_columns : (g + 1) * group_columns] = heads_ref[g]
        hidden = tokens_ref[0].astype(jnp.float32) + jnp.dot(
            wide_ref[...], weight_ref[...], preferred_element_type=jnp.float32
        )
        row_scale = lax.rsqrt(jnp.mean(hidden * hidden, axis=-1, keepdims=True) + EPS)
        normed_ref[...] = (hidden * row_scale * gain_ref[...].astype(jnp.float32)).astype(
            jnp.bfloat16
        )

        @pl.when(step == at_ref[0])
        def _():
            hidden_ref[...] = hidden

    return pl.pallas_call(
        kernel,
        grid_spec=pltpu.PrefetchScalarGridSpec(
            num_scalar_prefetch=1,
            grid=(groups,),
            in_specs=[
                pl.BlockSpec((groups, tile, group_columns), lambda i, at_ref: (0, i, 0)),
                pl.BlockSpec(first.shape, lambda i, at_ref: (0, 0, 0, 0)),
                pl.BlockSpec(second.shape, lambda i, at_ref: (0, 0, 0, 0)),
                pl.BlockSpec((1, tile, width), lambda i, at_ref: (i, 0, 0)),
                pl.BlockSpec((1, width), lambda i, at_ref: (0, 0)),
            ],
            out_specs=[
                pl.BlockSpec((tile, width), lambda i, at_ref: (0, 0)),
                pl.BlockSpec((tile, width), lambda i, at_ref: (i, 0)),
            ],
            scratch_shapes=[
                pltpu.VMEM((groups * group_columns, width), jnp.bfloat16),
                pltpu.VMEM((tile, groups * group_columns), jnp.bfloat16),
            ],
        ),
        out_shape=[
            jax.ShapeDtypeStruct((tile, width), jnp.float32),
            jax.ShapeDtypeStruct((rows, width), jnp.bfloat16),
        ],
        cost_estimate=pl.CostEstimate(
            flops=2 * rows * width * width, transcendentals=rows, bytes_accessed=20 << 20
        ),
        name="project_and_norm",
    )(places, all_heads, first, second, gathered, gain_vec.reshape(1, -1))


def gated_back(all_cot, w_down, gate_proj, up_proj):
    rows, width = all_cot.shape
    columns = w_down.shape[0]
    tile = 256

    def kernel(cot_ref, weight_ref, gate_ref, up_ref, d_gate_ref, d_up_ref):
        d_active = dot_lanes(cot_ref[...], weight_ref[...])
        gate = gate_ref[...]
        chance = jax.nn.sigmoid(gate)
        smooth = gate * chance
        d_up_ref[...] = (d_active * smooth).astype(jnp.bfloat16)
        slope = chance * (1.0 + gate * (1.0 - chance))
        d_gate_ref[...] = (d_active * up_ref[...] * slope).astype(jnp.bfloat16)

    column_block = pl.BlockSpec((rows, tile), lambda j: (0, j))
    return pl.pallas_call(
        kernel,
        grid=(columns // tile,),
        in_specs=[
            pl.BlockSpec((rows, width), lambda j: (0, 0)),
            pl.BlockSpec((tile, width), lambda j: (j, 0)),
            column_block,
            column_block,
        ],
        out_specs=[column_block] * 2,
        out_shape=[jax.ShapeDtypeStruct((rows, columns), jnp.bfloat16)] * 2,
        cost_estimate=pl.CostEstimate(
            flops=2 * rows * width * columns,
            transcendentals=rows * columns,
            bytes_accessed=36 << 20,
        ),
        name="gated_back",
    )(all_cot, w_down, gate_proj, up_proj)


def pair_product(first, first_weight, second, second_weight):
    rows, depth = first.shape
    columns = first_weight.shape[0]
    tile = 256

    def kernel(first_ref, second_ref, first_w_ref, second_w_ref, out_ref):
        out_ref[...] = (
            dot_lanes(first_ref[...], first_w_ref[...])
            + dot_lanes(second_ref[...], second_w_ref[...])
        ).astype(jnp.bfloat16)

    whole = pl.BlockSpec((rows, depth), lambda j: (0, 0))
    weight_block = pl.BlockSpec((tile, depth), lambda j: (j, 0))
    return pl.pallas_call(
        kernel,
        grid=(columns // tile,),
        in_specs=[whole, whole, weight_block, weight_block],
        out_specs=pl.BlockSpec((rows, tile), lambda j: (0, j)),
        out_shape=jax.ShapeDtypeStruct((rows, columns), jnp.bfloat16),
        cost_estimate=pl.CostEstimate(
            flops=4 * rows * depth * columns, transcendentals=0, bytes_accessed=28 << 20
        ),
        name="pair_product",
    )(first, second, first_weight, second_weight)


def gated_up(normed, w_gate, w_up):
    rows, width = normed.shape
    columns = w_gate.shape[1]
    tile = 256

    def kernel(normed_ref, gate_w_ref, up_w_ref, gate_ref, up_ref, active_ref):
        gate = jnp.dot(normed_ref[...], gate_w_ref[...], preferred_element_type=jnp.float32)
        up = jnp.dot(normed_ref[...], up_w_ref[...], preferred_element_type=jnp.float32)
        gate_ref[...] = gate
        up_ref[...] = up
        active_ref[...] = (gate * jax.nn.sigmoid(gate) * up).astype(jnp.bfloat16)

    column_block = pl.BlockSpec((rows, tile), lambda j: (0, j))
    weight_block = pl.BlockSpec((width, tile), lambda j: (0, j))
    return pl.pallas_call(
        kernel,
        grid=(columns // tile,),
        in_specs=[pl.BlockSpec((rows, width), lambda j: (0, 0)), weight_block, weight_block],
        out_specs=[column_block] * 3,
        out_shape=[
            jax.ShapeDtypeStruct((rows, columns), jnp.float32),
            jax.ShapeDtypeStruct((rows, columns), jnp.float32),
            jax.ShapeDtypeStruct((rows, columns), jnp.bfloat16),
        ],
        cost_estimate=pl.CostEstimate(
            flops=4 * rows * width * columns,
            transcendentals=rows * columns,
            bytes_accessed=40 << 20,
        ),
        name="gated_up",
    )(normed, w_gate, w_up)


def place_blocks(halves, axis):
    (first, first_offsets), (second, second_offsets) = halves
    parts, rows, half = first.shape

    def kernel(at_ref, first_ref, second_ref, out_ref):
        out_ref[:, :half] = first_ref[0].astype(jnp.float32)
        out_ref[:, half:] = second_ref[0].astype(jnp.float32)

    def entry(offsets):
        where = [offsets.index(k) for k in range(parts)]

        def index(k, at_ref):
            found = where[0]
            for candidate in range(1, parts):
                found = jnp.where(k == candidate, where[candidate], found)
            return (found, 0, 0)

        return pl.BlockSpec((1, rows, half), index)

    return pl.pallas_call(
        kernel,
        grid_spec=pltpu.PrefetchScalarGridSpec(
            num_scalar_prefetch=1,
            grid=(parts,),
            in_specs=[entry(first_offsets), entry(second_offsets)],
            out_specs=pl.BlockSpec((rows, 2 * half), lambda k, at_ref: (at_ref[0] ^ k, 0)),
        ),
        out_shape=jax.ShapeDtypeStruct((parts * rows, 2 * half), jnp.float32),
        cost_estimate=pl.CostEstimate(
            flops=0, transcendentals=0, bytes_accessed=12 * parts * rows * half
        ),
        name="place_blocks",
    )(lax.axis_index(axis).reshape(1), first, second)


def unpack_attention(shared, q_columns, k_columns, folds):
    rows, columns = shared.shape
    block = rows // folds
    ends = (q_columns, q_columns + k_columns, q_columns + 2 * k_columns)

    def kernel(shared_ref, query_ref, key_ref, value_ref, output_ref):
        query_ref[...] = shared_ref[:, : ends[0]].astype(jnp.float32)
        key_ref[...] = shared_ref[:, ends[0] : ends[1]].astype(jnp.float32)
        value_ref[...] = shared_ref[:, ends[1] : ends[2]].astype(jnp.float32)
        output_ref[...] = shared_ref[:, ends[2] :].astype(jnp.float32)

    narrow = pl.BlockSpec((block, k_columns), lambda p: (p, 0))
    return pl.pallas_call(
        kernel,
        grid=(folds,),
        in_specs=[pl.BlockSpec((block, columns), lambda p: (p, 0))],
        out_specs=[
            pl.BlockSpec((block, q_columns), lambda p: (p, 0)),
            narrow,
            narrow,
            pl.BlockSpec((block, columns - ends[2]), lambda p: (0, p)),
        ],
        out_shape=[
            jax.ShapeDtypeStruct((rows, q_columns), jnp.float32),
            jax.ShapeDtypeStruct((rows, k_columns), jnp.float32),
            jax.ShapeDtypeStruct((rows, k_columns), jnp.float32),
            jax.ShapeDtypeStruct((block, (columns - ends[2]) * folds), jnp.float32),
        ],
        cost_estimate=pl.CostEstimate(
            flops=0, transcendentals=0, bytes_accessed=6 * rows * columns
        ),
        name="unpack_attention",
    )(shared)


def row_major(array):
    return with_layout_constraint(array, Layout(major_to_minor=tuple(range(array.ndim))))


def split_columns(array, parts):
    if parts == 1:
        return array
    rows, columns = array.shape[0], array.shape[1] // parts
    return array.reshape(rows, parts, columns).swapaxes(0, 1).reshape(parts * rows, columns)


def join_columns(array, parts):
    if parts == 1:
        return array
    rows, columns = array.shape[0] // parts, array.shape[1]
    return array.reshape(parts, rows, columns).swapaxes(0, 1).reshape(rows, parts * columns)


def block(
    tokens,
    cotangent,
    norm1_gain,
    w_query,
    w_key,
    w_value,
    w_output,
    norm2_gain,
    w_gate,
    w_up,
    w_down,
):
    low = jnp.bfloat16
    n_dp = lax.axis_size("dp")
    nothing = scatter_sum(tokens[:, :128] * 0, "dp")[0, 0]
    own_rows, width = tokens.shape
    depth = w_output.shape[0] // n_dp
    gathered = lax.all_gather(tokens, "tensor", axis=0)
    own_part = lax.dynamic_slice_in_dim(w_output, lax.axis_index("dp") * depth, depth, 0)
    output_part = lax.all_gather(own_part, "tensor", axis=0)
    all_output = cube_gather(output_part, "dp")
    q_columns, k_columns = w_query.shape[1], w_key.shape[1]
    q_heads, kv_heads = q_columns // HD, k_columns // HD
    gain_one = norm1_gain.astype(jnp.float32)
    gain_two = norm2_gain.astype(jnp.float32)
    own_tokens = tokens.astype(jnp.float32)
    cos_table, sin_table = rope_tables(SEQLEN, HD)
    cos_rows, sin_rows = cos_table.T, sin_table.T
    weight_rows = jnp.concatenate([w_query.T, w_key.T, w_value.T], axis=0)
    normed1, projected = norm_project(
        gathered, own_rows, norm1_gain, weight_rows, cos_rows, sin_rows, q_columns + k_columns
    )
    heads_out, heads_rows, totals = attend(projected, q_heads, kv_heads)
    all_heads = lax.all_gather(heads_out, "tensor", axis=0)
    all_cot = gather_rows(cotangent, "tensor")
    hidden_state, normed2 = project_and_norm(
        all_heads, all_output, gathered, (gain_two + nothing.astype(jnp.float32))
    )
    gate_proj, up_proj, activated = gated_up(normed2, w_gate, w_up)
    mlp_part = jnp.dot(activated, w_down, preferred_element_type=jnp.float32).astype(low)
    ff_columns = w_gate.shape[1]
    ff_folds = w_gate.shape[0] // w_down.shape[0]
    grad_down = row_major(split_columns(contract_rows(activated, all_cot).astype(low), ff_folds))
    part_down = scatter_sum(grad_down, "dp")
    d_gate, d_up = gated_back(all_cot, w_down, gate_proj, up_proj)
    dn2_part = pair_product(d_gate, w_gate, d_up, w_up)
    d_normed2 = exchange_sum(dn2_part, "tensor")
    gate_up_grads = row_major(
        jnp.concatenate(
            [contract_rows(normed2, d_gate).astype(low), contract_rows(normed2, d_up).astype(low)],
            axis=1,
        )
    )
    part_gate_up = scatter_sum(gate_up_grads, "dp")
    half_width = mlp_part.shape[1] // 2
    mlp_sum_a = exchange_sum(mlp_part[:, :half_width], "tensor")
    mlp_sum_b = exchange_sum(mlp_part[:, half_width:], "tensor")
    output = (hidden_state + jnp.concatenate([mlp_sum_a, mlp_sum_b], axis=1)).astype(low)
    d_state = cotangent.astype(jnp.float32) + norm_backward(hidden_state, gain_two, d_normed2)
    d_state_low = gather_rows(d_state.astype(low), "tensor")
    gain_two_sum = cube_sum(gain_gradient(hidden_state, d_normed2), ("dp", "tensor"))
    d_heads_rows = contract_cols(w_output, d_state_low).astype(low)
    d_query, d_key, d_value = attend_back(
        projected, d_heads_rows, totals, cos_rows, sin_rows, q_heads, kv_heads
    )
    d_projected = jnp.concatenate([d_query, d_key, d_value], axis=0)
    dn1_part = contract_rows(d_projected, weight_rows).astype(low)
    d_normed1 = exchange_sum(dn1_part, "tensor")
    gain_one_sum = cube_sum(
        gain_gradient(
            gathered.reshape(-1, width).astype(jnp.float32),
            dn1_part.astype(jnp.float32),
        ), ("dp", "tensor")
    )
    folds = w_query.shape[0] // w_output.shape[0]
    grad_qkv = lax.dot_general(
        normed1,
        d_projected,
        (((0,), (1,)), ((), ())),
        preferred_element_type=jnp.float32,
    ).astype(low)
    grad_output = jnp.dot(heads_rows, d_state_low, preferred_element_type=jnp.float32).astype(low)
    low_attn = row_major(
        jnp.concatenate([grad_qkv, split_columns(grad_output, folds)], axis=1)
    )
    part_attn = scatter_sum(low_attn, "dp")
    down_halves = cube_gather(part_down, "dp")
    full_down = join_columns(place_blocks(down_halves, "dp"), ff_folds)
    shared_ff = row_major(gather_rows(part_gate_up, "dp"))
    shared_attn = row_major(gather_rows(part_attn, "dp"))
    input_grad = (d_state + norm_backward(own_tokens, gain_one, d_normed1)).astype(low)
    full_gate = shared_ff[:, :ff_columns].astype(jnp.float32)
    full_up = shared_ff[:, ff_columns:].astype(jnp.float32)
    full_query, full_key, full_value, full_output = unpack_attention(
        shared_attn, q_columns, k_columns, folds
    )
    return (
        output,
        input_grad,
        gain_one_sum,
        full_query,
        full_key,
        full_value,
        full_output,
        gain_two_sum,
        full_gate,
        full_up,
        full_down,
    )


def solution(mesh):
    return jax.shard_map(
        block,
        mesh=mesh,
        in_specs=(
            P(("dp", "tensor"), None),
            P(("dp", "tensor"), None),
            P(),
            P(None, "tensor"),
            P(None, "tensor"),
            P(None, "tensor"),
            P("tensor", None),
            P(),
            P(None, "tensor"),
            P(None, "tensor"),
            P("tensor", None),
        ),
        out_specs=(
            P(("dp", "tensor"), None),
            P(("dp", "tensor"), None),
            P(),
            P(None, "tensor"),
            P(None, "tensor"),
            P(None, "tensor"),
            P("tensor", None),
            P(),
            P(None, "tensor"),
            P(None, "tensor"),
            P("tensor", None),
        ),
        check_vma=False,
    )
```

```python
import functools

import jax
import jax.numpy as jnp
from jax import lax
from jax.experimental import pallas as pl
from jax.experimental.pallas import tpu as pltpu
from jax.experimental.layout import Layout, with_layout_constraint
from jax.sharding import PartitionSpec as P


LOW = jnp.bfloat16
DP, TP = "dp", "tensor"

HD = 64
SEQLEN = 512


EPS = 1e-05
ROPE_BASE = 500000.0
MASKED = -1e30


def rope_tables(length, columns):
    half_width = columns // 2
    frequency = ROPE_BASE ** (-(jnp.arange(half_width, dtype=jnp.float32) * 2.0 / columns))
    angles = jnp.arange(length, dtype=jnp.float32)[:, None] * frequency[None, :]
    return (jnp.cos(angles), jnp.sin(angles))


def contract_rows(left_side, right_side):
    return lax.dot_general(
        left_side, right_side, (((0,), (0,)), ((), ())), preferred_element_type=jnp.float32
    )


def contract_cols(left_side, right_side):
    return lax.dot_general(
        left_side, right_side, (((1,), (1,)), ((), ())), preferred_element_type=jnp.float32
    )


def gather_rows(block, axis):
    return lax.all_gather(block, axis, axis=0, tiled=True)


def scatter_sum(partial, axis):
    return lax.psum_scatter(partial, axis, scatter_dimension=0, tiled=True)


def cube_gather(blocks, axis):
    n = lax.axis_size(axis)
    bits = [1 << b for b in range(n.bit_length() - 1)]
    half = blocks.shape[-1] // 2
    halves = []
    for part, order in (
        (blocks[..., :half], bits[1:] + bits[:1]),
        (blocks[..., half:], bits[:0:-1] + bits[:1]),
    ):
        held, offsets = part[None], [0]
        for bit in order:
            moved = lax.ppermute(held, axis, [(i, i ^ bit) for i in range(n)])
            held = jnp.concatenate([held, moved], axis=0)
            offsets = offsets + [o ^ bit for o in offsets]
        halves.append((held, tuple(offsets)))
    return halves


def cube_sum(vector, axes):
    for axis in axes:
        n = lax.axis_size(axis)
        bit = 1
        while bit < n:
            vector = vector + lax.ppermute(vector, axis, [(i, i ^ bit) for i in range(n)])
            bit *= 2
    return vector


def rotate_rows(values, cos_rows, sin_rows):
    half = HD // 2
    heads = []
    for h in range(values.shape[0] // HD):
        upper = values[h * HD : h * HD + half]
        lower = values[h * HD + half : (h + 1) * HD]
        heads.append(upper * cos_rows - lower * sin_rows)
        heads.append(lower * cos_rows + upper * sin_rows)
    return jnp.concatenate(heads, axis=0)


def dot_lanes(left_side, right_side):
    return lax.dot_general(
        left_side, right_side, (((1,), (1,)), ((), ())), preferred_element_type=jnp.float32
    )


def norm_project(gathered, gain_vec, weight_rows, cos_rows, sin_rows, group):
    blocks, tile, width = gathered.shape
    rows = blocks * tile
    columns = weight_rows.shape[0]
    packed = (group + 2) * HD

    def kernel(tokens_ref, gain_ref, weight_ref, cos_ref, sin_ref, normed_ref, out_ref):
        values = tokens_ref[0].astype(jnp.float32)
        row_scale = lax.rsqrt(jnp.mean(values * values, axis=-1, keepdims=True) + EPS)
        normed = (values * row_scale * gain_ref[...].astype(jnp.float32)).astype(LOW)
        normed_ref[...] = normed
        projected = dot_lanes(weight_ref[...], normed)
        for start in range(0, columns, packed):
            turned = start + packed - HD
            out_ref[start:turned] = rotate_rows(
                projected[start:turned], cos_ref[...], sin_ref[...]
            ).astype(LOW)
            out_ref[turned : turned + HD] = projected[turned : turned + HD].astype(LOW)

    half = HD // 2
    return pl.pallas_call(
        kernel,
        grid=(blocks,),
        in_specs=[
            pl.BlockSpec((1, tile, width), lambda i: (i, 0, 0)),
            pl.BlockSpec((1, width), lambda i: (0, 0)),
            pl.BlockSpec((columns, width), lambda i: (0, 0)),
            pl.BlockSpec((half, tile), lambda i: (0, i % (SEQLEN // tile))),
            pl.BlockSpec((half, tile), lambda i: (0, i % (SEQLEN // tile))),
        ],
        out_specs=[
            pl.BlockSpec((tile, width), lambda i: (i, 0)),
            pl.BlockSpec((columns, tile), lambda i: (0, i)),
        ],
        out_shape=[
            jax.ShapeDtypeStruct((rows, width), LOW),
            jax.ShapeDtypeStruct((columns, rows), LOW),
        ],
        cost_estimate=pl.CostEstimate(
            flops=2 * rows * width * columns, transcendentals=rows, bytes_accessed=12 << 20
        ),
        name="norm_project",
    )(gathered, gain_vec.reshape(1, -1), weight_rows, cos_rows, sin_rows)


def key_tiles(step, tile):
    return [(t * tile, t == step) for t in range(step + 1)]


def causal_tile(tile):
    key_at = lax.broadcasted_iota(jnp.int32, (tile, tile), 0)
    query_at = lax.broadcasted_iota(jnp.int32, (tile, tile), 1)
    return key_at <= query_at


def attend(projected, group):
    columns, rows = projected.shape
    packed = (group + 2) * HD
    kv_heads = columns // packed
    wide = group * HD
    tile = 256
    score_scale = HD ** (-0.5)

    def kernel(packed_ref, heads_ref, heads_t_ref, total_ref):
        keys = packed_ref[wide : wide + HD].astype(jnp.float32).T.astype(LOW)
        visible = causal_tile(tile)
        for step in range(SEQLEN // tile):
            here = slice(step * tile, (step + 1) * tile)
            for h in range(group):
                query = packed_ref[h * HD : (h + 1) * HD, here]
                parts = []
                for start, masked in key_tiles(step, tile):
                    part = jnp.dot(
                        keys[start : start + tile], query, preferred_element_type=jnp.float32
                    )
                    parts.append(jnp.where(visible, part, MASKED) if masked else part)
                top = functools.reduce(
                    jnp.maximum, [jnp.max(part, axis=0, keepdims=True) for part in parts]
                )
                parts = [jnp.exp((part - top) * score_scale) for part in parts]
                total = sum(jnp.sum(part, axis=0, keepdims=True) for part in parts)
                inverse = 1.0 / total
                mixed = sum(
                    jnp.dot(
                        packed_ref[wide + HD : packed, start : start + tile],
                        (part * inverse).astype(LOW),
                        preferred_element_type=jnp.float32,
                    )
                    for part, (start, _) in zip(parts, key_tiles(step, tile))
                )
                heads_t_ref[h * HD : (h + 1) * HD, here] = mixed.astype(LOW)
                total_ref[0, h : h + 1, here] = top * score_scale + jnp.log(total)
        heads_ref[...] = heads_t_ref[...].astype(jnp.float32).T.astype(LOW)

    return pl.pallas_call(
        kernel,
        grid=(rows // SEQLEN, kv_heads),
        in_specs=[pl.BlockSpec((packed, SEQLEN), lambda s, j: (j, s))],
        out_specs=[
            pl.BlockSpec((SEQLEN, wide), lambda s, j: (s, j)),
            pl.BlockSpec((wide, SEQLEN), lambda s, j: (j, s)),
            pl.BlockSpec((1, group, SEQLEN), lambda s, j: (j, 0, s)),
        ],
        out_shape=[
            jax.ShapeDtypeStruct((rows, kv_heads * wide), LOW),
            jax.ShapeDtypeStruct((kv_heads * wide, rows), LOW),
            jax.ShapeDtypeStruct((kv_heads, group, rows), jnp.float32),
        ],
        cost_estimate=pl.CostEstimate(
            flops=4 * rows * SEQLEN * kv_heads * wide,
            transcendentals=rows * SEQLEN * kv_heads * group,
            bytes_accessed=4 << 20,
        ),
        name="attend",
    )(projected)


def attend_back(projected, d_heads, totals, cos_rows, sin_rows):
    columns, rows = projected.shape
    kv_heads, group, _ = totals.shape
    packed = (group + 2) * HD
    wide = group * HD
    tile = 256
    score_scale = HD ** (-0.5)

    def kernel(
        packed_ref, d_heads_ref, total_ref, cos_ref, sin_ref, out_ref, key_sum, value_sum
    ):
        keys = packed_ref[wide : wide + HD].astype(jnp.float32).T.astype(LOW)
        values = packed_ref[wide + HD : packed].astype(jnp.float32).T.astype(LOW)
        visible = causal_tile(tile)
        key_sum[...] = jnp.zeros_like(key_sum)
        value_sum[...] = jnp.zeros_like(value_sum)
        for step in range(SEQLEN // tile):
            here = slice(step * tile, (step + 1) * tile)
            for h in range(group):
                query = packed_ref[h * HD : (h + 1) * HD, here]
                d_head = d_heads_ref[h * HD : (h + 1) * HD, here]
                log_total = total_ref[0, h : h + 1, here]
                probs, d_probs = [], []
                for start, masked in key_tiles(step, tile):
                    span = slice(start, start + tile)
                    part = jnp.dot(keys[span], query, preferred_element_type=jnp.float32)
                    part = jnp.exp(part * score_scale - log_total)
                    if masked:
                        part = jnp.where(visible, part, 0.0)
                    probs.append(part)
                    value_sum[:, span] += dot_lanes(d_head, part.astype(LOW))
                    d_probs.append(
                        jnp.dot(values[span], d_head, preferred_element_type=jnp.float32)
                    )
                row_sum = sum(
                    jnp.sum(part * d_part, axis=0, keepdims=True)
                    for part, d_part in zip(probs, d_probs)
                )
                d_query = jnp.zeros((HD, tile), jnp.float32)
                for (start, _), part, d_part in zip(key_tiles(step, tile), probs, d_probs):
                    span = slice(start, start + tile)
                    d_scores = (part * (d_part - row_sum)).astype(LOW)
                    d_query += jnp.dot(
                        packed_ref[wide : wide + HD, span],
                        d_scores,
                        preferred_element_type=jnp.float32,
                    )
                    key_sum[:, span] += dot_lanes(query, d_scores)
                out_ref[h * HD : (h + 1) * HD, here] = rotate_rows(
                    d_query * score_scale, cos_ref[:, here], -sin_ref[:, here]
                ).astype(LOW)
        out_ref[wide : wide + HD] = rotate_rows(
            key_sum[...] * score_scale, cos_ref[...], -sin_ref[...]
        ).astype(LOW)
        out_ref[wide + HD : packed] = value_sum[...].astype(LOW)

    half = HD // 2
    return pl.pallas_call(
        kernel,
        grid=(rows // SEQLEN, kv_heads),
        in_specs=[
            pl.BlockSpec((packed, SEQLEN), lambda s, j: (j, s)),
            pl.BlockSpec((wide, SEQLEN), lambda s, j: (j, s)),
            pl.BlockSpec((1, group, SEQLEN), lambda s, j: (j, 0, s)),
            pl.BlockSpec((half, SEQLEN), lambda s, j: (0, 0)),
            pl.BlockSpec((half, SEQLEN), lambda s, j: (0, 0)),
        ],
        out_specs=pl.BlockSpec((packed, SEQLEN), lambda s, j: (j, s)),
        out_shape=jax.ShapeDtypeStruct((columns, rows), LOW),
        scratch_shapes=[
            pltpu.VMEM((HD, SEQLEN), jnp.float32),
            pltpu.VMEM((HD, SEQLEN), jnp.float32),
        ],
        cost_estimate=pl.CostEstimate(
            flops=10 * rows * SEQLEN * kv_heads * wide,
            transcendentals=rows * SEQLEN * kv_heads * group,
            bytes_accessed=6 << 20,
        ),
        name="attend_back",
    )(projected, d_heads, totals, cos_rows, sin_rows)


def project_and_norm(all_heads, weights, gathered, gain_vec):
    groups, rows, group_columns = all_heads.shape
    (first, first_offsets), (second, second_offsets) = weights
    parts, _, depth, half = first.shape
    width = 2 * half
    tile = rows // groups
    places = jnp.stack([lax.axis_index(TP), lax.axis_index(DP)])

    def kernel(
        at_ref,
        heads_ref,
        first_ref,
        second_ref,
        tokens_ref,
        gain_ref,
        hidden_ref,
        normed_ref,
        weight_ref,
        wide_ref,
    ):
        step = pl.program_id(0)

        @pl.when(step == 0)
        def _():
            for side, part_ref, offsets in (
                (0, first_ref, first_offsets),
                (half, second_ref, second_offsets),
            ):
                for part in range(parts):
                    for g in range(groups):
                        start = g * group_columns + (at_ref[1] ^ offsets[part]) * depth
                        at = pl.ds(pl.multiple_of(start, depth), depth)
                        weight_ref[at, side : side + half] = part_ref[part, g]

        for g in range(groups):
            wide_ref[:, g * group_columns : (g + 1) * group_columns] = heads_ref[g]
        hidden = tokens_ref[0].astype(jnp.float32) + jnp.dot(
            wide_ref[...], weight_ref[...], preferred_element_type=jnp.float32
        )
        row_scale = lax.rsqrt(jnp.mean(hidden * hidden, axis=-1, keepdims=True) + EPS)
        normed_ref[...] = (hidden * row_scale * gain_ref[...].astype(jnp.float32)).astype(
            LOW
        )

        @pl.when(step == at_ref[0])
        def _():
            hidden_ref[...] = hidden

    return pl.pallas_call(
        kernel,
        grid_spec=pltpu.PrefetchScalarGridSpec(
            num_scalar_prefetch=1,
            grid=(groups,),
            in_specs=[
                pl.BlockSpec((groups, tile, group_columns), lambda i, at_ref: (0, i, 0)),
                pl.BlockSpec(first.shape, lambda i, at_ref: (0, 0, 0, 0)),
                pl.BlockSpec(second.shape, lambda i, at_ref: (0, 0, 0, 0)),
                pl.BlockSpec((1, tile, width), lambda i, at_ref: (i, 0, 0)),
                pl.BlockSpec((1, width), lambda i, at_ref: (0, 0)),
            ],
            out_specs=[
                pl.BlockSpec((tile, width), lambda i, at_ref: (0, 0)),
                pl.BlockSpec((tile, width), lambda i, at_ref: (i, 0)),
            ],
            scratch_shapes=[
                pltpu.VMEM((groups * group_columns, width), LOW),
                pltpu.VMEM((tile, groups * group_columns), LOW),
            ],
        ),
        out_shape=[
            jax.ShapeDtypeStruct((tile, width), jnp.float32),
            jax.ShapeDtypeStruct((rows, width), LOW),
        ],
        cost_estimate=pl.CostEstimate(
            flops=2 * rows * width * width, transcendentals=rows, bytes_accessed=20 << 20
        ),
        name="project_and_norm",
    )(places, all_heads, first, second, gathered, gain_vec.reshape(1, -1))


def gated_up(normed, w_gate, w_up):
    rows, width = normed.shape
    columns = w_gate.shape[1]
    tile = 256

    def kernel(normed_ref, gate_w_ref, up_w_ref, gate_ref, up_ref, active_ref):
        gate = jnp.dot(normed_ref[...], gate_w_ref[...], preferred_element_type=jnp.float32)
        up = jnp.dot(normed_ref[...], up_w_ref[...], preferred_element_type=jnp.float32)
        gate_ref[...] = gate
        up_ref[...] = up
        active_ref[...] = (gate * jax.nn.sigmoid(gate) * up).astype(LOW)

    column_block = pl.BlockSpec((rows, tile), lambda j: (0, j))
    weight_block = pl.BlockSpec((width, tile), lambda j: (0, j))
    return pl.pallas_call(
        kernel,
        grid=(columns // tile,),
        in_specs=[pl.BlockSpec((rows, width), lambda j: (0, 0)), weight_block, weight_block],
        out_specs=[column_block] * 3,
        out_shape=[
            jax.ShapeDtypeStruct((rows, columns), jnp.float32),
            jax.ShapeDtypeStruct((rows, columns), jnp.float32),
            jax.ShapeDtypeStruct((rows, columns), LOW),
        ],
        cost_estimate=pl.CostEstimate(
            flops=4 * rows * width * columns,
            transcendentals=rows * columns,
            bytes_accessed=40 << 20,
        ),
        name="gated_up",
    )(normed, w_gate, w_up)


def gated_back(all_cot, w_down, gate_proj, up_proj):
    rows, width = all_cot.shape
    columns = w_down.shape[0]
    tile = 256

    def kernel(cot_ref, weight_ref, gate_ref, up_ref, d_gate_ref, d_up_ref):
        d_active = dot_lanes(cot_ref[...], weight_ref[...])
        gate = gate_ref[...]
        chance = jax.nn.sigmoid(gate)
        smooth = gate * chance
        d_up_ref[...] = (d_active * smooth).astype(LOW)
        slope = chance * (1.0 + gate * (1.0 - chance))
        d_gate_ref[...] = (d_active * up_ref[...] * slope).astype(LOW)

    column_block = pl.BlockSpec((rows, tile), lambda j: (0, j))
    return pl.pallas_call(
        kernel,
        grid=(columns // tile,),
        in_specs=[
            pl.BlockSpec((rows, width), lambda j: (0, 0)),
            pl.BlockSpec((tile, width), lambda j: (j, 0)),
            column_block,
            column_block,
        ],
        out_specs=[column_block] * 2,
        out_shape=[jax.ShapeDtypeStruct((rows, columns), LOW)] * 2,
        cost_estimate=pl.CostEstimate(
            flops=2 * rows * width * columns,
            transcendentals=rows * columns,
            bytes_accessed=36 << 20,
        ),
        name="gated_back",
    )(all_cot, w_down, gate_proj, up_proj)


def pair_product(place, tile, first, first_weight, second, second_weight):
    depth = first.shape[1]
    columns = first_weight.shape[0]
    part = min(columns, 512)

    def kernel(at_ref, first_ref, second_ref, first_w_ref, second_w_ref, out_ref):
        out_ref[...] = (
            dot_lanes(first_ref[...], first_w_ref[...])
            + dot_lanes(second_ref[...], second_w_ref[...])
        ).astype(LOW)

    here = pl.BlockSpec((tile, depth), lambda j, at_ref: (at_ref[0], 0))
    weight_block = pl.BlockSpec((part, depth), lambda j, at_ref: (j, 0))
    return pl.pallas_call(
        kernel,
        grid_spec=pltpu.PrefetchScalarGridSpec(
            num_scalar_prefetch=1,
            grid=(columns // part,),
            in_specs=[here, here, weight_block, weight_block],
            out_specs=pl.BlockSpec((tile, part), lambda j, at_ref: (0, j)),
        ),
        out_shape=jax.ShapeDtypeStruct((tile, columns), LOW),
        cost_estimate=pl.CostEstimate(
            flops=4 * tile * depth * columns, transcendentals=0, bytes_accessed=20 << 20
        ),
        name="pair_product",
    )(place.reshape(1), first, second, first_weight, second_weight)


def projection_back(place, d_projected, weight_rows, gathered):
    columns, width = weight_rows.shape
    tile = gathered.shape[1]
    part = 128

    def kernel(at_ref, d_ref, weight_ref, tokens_ref, out_ref, gain_ref):
        step = pl.program_id(0)
        grads = d_ref[...].astype(jnp.float32).T.astype(LOW)
        block = jnp.dot(grads, weight_ref[...], preferred_element_type=jnp.float32).astype(LOW)
        out_ref[...] = block
        values = tokens_ref[0].astype(jnp.float32)
        row_scale = lax.rsqrt(jnp.mean(values * values, axis=-1, keepdims=True) + EPS)
        added = jnp.sum(block.astype(jnp.float32) * values * row_scale, axis=0, keepdims=True)
        gain_ref[...] = jnp.where(step == 0, added, gain_ref[...] + added)

    return pl.pallas_call(
        kernel,
        grid_spec=pltpu.PrefetchScalarGridSpec(
            num_scalar_prefetch=1,
            grid=(tile // part,),
            in_specs=[
                pl.BlockSpec(
                    (columns, part), lambda i, at_ref: (0, at_ref[0] * (tile // part) + i)
                ),
                pl.BlockSpec((columns, width), lambda i, at_ref: (0, 0)),
                pl.BlockSpec((1, part, width), lambda i, at_ref: (at_ref[0], i, 0)),
            ],
            out_specs=[
                pl.BlockSpec((part, width), lambda i, at_ref: (i, 0)),
                pl.BlockSpec((1, width), lambda i, at_ref: (0, 0)),
            ],
        ),
        out_shape=[
            jax.ShapeDtypeStruct((tile, width), LOW),
            jax.ShapeDtypeStruct((1, width), jnp.float32),
        ],
        cost_estimate=pl.CostEstimate(
            flops=2 * tile * columns * width, transcendentals=0, bytes_accessed=6 << 20
        ),
        name="projection_back",
    )(place.reshape(1), d_projected, weight_rows, gathered)


def norm_back(values, gain_vec, base, blocks):
    rows, width = values.shape
    part = 64
    count = len(blocks)

    def kernel(values_ref, gain_ref, base_ref, *refs):
        wide_ref, low_ref, sum_ref = refs[count:]
        step = pl.program_id(0)
        upstream = sum(ref[...].astype(jnp.float32) for ref in refs[:count])
        held = values_ref[...].astype(jnp.float32)
        row_scale = lax.rsqrt(jnp.mean(held * held, axis=-1, keepdims=True) + EPS)
        scaled = held * row_scale
        added = jnp.sum(upstream * scaled, axis=0, keepdims=True)
        sum_ref[...] = jnp.where(step == 0, added, sum_ref[...] + added)
        weighted = upstream * gain_ref[...].astype(jnp.float32)
        inner = jnp.mean(weighted * scaled, axis=-1, keepdims=True)
        result = base_ref[...].astype(jnp.float32) + row_scale * (weighted - scaled * inner)
        wide_ref[...] = result
        low_ref[...] = result.astype(LOW)

    tile_block = pl.BlockSpec((part, width), lambda i: (i, 0))
    line = pl.BlockSpec((1, width), lambda i: (0, 0))
    return pl.pallas_call(
        kernel,
        grid=(rows // part,),
        in_specs=[tile_block, line, tile_block] + [tile_block] * count,
        out_specs=[tile_block, tile_block, line],
        out_shape=[
            jax.ShapeDtypeStruct((rows, width), jnp.float32),
            jax.ShapeDtypeStruct((rows, width), LOW),
            jax.ShapeDtypeStruct((1, width), jnp.float32),
        ],
        cost_estimate=pl.CostEstimate(
            flops=16 * rows * width, transcendentals=rows, bytes_accessed=10 << 20
        ),
        name="norm_back",
    )(values, gain_vec.reshape(1, -1), base, *blocks)


def exchange(make_block, axis):
    n = lax.axis_size(axis)
    me = lax.axis_index(axis)
    blocks = []
    for hop in range(1, n):
        made = make_block((me + hop) % n)
        blocks.append(lax.ppermute(made, axis, [(i, (i + hop) % n) for i in range(n)]))
    blocks.append(make_block(me))
    return blocks


def place_blocks(halves, axis):
    (first, first_offsets), (second, second_offsets) = halves
    parts, rows, half = first.shape

    def kernel(at_ref, first_ref, second_ref, out_ref):
        out_ref[:, :half] = first_ref[0].astype(jnp.float32)
        out_ref[:, half:] = second_ref[0].astype(jnp.float32)

    def entry(offsets):
        where = [offsets.index(k) for k in range(parts)]

        def index(k, at_ref):
            found = where[0]
            for candidate in range(1, parts):
                found = jnp.where(k == candidate, where[candidate], found)
            return (found, 0, 0)

        return pl.BlockSpec((1, rows, half), index)

    return pl.pallas_call(
        kernel,
        grid_spec=pltpu.PrefetchScalarGridSpec(
            num_scalar_prefetch=1,
            grid=(parts,),
            in_specs=[entry(first_offsets), entry(second_offsets)],
            out_specs=pl.BlockSpec((rows, 2 * half), lambda k, at_ref: (at_ref[0] ^ k, 0)),
        ),
        out_shape=jax.ShapeDtypeStruct((parts * rows, 2 * half), jnp.float32),
        cost_estimate=pl.CostEstimate(
            flops=0, transcendentals=0, bytes_accessed=12 * parts * rows * half
        ),
        name="place_blocks",
    )(lax.axis_index(axis).reshape(1), first, second)


def unpack_attention(shared, q_columns, k_columns, folds):
    rows, columns = shared.shape
    block = rows // folds
    kv_heads = k_columns // HD
    wide = q_columns // kv_heads
    packed = wide + 2 * HD
    end = kv_heads * packed

    def kernel(shared_ref, query_ref, key_ref, value_ref, output_ref):
        for j in range(kv_heads):
            start = j * packed
            query_ref[:, j * wide : (j + 1) * wide] = shared_ref[
                :, start : start + wide
            ].astype(jnp.float32)
            for at, ref in ((start + wide, key_ref), (start + wide + HD, value_ref)):
                ref[:, j * HD : (j + 1) * HD] = shared_ref[:, at : at + HD].astype(jnp.float32)
        output_ref[...] = shared_ref[:, end:].astype(jnp.float32)

    narrow = pl.BlockSpec((block, k_columns), lambda p: (p, 0))
    return pl.pallas_call(
        kernel,
        grid=(folds,),
        in_specs=[pl.BlockSpec((block, columns), lambda p: (p, 0))],
        out_specs=[
            pl.BlockSpec((block, q_columns), lambda p: (p, 0)),
            narrow,
            narrow,
            pl.BlockSpec((block, columns - end), lambda p: (0, p)),
        ],
        out_shape=[
            jax.ShapeDtypeStruct((rows, q_columns), jnp.float32),
            jax.ShapeDtypeStruct((rows, k_columns), jnp.float32),
            jax.ShapeDtypeStruct((rows, k_columns), jnp.float32),
            jax.ShapeDtypeStruct((block, (columns - end) * folds), jnp.float32),
        ],
        cost_estimate=pl.CostEstimate(
            flops=0, transcendentals=0, bytes_accessed=6 * rows * columns
        ),
        name="unpack_attention",
    )(shared)


def add_all(blocks):
    return sum(block.astype(jnp.float32) for block in blocks)


def row_major(array):
    return with_layout_constraint(array, Layout(major_to_minor=tuple(range(array.ndim))))


def split_columns(array, parts):
    if parts == 1:
        return array
    rows, columns = array.shape[0], array.shape[1] // parts
    return array.reshape(rows, parts, columns).swapaxes(0, 1).reshape(parts * rows, columns)


def join_columns(array, parts):
    if parts == 1:
        return array
    rows, columns = array.shape[0] // parts, array.shape[1]
    return array.reshape(parts, rows, columns).swapaxes(0, 1).reshape(rows, parts * columns)


def block(
    tokens,
    cotangent,
    norm1_gain,
    w_query,
    w_key,
    w_value,
    w_output,
    norm2_gain,
    w_gate,
    w_up,
    w_down,
):
    n_dp = lax.axis_size(DP)
    own_rows, width = tokens.shape
    depth = w_output.shape[0] // n_dp
    q_columns, k_columns = w_query.shape[1], w_key.shape[1]
    kv_heads = k_columns // HD
    group = q_columns // k_columns
    ff_columns = w_gate.shape[1]
    ff_folds = width // w_down.shape[0]
    folds = width // w_output.shape[0]
    nothing = scatter_sum(tokens[:, :128] * 0, DP)[0, 0]
    gathered = lax.all_gather(tokens, TP, axis=0)
    own_part = lax.dynamic_slice_in_dim(w_output, lax.axis_index(DP) * depth, depth, 0)
    output_part = lax.all_gather(own_part, TP, axis=0)
    all_output = cube_gather(output_part, DP)
    cos_table, sin_table = rope_tables(SEQLEN, HD)
    cos_rows, sin_rows = cos_table.T, sin_table.T
    pieces = []
    for j in range(kv_heads):
        pieces.append(w_query[:, j * group * HD : (j + 1) * group * HD].T)
        pieces.append(w_key[:, j * HD : (j + 1) * HD].T)
        pieces.append(w_value[:, j * HD : (j + 1) * HD].T)
    weight_rows = jnp.concatenate(pieces, axis=0)
    normed1, projected = norm_project(
        gathered, norm1_gain, weight_rows, cos_rows, sin_rows, group
    )
    heads_out, heads_rows, totals = attend(projected, group)
    all_heads = lax.all_gather(heads_out, TP, axis=0)
    all_cot = gather_rows(cotangent, TP)
    hidden_state, normed2 = project_and_norm(
        all_heads, all_output, gathered, norm2_gain.astype(jnp.float32) + nothing.astype(jnp.float32)
    )
    gate_proj, up_proj, activated = gated_up(normed2, w_gate, w_up)
    mlp_part = jnp.dot(activated, w_down, preferred_element_type=jnp.float32).astype(LOW)
    half_width = width // 2

    def part_of(columns):
        return lambda place: lax.dynamic_slice(
            mlp_part, (place * own_rows, columns), (own_rows, half_width)
        )

    first_half = exchange(part_of(0), TP)
    second_half = exchange(part_of(half_width), TP)
    output = (
        hidden_state
        + jnp.concatenate([add_all(first_half), add_all(second_half)], axis=1)
    ).astype(LOW)
    d_gate, d_up = gated_back(all_cot, w_down, gate_proj, up_proj)
    grad_down = row_major(split_columns(contract_rows(activated, all_cot).astype(LOW), ff_folds))
    part_down = scatter_sum(grad_down, DP)
    dn2_blocks = exchange(
        lambda place: pair_product(place, own_rows, d_gate, w_gate, d_up, w_up), TP
    )
    gate_up_grads = row_major(
        jnp.concatenate(
            [contract_rows(normed2, d_gate).astype(LOW), contract_rows(normed2, d_up).astype(LOW)],
            axis=1,
        )
    )
    part_gate_up = scatter_sum(gate_up_grads, DP)
    d_state, state_low, gain_two = norm_back(hidden_state, norm2_gain, cotangent, dn2_blocks)
    d_state_low = gather_rows(state_low, TP)
    gain_two_sum = cube_sum(gain_two[0], (DP, TP))
    d_heads_rows = contract_cols(w_output, d_state_low).astype(LOW)
    d_projected = attend_back(projected, d_heads_rows, totals, cos_rows, sin_rows)
    gains = []

    def dn1_block(place):
        made, gain = projection_back(place, d_projected, weight_rows, gathered)
        gains.append(gain)
        return made

    dn1_blocks = exchange(dn1_block, TP)
    gain_one_sum = cube_sum(sum(gains)[0], (DP, TP))
    grad_qkv = lax.dot_general(
        normed1,
        d_projected,
        (((0,), (1,)), ((), ())),
        preferred_element_type=jnp.float32,
    ).astype(LOW)
    grad_output = jnp.dot(heads_rows, d_state_low, preferred_element_type=jnp.float32).astype(LOW)
    low_attn = row_major(
        jnp.concatenate([grad_qkv, split_columns(grad_output, folds)], axis=1)
    )
    part_attn = scatter_sum(low_attn, DP)
    down_halves = cube_gather(part_down, DP)
    full_down = join_columns(place_blocks(down_halves, DP), ff_folds)
    shared_ff = row_major(gather_rows(part_gate_up, DP))
    shared_attn = row_major(gather_rows(part_attn, DP))
    _, input_grad, _ = norm_back(tokens, norm1_gain, d_state, dn1_blocks)
    full_gate = shared_ff[:, :ff_columns].astype(jnp.float32)
    full_up = shared_ff[:, ff_columns:].astype(jnp.float32)
    full_query, full_key, full_value, full_output = unpack_attention(
        shared_attn, q_columns, k_columns, folds
    )
    return (
        output,
        input_grad,
        gain_one_sum,
        full_query,
        full_key,
        full_value,
        full_output,
        gain_two_sum,
        full_gate,
        full_up,
        full_down,
    )


ROWS, COLUMNS, HIDDEN = P((DP, TP), None), P(None, TP), P(TP, None)


def solution(mesh):
    return jax.shard_map(
        block,
        mesh=mesh,
        in_specs=(ROWS, ROWS, P(), COLUMNS, COLUMNS, COLUMNS, HIDDEN, P(), COLUMNS, COLUMNS, HIDDEN),
        out_specs=(ROWS, ROWS, P(), COLUMNS, COLUMNS, COLUMNS, HIDDEN, P(), COLUMNS, COLUMNS, HIDDEN),
        check_vma=False,
    )
```

```python
import functools

import jax
import jax.numpy as jnp
from jax import lax
from jax.experimental import pallas as pl
from jax.experimental.pallas import tpu as pltpu
from jax.experimental.layout import Layout, with_layout_constraint
from jax.sharding import PartitionSpec as P


LOW = jnp.bfloat16
DP, TP = "dp", "tensor"

HD = 64
SEQLEN = 512


EPS = 1e-05
ROPE_BASE = 500000.0
MASKED = -1e30


def rope_tables(length, columns):
    half_width = columns // 2
    frequency = ROPE_BASE ** (-(jnp.arange(half_width, dtype=jnp.float32) * 2.0 / columns))
    angles = jnp.arange(length, dtype=jnp.float32)[:, None] * frequency[None, :]
    return (jnp.cos(angles), jnp.sin(angles))


def contract_rows(left_side, right_side):
    return lax.dot_general(
        left_side, right_side, (((0,), (0,)), ((), ())), preferred_element_type=jnp.float32
    )


def contract_cols(left_side, right_side):
    return lax.dot_general(
        left_side, right_side, (((1,), (1,)), ((), ())), preferred_element_type=jnp.float32
    )


def gather_rows(block, axis):
    return lax.all_gather(block, axis, axis=0, tiled=True)


def scatter_sum(partial, axis):
    return lax.psum_scatter(partial, axis, scatter_dimension=0, tiled=True)


def cube_gather(blocks, axis):
    n = lax.axis_size(axis)
    bits = [1 << b for b in range(n.bit_length() - 1)]
    half = blocks.shape[-1] // 2
    halves = []
    for part, order in (
        (blocks[..., :half], bits[1:] + bits[:1]),
        (blocks[..., half:], bits[:0:-1] + bits[:1]),
    ):
        held, offsets = part[None], [0]
        for bit in order:
            moved = lax.ppermute(held, axis, [(i, i ^ bit) for i in range(n)])
            held = jnp.concatenate([held, moved], axis=0)
            offsets = offsets + [o ^ bit for o in offsets]
        halves.append((held, tuple(offsets)))
    return halves


def cube_sum(vector, axes):
    for axis in axes:
        n = lax.axis_size(axis)
        bit = 1
        while bit < n:
            vector = vector + lax.ppermute(vector, axis, [(i, i ^ bit) for i in range(n)])
            bit *= 2
    return vector


def rotate_rows(values, cos_rows, sin_rows):
    half = HD // 2
    heads = []
    for h in range(values.shape[0] // HD):
        upper = values[h * HD : h * HD + half]
        lower = values[h * HD + half : (h + 1) * HD]
        heads.append(upper * cos_rows - lower * sin_rows)
        heads.append(lower * cos_rows + upper * sin_rows)
    return jnp.concatenate(heads, axis=0)


def dot_lanes(left_side, right_side):
    return lax.dot_general(
        left_side, right_side, (((1,), (1,)), ((), ())), preferred_element_type=jnp.float32
    )


def norm_project(gathered, gain_vec, weight_rows, cos_rows, sin_rows, group):
    blocks, tile, width = gathered.shape
    rows = blocks * tile
    columns = weight_rows.shape[0]
    packed = (group + 2) * HD

    def kernel(tokens_ref, gain_ref, weight_ref, cos_ref, sin_ref, normed_ref, out_ref):
        values = tokens_ref[0].astype(jnp.float32)
        row_scale = lax.rsqrt(jnp.mean(values * values, axis=-1, keepdims=True) + EPS)
        normed = (values * row_scale * gain_ref[...].astype(jnp.float32)).astype(LOW)
        normed_ref[...] = normed
        projected = dot_lanes(weight_ref[...], normed)
        for start in range(0, columns, packed):
            turned = start + packed - HD
            out_ref[start:turned] = rotate_rows(
                projected[start:turned], cos_ref[...], sin_ref[...]
            ).astype(LOW)
            out_ref[turned : turned + HD] = projected[turned : turned + HD].astype(LOW)

    half = HD // 2
    return pl.pallas_call(
        kernel,
        grid=(blocks,),
        in_specs=[
            pl.BlockSpec((1, tile, width), lambda i: (i, 0, 0)),
            pl.BlockSpec((1, width), lambda i: (0, 0)),
            pl.BlockSpec((columns, width), lambda i: (0, 0)),
            pl.BlockSpec((half, tile), lambda i: (0, i % (SEQLEN // tile))),
            pl.BlockSpec((half, tile), lambda i: (0, i % (SEQLEN // tile))),
        ],
        out_specs=[
            pl.BlockSpec((tile, width), lambda i: (i, 0)),
            pl.BlockSpec((columns, tile), lambda i: (0, i)),
        ],
        out_shape=[
            jax.ShapeDtypeStruct((rows, width), LOW),
            jax.ShapeDtypeStruct((columns, rows), LOW),
        ],
        cost_estimate=pl.CostEstimate(
            flops=2 * rows * width * columns, transcendentals=rows, bytes_accessed=12 << 20
        ),
        name="norm_project",
    )(gathered, gain_vec.reshape(1, -1), weight_rows, cos_rows, sin_rows)


def key_tiles(step, tile):
    return [(t * tile, t == step) for t in range(step + 1)]


def causal_tile(tile):
    key_at = lax.broadcasted_iota(jnp.int32, (tile, tile), 0)
    query_at = lax.broadcasted_iota(jnp.int32, (tile, tile), 1)
    return key_at <= query_at


def attend(projected, group):
    columns, rows = projected.shape
    packed = (group + 2) * HD
    kv_heads = columns // packed
    wide = group * HD
    tile = 256
    score_scale = HD ** (-0.5)

    def kernel(packed_ref, heads_ref, heads_t_ref, total_ref):
        keys = packed_ref[wide : wide + HD].astype(jnp.float32).T.astype(LOW)
        visible = causal_tile(tile)
        for step in range(SEQLEN // tile):
            here = slice(step * tile, (step + 1) * tile)
            for h in range(group):
                query = packed_ref[h * HD : (h + 1) * HD, here]
                parts = []
                for start, masked in key_tiles(step, tile):
                    part = jnp.dot(
                        keys[start : start + tile], query, preferred_element_type=jnp.float32
                    )
                    parts.append(jnp.where(visible, part, MASKED) if masked else part)
                top = functools.reduce(
                    jnp.maximum, [jnp.max(part, axis=0, keepdims=True) for part in parts]
                )
                parts = [jnp.exp((part - top) * score_scale) for part in parts]
                total = sum(jnp.sum(part, axis=0, keepdims=True) for part in parts)
                inverse = 1.0 / total
                mixed = sum(
                    jnp.dot(
                        packed_ref[wide + HD : packed, start : start + tile],
                        (part * inverse).astype(LOW),
                        preferred_element_type=jnp.float32,
                    )
                    for part, (start, _) in zip(parts, key_tiles(step, tile))
                )
                heads_t_ref[h * HD : (h + 1) * HD, here] = mixed.astype(LOW)
                total_ref[0, h : h + 1, here] = top * score_scale + jnp.log(total)
        heads_ref[...] = heads_t_ref[...].astype(jnp.float32).T.astype(LOW)

    return pl.pallas_call(
        kernel,
        grid=(rows // SEQLEN, kv_heads),
        in_specs=[pl.BlockSpec((packed, SEQLEN), lambda s, j: (j, s))],
        out_specs=[
            pl.BlockSpec((SEQLEN, wide), lambda s, j: (s, j)),
            pl.BlockSpec((wide, SEQLEN), lambda s, j: (j, s)),
            pl.BlockSpec((1, group, SEQLEN), lambda s, j: (j, 0, s)),
        ],
        out_shape=[
            jax.ShapeDtypeStruct((rows, kv_heads * wide), LOW),
            jax.ShapeDtypeStruct((kv_heads * wide, rows), LOW),
            jax.ShapeDtypeStruct((kv_heads, group, rows), jnp.float32),
        ],
        cost_estimate=pl.CostEstimate(
            flops=4 * rows * SEQLEN * kv_heads * wide,
            transcendentals=rows * SEQLEN * kv_heads * group,
            bytes_accessed=4 << 20,
        ),
        name="attend",
    )(projected)


def attend_back(projected, d_heads, totals, cos_rows, sin_rows):
    columns, rows = projected.shape
    kv_heads, group, _ = totals.shape
    packed = (group + 2) * HD
    wide = group * HD
    tile = 256
    score_scale = HD ** (-0.5)

    def kernel(
        packed_ref, d_heads_ref, total_ref, cos_ref, sin_ref, out_ref, key_sum, value_sum
    ):
        keys = packed_ref[wide : wide + HD].astype(jnp.float32).T.astype(LOW)
        values = packed_ref[wide + HD : packed].astype(jnp.float32).T.astype(LOW)
        visible = causal_tile(tile)
        key_sum[...] = jnp.zeros_like(key_sum)
        value_sum[...] = jnp.zeros_like(value_sum)
        for step in range(SEQLEN // tile):
            here = slice(step * tile, (step + 1) * tile)
            for h in range(group):
                query = packed_ref[h * HD : (h + 1) * HD, here]
                d_head = d_heads_ref[h * HD : (h + 1) * HD, here]
                log_total = total_ref[0, h : h + 1, here]
                probs, d_probs = [], []
                for start, masked in key_tiles(step, tile):
                    span = slice(start, start + tile)
                    part = jnp.dot(keys[span], query, preferred_element_type=jnp.float32)
                    part = jnp.exp(part * score_scale - log_total)
                    if masked:
                        part = jnp.where(visible, part, 0.0)
                    probs.append(part)
                    value_sum[:, span] += dot_lanes(d_head, part.astype(LOW))
                    d_probs.append(
                        jnp.dot(values[span], d_head, preferred_element_type=jnp.float32)
                    )
                row_sum = sum(
                    jnp.sum(part * d_part, axis=0, keepdims=True)
                    for part, d_part in zip(probs, d_probs)
                )
                d_query = jnp.zeros((HD, tile), jnp.float32)
                for (start, _), part, d_part in zip(key_tiles(step, tile), probs, d_probs):
                    span = slice(start, start + tile)
                    d_scores = (part * (d_part - row_sum)).astype(LOW)
                    d_query += jnp.dot(
                        packed_ref[wide : wide + HD, span],
                        d_scores,
                        preferred_element_type=jnp.float32,
                    )
                    key_sum[:, span] += dot_lanes(query, d_scores)
                out_ref[h * HD : (h + 1) * HD, here] = rotate_rows(
                    d_query * score_scale, cos_ref[:, here], -sin_ref[:, here]
                ).astype(LOW)
        out_ref[wide : wide + HD] = rotate_rows(
            key_sum[...] * score_scale, cos_ref[...], -sin_ref[...]
        ).astype(LOW)
        out_ref[wide + HD : packed] = value_sum[...].astype(LOW)

    half = HD // 2
    return pl.pallas_call(
        kernel,
        grid=(rows // SEQLEN, kv_heads),
        in_specs=[
            pl.BlockSpec((packed, SEQLEN), lambda s, j: (j, s)),
            pl.BlockSpec((wide, SEQLEN), lambda s, j: (j, s)),
            pl.BlockSpec((1, group, SEQLEN), lambda s, j: (j, 0, s)),
            pl.BlockSpec((half, SEQLEN), lambda s, j: (0, 0)),
            pl.BlockSpec((half, SEQLEN), lambda s, j: (0, 0)),
        ],
        out_specs=pl.BlockSpec((packed, SEQLEN), lambda s, j: (j, s)),
        out_shape=jax.ShapeDtypeStruct((columns, rows), LOW),
        scratch_shapes=[
            pltpu.VMEM((HD, SEQLEN), jnp.float32),
            pltpu.VMEM((HD, SEQLEN), jnp.float32),
        ],
        cost_estimate=pl.CostEstimate(
            flops=10 * rows * SEQLEN * kv_heads * wide,
            transcendentals=rows * SEQLEN * kv_heads * group,
            bytes_accessed=6 << 20,
        ),
        name="attend_back",
    )(projected, d_heads, totals, cos_rows, sin_rows)


def project_and_norm(all_heads, weights, gathered, gain_vec):
    groups, rows, group_columns = all_heads.shape
    (first, first_offsets), (second, second_offsets) = weights
    parts, _, depth, half = first.shape
    width = 2 * half
    tile = rows // groups
    places = jnp.stack([lax.axis_index(TP), lax.axis_index(DP)])

    def kernel(
        at_ref,
        heads_ref,
        first_ref,
        second_ref,
        tokens_ref,
        gain_ref,
        hidden_ref,
        normed_ref,
        weight_ref,
        wide_ref,
    ):
        step = pl.program_id(0)

        @pl.when(step == 0)
        def _():
            for side, part_ref, offsets in (
                (0, first_ref, first_offsets),
                (half, second_ref, second_offsets),
            ):
                for part in range(parts):
                    for g in range(groups):
                        start = g * group_columns + (at_ref[1] ^ offsets[part]) * depth
                        at = pl.ds(pl.multiple_of(start, depth), depth)
                        weight_ref[at, side : side + half] = part_ref[part, g]

        for g in range(groups):
            wide_ref[:, g * group_columns : (g + 1) * group_columns] = heads_ref[g]
        hidden = tokens_ref[0].astype(jnp.float32) + jnp.dot(
            wide_ref[...], weight_ref[...], preferred_element_type=jnp.float32
        )
        row_scale = lax.rsqrt(jnp.mean(hidden * hidden, axis=-1, keepdims=True) + EPS)
        normed_ref[...] = (hidden * row_scale * gain_ref[...].astype(jnp.float32)).astype(
            LOW
        )

        @pl.when(step == at_ref[0])
        def _():
            hidden_ref[...] = hidden

    return pl.pallas_call(
        kernel,
        grid_spec=pltpu.PrefetchScalarGridSpec(
            num_scalar_prefetch=1,
            grid=(groups,),
            in_specs=[
                pl.BlockSpec((groups, tile, group_columns), lambda i, at_ref: (0, i, 0)),
                pl.BlockSpec(first.shape, lambda i, at_ref: (0, 0, 0, 0)),
                pl.BlockSpec(second.shape, lambda i, at_ref: (0, 0, 0, 0)),
                pl.BlockSpec((1, tile, width), lambda i, at_ref: (i, 0, 0)),
                pl.BlockSpec((1, width), lambda i, at_ref: (0, 0)),
            ],
            out_specs=[
                pl.BlockSpec((tile, width), lambda i, at_ref: (0, 0)),
                pl.BlockSpec((tile, width), lambda i, at_ref: (i, 0)),
            ],
            scratch_shapes=[
                pltpu.VMEM((groups * group_columns, width), LOW),
                pltpu.VMEM((tile, groups * group_columns), LOW),
            ],
        ),
        out_shape=[
            jax.ShapeDtypeStruct((tile, width), jnp.float32),
            jax.ShapeDtypeStruct((rows, width), LOW),
        ],
        cost_estimate=pl.CostEstimate(
            flops=2 * rows * width * width, transcendentals=rows, bytes_accessed=20 << 20
        ),
        name="project_and_norm",
    )(places, all_heads, first, second, gathered, gain_vec.reshape(1, -1))


def gated_up(normed, w_gate, w_up):
    rows, width = normed.shape
    columns = w_gate.shape[1]
    tile = 256

    def kernel(normed_ref, gate_w_ref, up_w_ref, gate_ref, up_ref, active_ref):
        gate = jnp.dot(normed_ref[...], gate_w_ref[...], preferred_element_type=jnp.float32)
        up = jnp.dot(normed_ref[...], up_w_ref[...], preferred_element_type=jnp.float32)
        gate_ref[...] = gate
        up_ref[...] = up
        active_ref[...] = (gate * jax.nn.sigmoid(gate) * up).astype(LOW)

    column_block = pl.BlockSpec((rows, tile), lambda j: (0, j))
    weight_block = pl.BlockSpec((width, tile), lambda j: (0, j))
    return pl.pallas_call(
        kernel,
        grid=(columns // tile,),
        in_specs=[pl.BlockSpec((rows, width), lambda j: (0, 0)), weight_block, weight_block],
        out_specs=[column_block] * 3,
        out_shape=[
            jax.ShapeDtypeStruct((rows, columns), jnp.float32),
            jax.ShapeDtypeStruct((rows, columns), jnp.float32),
            jax.ShapeDtypeStruct((rows, columns), LOW),
        ],
        cost_estimate=pl.CostEstimate(
            flops=4 * rows * width * columns,
            transcendentals=rows * columns,
            bytes_accessed=40 << 20,
        ),
        name="gated_up",
    )(normed, w_gate, w_up)


def gated_back(all_cot, w_down, gate_proj, up_proj):
    rows, width = all_cot.shape
    columns = w_down.shape[0]
    tile = 256

    def kernel(cot_ref, weight_ref, gate_ref, up_ref, d_gate_ref, d_up_ref):
        d_active = dot_lanes(cot_ref[...], weight_ref[...])
        gate = gate_ref[...]
        chance = jax.nn.sigmoid(gate)
        smooth = gate * chance
        d_up_ref[...] = (d_active * smooth).astype(LOW)
        slope = chance * (1.0 + gate * (1.0 - chance))
        d_gate_ref[...] = (d_active * up_ref[...] * slope).astype(LOW)

    column_block = pl.BlockSpec((rows, tile), lambda j: (0, j))
    return pl.pallas_call(
        kernel,
        grid=(columns // tile,),
        in_specs=[
            pl.BlockSpec((rows, width), lambda j: (0, 0)),
            pl.BlockSpec((tile, width), lambda j: (j, 0)),
            column_block,
            column_block,
        ],
        out_specs=[column_block] * 2,
        out_shape=[jax.ShapeDtypeStruct((rows, columns), LOW)] * 2,
        cost_estimate=pl.CostEstimate(
            flops=2 * rows * width * columns,
            transcendentals=rows * columns,
            bytes_accessed=36 << 20,
        ),
        name="gated_back",
    )(all_cot, w_down, gate_proj, up_proj)


def pair_product(places, tile, first, first_weight, second, second_weight):
    rows, depth = first.shape
    columns = first_weight.shape[0]
    count = len(places)
    part = 512 if count == 1 else 256
    at = jnp.stack(places)

    def kernel(at_ref, first_ref, second_ref, first_w_ref, second_w_ref, *out_refs):
        for k, out_ref in enumerate(out_refs):
            here = (
                slice(None)
                if count == 1
                else pl.ds(pl.multiple_of(at_ref[k] * tile, tile), tile)
            )
            out_ref[...] = (
                dot_lanes(first_ref[here, :], first_w_ref[...])
                + dot_lanes(second_ref[here, :], second_w_ref[...])
            ).astype(LOW)

    held = (
        pl.BlockSpec((tile, depth), lambda j, at_ref: (at_ref[0], 0))
        if count == 1
        else pl.BlockSpec((rows, depth), lambda j, at_ref: (0, 0))
    )
    weight_block = pl.BlockSpec((part, depth), lambda j, at_ref: (j, 0))
    return pl.pallas_call(
        kernel,
        grid_spec=pltpu.PrefetchScalarGridSpec(
            num_scalar_prefetch=1,
            grid=(columns // part,),
            in_specs=[held, held, weight_block, weight_block],
            out_specs=[pl.BlockSpec((tile, part), lambda j, at_ref: (0, j))] * count,
        ),
        out_shape=[jax.ShapeDtypeStruct((tile, columns), LOW)] * count,
        cost_estimate=pl.CostEstimate(
            flops=4 * count * tile * depth * columns, transcendentals=0, bytes_accessed=20 << 20
        ),
        name="pair_product",
    )(at, first, second, first_weight, second_weight)


def projection_back(places, d_projected, weight_rows, gathered):
    columns, width = weight_rows.shape
    tile = gathered.shape[1]
    count = len(places)
    at = jnp.stack(places)

    def kernel(at_ref, d_ref, weight_ref, tokens_ref, *out_refs):
        step = pl.program_id(0)
        grads = d_ref[...].astype(jnp.float32).T.astype(LOW)
        made = jnp.dot(grads, weight_ref[...], preferred_element_type=jnp.float32).astype(LOW)
        values = tokens_ref[0].astype(jnp.float32)
        row_scale = lax.rsqrt(jnp.mean(values * values, axis=-1, keepdims=True) + EPS)
        added = jnp.sum(made.astype(jnp.float32) * values * row_scale, axis=0, keepdims=True)
        gain_ref = out_refs[count]
        gain_ref[...] = jnp.where(step == 0, added, gain_ref[...] + added)
        for k in range(count):

            @pl.when(step == k)
            def _():
                out_refs[k][...] = made

    return pl.pallas_call(
        kernel,
        grid_spec=pltpu.PrefetchScalarGridSpec(
            num_scalar_prefetch=1,
            grid=(count,),
            in_specs=[
                pl.BlockSpec((columns, tile), lambda i, at_ref: (0, at_ref[i])),
                pl.BlockSpec((columns, width), lambda i, at_ref: (0, 0)),
                pl.BlockSpec((1, tile, width), lambda i, at_ref: (at_ref[i], 0, 0)),
            ],
            out_specs=[pl.BlockSpec((tile, width), lambda i, at_ref: (0, 0))] * count
            + [pl.BlockSpec((1, width), lambda i, at_ref: (0, 0))],
        ),
        out_shape=[jax.ShapeDtypeStruct((tile, width), LOW)] * count
        + [jax.ShapeDtypeStruct((1, width), jnp.float32)],
        cost_estimate=pl.CostEstimate(
            flops=2 * count * tile * columns * width, transcendentals=0, bytes_accessed=8 << 20
        ),
        name="projection_back",
    )(at, d_projected, weight_rows, gathered)


def norm_back(values, gain_vec, base, blocks):
    rows, width = values.shape
    part = 64
    count = len(blocks)

    def kernel(values_ref, gain_ref, base_ref, *refs):
        wide_ref, low_ref, sum_ref = refs[count:]
        step = pl.program_id(0)
        upstream = sum(ref[...].astype(jnp.float32) for ref in refs[:count])
        held = values_ref[...].astype(jnp.float32)
        row_scale = lax.rsqrt(jnp.mean(held * held, axis=-1, keepdims=True) + EPS)
        scaled = held * row_scale
        added = jnp.sum(upstream * scaled, axis=0, keepdims=True)
        sum_ref[...] = jnp.where(step == 0, added, sum_ref[...] + added)
        weighted = upstream * gain_ref[...].astype(jnp.float32)
        inner = jnp.mean(weighted * scaled, axis=-1, keepdims=True)
        result = base_ref[...].astype(jnp.float32) + row_scale * (weighted - scaled * inner)
        wide_ref[...] = result
        low_ref[...] = result.astype(LOW)

    tile_block = pl.BlockSpec((part, width), lambda i: (i, 0))
    line = pl.BlockSpec((1, width), lambda i: (0, 0))
    return pl.pallas_call(
        kernel,
        grid=(rows // part,),
        in_specs=[tile_block, line, tile_block] + [tile_block] * count,
        out_specs=[tile_block, tile_block, line],
        out_shape=[
            jax.ShapeDtypeStruct((rows, width), jnp.float32),
            jax.ShapeDtypeStruct((rows, width), LOW),
            jax.ShapeDtypeStruct((1, width), jnp.float32),
        ],
        cost_estimate=pl.CostEstimate(
            flops=16 * rows * width, transcendentals=rows, bytes_accessed=10 << 20
        ),
        name="norm_back",
    )(values, gain_vec.reshape(1, -1), base, *blocks)


def exchange(make_blocks, axis):
    n = lax.axis_size(axis)
    me = lax.axis_index(axis)
    places = [(me + hop) % n for hop in range(1, n)] + [me]
    made = list(make_blocks(places[:1]))
    moved = []
    for hop in range(1, n):
        if hop == 2:
            made += make_blocks(places[1:])
        pairs = [(i, (i + hop) % n) for i in range(n)]
        moved.append(lax.ppermute(made[hop - 1], axis, pairs))
    return moved + made[n - 1 :]


def place_blocks(halves, axis):
    (first, first_offsets), (second, second_offsets) = halves
    parts, rows, half = first.shape

    def kernel(at_ref, first_ref, second_ref, out_ref):
        out_ref[:, :half] = first_ref[0].astype(jnp.float32)
        out_ref[:, half:] = second_ref[0].astype(jnp.float32)

    def entry(offsets):
        where = [offsets.index(k) for k in range(parts)]

        def index(k, at_ref):
            found = where[0]
            for candidate in range(1, parts):
                found = jnp.where(k == candidate, where[candidate], found)
            return (found, 0, 0)

        return pl.BlockSpec((1, rows, half), index)

    return pl.pallas_call(
        kernel,
        grid_spec=pltpu.PrefetchScalarGridSpec(
            num_scalar_prefetch=1,
            grid=(parts,),
            in_specs=[entry(first_offsets), entry(second_offsets)],
            out_specs=pl.BlockSpec((rows, 2 * half), lambda k, at_ref: (at_ref[0] ^ k, 0)),
        ),
        out_shape=jax.ShapeDtypeStruct((parts * rows, 2 * half), jnp.float32),
        cost_estimate=pl.CostEstimate(
            flops=0, transcendentals=0, bytes_accessed=12 * parts * rows * half
        ),
        name="place_blocks",
    )(lax.axis_index(axis).reshape(1), first, second)


def unpack_attention(shared, q_columns, k_columns, folds):
    rows, columns = shared.shape
    block = rows // folds
    kv_heads = k_columns // HD
    wide = q_columns // kv_heads
    packed = wide + 2 * HD
    end = kv_heads * packed

    def kernel(shared_ref, query_ref, key_ref, value_ref, output_ref):
        for j in range(kv_heads):
            start = j * packed
            query_ref[:, j * wide : (j + 1) * wide] = shared_ref[
                :, start : start + wide
            ].astype(jnp.float32)
            for at, ref in ((start + wide, key_ref), (start + wide + HD, value_ref)):
                ref[:, j * HD : (j + 1) * HD] = shared_ref[:, at : at + HD].astype(jnp.float32)
        output_ref[...] = shared_ref[:, end:].astype(jnp.float32)

    narrow = pl.BlockSpec((block, k_columns), lambda p: (p, 0))
    return pl.pallas_call(
        kernel,
        grid=(folds,),
        in_specs=[pl.BlockSpec((block, columns), lambda p: (p, 0))],
        out_specs=[
            pl.BlockSpec((block, q_columns), lambda p: (p, 0)),
            narrow,
            narrow,
            pl.BlockSpec((block, columns - end), lambda p: (0, p)),
        ],
        out_shape=[
            jax.ShapeDtypeStruct((rows, q_columns), jnp.float32),
            jax.ShapeDtypeStruct((rows, k_columns), jnp.float32),
            jax.ShapeDtypeStruct((rows, k_columns), jnp.float32),
            jax.ShapeDtypeStruct((block, (columns - end) * folds), jnp.float32),
        ],
        cost_estimate=pl.CostEstimate(
            flops=0, transcendentals=0, bytes_accessed=6 * rows * columns
        ),
        name="unpack_attention",
    )(shared)


def add_all(blocks):
    return sum(block.astype(jnp.float32) for block in blocks)


def row_major(array):
    return with_layout_constraint(array, Layout(major_to_minor=tuple(range(array.ndim))))


def split_columns(array, parts):
    if parts == 1:
        return array
    rows, columns = array.shape[0], array.shape[1] // parts
    return array.reshape(rows, parts, columns).swapaxes(0, 1).reshape(parts * rows, columns)


def join_columns(array, parts):
    if parts == 1:
        return array
    rows, columns = array.shape[0] // parts, array.shape[1]
    return array.reshape(parts, rows, columns).swapaxes(0, 1).reshape(rows, parts * columns)


def block(
    tokens,
    cotangent,
    norm1_gain,
    w_query,
    w_key,
    w_value,
    w_output,
    norm2_gain,
    w_gate,
    w_up,
    w_down,
):
    n_dp = lax.axis_size(DP)
    own_rows, width = tokens.shape
    depth = w_output.shape[0] // n_dp
    q_columns, k_columns = w_query.shape[1], w_key.shape[1]
    kv_heads = k_columns // HD
    group = q_columns // k_columns
    ff_columns = w_gate.shape[1]
    ff_folds = width // w_down.shape[0]
    folds = width // w_output.shape[0]
    nothing = scatter_sum(tokens[:, :128] * 0, DP)[0, 0]
    gathered = lax.all_gather(tokens, TP, axis=0)
    own_part = lax.dynamic_slice_in_dim(w_output, lax.axis_index(DP) * depth, depth, 0)
    output_part = lax.all_gather(own_part, TP, axis=0)
    all_output = cube_gather(output_part, DP)
    cos_table, sin_table = rope_tables(SEQLEN, HD)
    cos_rows, sin_rows = cos_table.T, sin_table.T
    pieces = []
    for j in range(kv_heads):
        pieces.append(w_query[:, j * group * HD : (j + 1) * group * HD].T)
        pieces.append(w_key[:, j * HD : (j + 1) * HD].T)
        pieces.append(w_value[:, j * HD : (j + 1) * HD].T)
    weight_rows = jnp.concatenate(pieces, axis=0)
    normed1, projected = norm_project(
        gathered, norm1_gain, weight_rows, cos_rows, sin_rows, group
    )
    heads_out, heads_rows, totals = attend(projected, group)
    all_heads = lax.all_gather(heads_out, TP, axis=0)
    all_cot = gather_rows(cotangent, TP)
    hidden_state, normed2 = project_and_norm(
        all_heads, all_output, gathered, norm2_gain.astype(jnp.float32) + nothing.astype(jnp.float32)
    )
    gate_proj, up_proj, activated = gated_up(normed2, w_gate, w_up)
    mlp_part = jnp.dot(activated, w_down, preferred_element_type=jnp.float32).astype(LOW)
    half_width = width // 2

    def part_of(columns):
        return lambda places: [
            lax.dynamic_slice(mlp_part, (place * own_rows, columns), (own_rows, half_width))
            for place in places
        ]

    first_half = exchange(part_of(0), TP)
    second_half = exchange(part_of(half_width), TP)
    output = (
        hidden_state
        + jnp.concatenate([add_all(first_half), add_all(second_half)], axis=1)
    ).astype(LOW)
    d_gate, d_up = gated_back(all_cot, w_down, gate_proj, up_proj)
    grad_down = row_major(split_columns(contract_rows(activated, all_cot).astype(LOW), ff_folds))
    part_down = scatter_sum(grad_down, DP)
    dn2_blocks = exchange(
        lambda places: pair_product(places, own_rows, d_gate, w_gate, d_up, w_up), TP
    )
    gate_up_grads = row_major(
        jnp.concatenate(
            [contract_rows(normed2, d_gate).astype(LOW), contract_rows(normed2, d_up).astype(LOW)],
            axis=1,
        )
    )
    part_gate_up = scatter_sum(gate_up_grads, DP)
    d_state, state_low, gain_two = norm_back(hidden_state, norm2_gain, cotangent, dn2_blocks)
    d_state_low = gather_rows(state_low, TP)
    gain_two_sum = cube_sum(gain_two[0], (DP, TP))
    d_heads_rows = contract_cols(w_output, d_state_low).astype(LOW)
    d_projected = attend_back(projected, d_heads_rows, totals, cos_rows, sin_rows)
    gains = []

    def dn1_blocks_of(places):
        *made, gain = projection_back(places, d_projected, weight_rows, gathered)
        gains.append(gain)
        return made

    dn1_blocks = exchange(dn1_blocks_of, TP)
    gain_one_sum = cube_sum(sum(gains)[0], (DP, TP))
    grad_qkv = lax.dot_general(
        normed1,
        d_projected,
        (((0,), (1,)), ((), ())),
        preferred_element_type=jnp.float32,
    ).astype(LOW)
    grad_output = jnp.dot(heads_rows, d_state_low, preferred_element_type=jnp.float32).astype(LOW)
    low_attn = row_major(
        jnp.concatenate([grad_qkv, split_columns(grad_output, folds)], axis=1)
    )
    part_attn = scatter_sum(low_attn, DP)
    down_halves = cube_gather(part_down, DP)
    full_down = join_columns(place_blocks(down_halves, DP), ff_folds)
    shared_ff = row_major(gather_rows(part_gate_up, DP))
    shared_attn = row_major(gather_rows(part_attn, DP))
    _, input_grad, _ = norm_back(tokens, norm1_gain, d_state, dn1_blocks)
    full_gate = shared_ff[:, :ff_columns].astype(jnp.float32)
    full_up = shared_ff[:, ff_columns:].astype(jnp.float32)
    full_query, full_key, full_value, full_output = unpack_attention(
        shared_attn, q_columns, k_columns, folds
    )
    return (
        output,
        input_grad,
        gain_one_sum,
        full_query,
        full_key,
        full_value,
        full_output,
        gain_two_sum,
        full_gate,
        full_up,
        full_down,
    )


ROWS, COLUMNS, HIDDEN = P((DP, TP), None), P(None, TP), P(TP, None)


def solution(mesh):
    return jax.shard_map(
        block,
        mesh=mesh,
        in_specs=(ROWS, ROWS, P(), COLUMNS, COLUMNS, COLUMNS, HIDDEN, P(), COLUMNS, COLUMNS, HIDDEN),
        out_specs=(ROWS, ROWS, P(), COLUMNS, COLUMNS, COLUMNS, HIDDEN, P(), COLUMNS, COLUMNS, HIDDEN),
        check_vma=False,
    )
```

```python
import functools

import jax
import jax.numpy as jnp
from jax import lax
from jax.experimental import pallas as pl
from jax.experimental.pallas import tpu as pltpu
from jax.experimental.layout import Layout, with_layout_constraint
from jax.sharding import PartitionSpec as P


LOW = jnp.bfloat16
DP, TP = "dp", "tensor"

HD = 64
SEQLEN = 512


EPS = 1e-05
ROPE_BASE = 500000.0
MASKED = -1e30


def rope_tables(length, columns):
    half_width = columns // 2
    frequency = ROPE_BASE ** (-(jnp.arange(half_width, dtype=jnp.float32) * 2.0 / columns))
    angles = jnp.arange(length, dtype=jnp.float32)[:, None] * frequency[None, :]
    return (jnp.cos(angles), jnp.sin(angles))


def contract_cols(left_side, right_side):
    return lax.dot_general(
        left_side, right_side, (((1,), (1,)), ((), ())), preferred_element_type=jnp.float32
    )


def gather_rows(block, axis):
    return lax.all_gather(block, axis, axis=0, tiled=True)


def scatter_sum(partial, axis):
    return lax.psum_scatter(partial, axis, scatter_dimension=0, tiled=True)


def cube_gather(blocks, axis, join=True):
    n = lax.axis_size(axis)
    bits = [1 << b for b in range(n.bit_length() - 1)]
    half = blocks.shape[-1] // 2
    halves = []
    for part, order in (
        (blocks[..., :half], bits[1:] + bits[:1]),
        (blocks[..., half:], bits[:0:-1] + bits[:1]),
    ):
        held, offsets = part[None], [0]
        for bit in order:
            moved = lax.ppermute(held, axis, [(i, i ^ bit) for i in range(n)])
            offsets = offsets + [o ^ bit for o in offsets]
            if join or bit != order[-1]:
                held = jnp.concatenate([held, moved], axis=0)
        halves.append((held if join else (held, moved), tuple(offsets)))
    return halves


def cube_sum(vector, axes):
    for axis in axes:
        n = lax.axis_size(axis)
        bit = 1
        while bit < n:
            vector = vector + lax.ppermute(vector, axis, [(i, i ^ bit) for i in range(n)])
            bit *= 2
    return vector


def rotate_rows(values, cos_rows, sin_rows):
    half = HD // 2
    heads = []
    for h in range(values.shape[0] // HD):
        upper = values[h * HD : h * HD + half]
        lower = values[h * HD + half : (h + 1) * HD]
        heads.append(upper * cos_rows - lower * sin_rows)
        heads.append(lower * cos_rows + upper * sin_rows)
    return jnp.concatenate(heads, axis=0)


def dot_lanes(left_side, right_side):
    return lax.dot_general(
        left_side, right_side, (((1,), (1,)), ((), ())), preferred_element_type=jnp.float32
    )


def norm_project(gathered, gain_vec, weight_rows, cos_rows, sin_rows, group):
    blocks, tile, width = gathered.shape
    rows = blocks * tile
    columns = weight_rows.shape[0]
    packed = (group + 2) * HD

    def kernel(tokens_ref, gain_ref, weight_ref, cos_ref, sin_ref, normed_ref, out_ref):
        values = tokens_ref[0].astype(jnp.float32)
        row_scale = lax.rsqrt(jnp.mean(values * values, axis=-1, keepdims=True) + EPS)
        normed = (values * row_scale * gain_ref[...].astype(jnp.float32)).astype(LOW)
        normed_ref[...] = normed
        projected = dot_lanes(weight_ref[...], normed)
        for start in range(0, columns, packed):
            turned = start + packed - HD
            out_ref[start:turned] = rotate_rows(
                projected[start:turned], cos_ref[...], sin_ref[...]
            ).astype(LOW)
            out_ref[turned : turned + HD] = projected[turned : turned + HD].astype(LOW)

    half = HD // 2
    return pl.pallas_call(
        kernel,
        grid=(blocks,),
        in_specs=[
            pl.BlockSpec((1, tile, width), lambda i: (i, 0, 0)),
            pl.BlockSpec((1, width), lambda i: (0, 0)),
            pl.BlockSpec((columns, width), lambda i: (0, 0)),
            pl.BlockSpec((half, tile), lambda i: (0, i % (SEQLEN // tile))),
            pl.BlockSpec((half, tile), lambda i: (0, i % (SEQLEN // tile))),
        ],
        out_specs=[
            pl.BlockSpec((tile, width), lambda i: (i, 0)),
            pl.BlockSpec((columns, tile), lambda i: (0, i)),
        ],
        out_shape=[
            jax.ShapeDtypeStruct((rows, width), LOW),
            jax.ShapeDtypeStruct((columns, rows), LOW),
        ],
        cost_estimate=pl.CostEstimate(
            flops=2 * rows * width * columns, transcendentals=rows, bytes_accessed=12 << 20
        ),
        name="norm_project",
    )(gathered, gain_vec.reshape(1, -1), weight_rows, cos_rows, sin_rows)


def key_tiles(step, tile):
    return [(t * tile, t == step) for t in range(step + 1)]


def causal_tile(tile):
    key_at = lax.broadcasted_iota(jnp.int32, (tile, tile), 0)
    query_at = lax.broadcasted_iota(jnp.int32, (tile, tile), 1)
    return key_at <= query_at


def attend(projected, group):
    columns, rows = projected.shape
    packed = (group + 2) * HD
    kv_heads = columns // packed
    wide = group * HD
    tile = 256
    score_scale = HD ** (-0.5)

    def kernel(packed_ref, heads_ref, heads_t_ref, total_ref):
        keys = packed_ref[wide : wide + HD].astype(jnp.float32).T.astype(LOW)
        visible = causal_tile(tile)
        for step in range(SEQLEN // tile):
            here = slice(step * tile, (step + 1) * tile)
            for h in range(group):
                query = packed_ref[h * HD : (h + 1) * HD, here]
                parts = []
                for start, masked in key_tiles(step, tile):
                    part = jnp.dot(
                        keys[start : start + tile], query, preferred_element_type=jnp.float32
                    )
                    parts.append(jnp.where(visible, part, MASKED) if masked else part)
                top = functools.reduce(
                    jnp.maximum, [jnp.max(part, axis=0, keepdims=True) for part in parts]
                )
                parts = [jnp.exp((part - top) * score_scale) for part in parts]
                total = sum(jnp.sum(part, axis=0, keepdims=True) for part in parts)
                inverse = 1.0 / total
                mixed = sum(
                    jnp.dot(
                        packed_ref[wide + HD : packed, start : start + tile],
                        (part * inverse).astype(LOW),
                        preferred_element_type=jnp.float32,
                    )
                    for part, (start, _) in zip(parts, key_tiles(step, tile))
                )
                heads_t_ref[h * HD : (h + 1) * HD, here] = mixed.astype(LOW)
                total_ref[0, h : h + 1, here] = top * score_scale + jnp.log(total)
        heads_ref[...] = heads_t_ref[...].astype(jnp.float32).T.astype(LOW)

    return pl.pallas_call(
        kernel,
        grid=(rows // SEQLEN, kv_heads),
        in_specs=[pl.BlockSpec((packed, SEQLEN), lambda s, j: (j, s))],
        out_specs=[
            pl.BlockSpec((SEQLEN, wide), lambda s, j: (s, j)),
            pl.BlockSpec((wide, SEQLEN), lambda s, j: (j, s)),
            pl.BlockSpec((1, group, SEQLEN), lambda s, j: (j, 0, s)),
        ],
        out_shape=[
            jax.ShapeDtypeStruct((rows, kv_heads * wide), LOW),
            jax.ShapeDtypeStruct((kv_heads * wide, rows), LOW),
            jax.ShapeDtypeStruct((kv_heads, group, rows), jnp.float32),
        ],
        cost_estimate=pl.CostEstimate(
            flops=4 * rows * SEQLEN * kv_heads * wide,
            transcendentals=rows * SEQLEN * kv_heads * group,
            bytes_accessed=4 << 20,
        ),
        name="attend",
    )(projected)


def attend_back(projected, d_heads, totals, cos_rows, sin_rows):
    columns, rows = projected.shape
    kv_heads, group, _ = totals.shape
    packed = (group + 2) * HD
    wide = group * HD
    tile = 256
    score_scale = HD ** (-0.5)

    def kernel(
        packed_ref, d_heads_ref, total_ref, cos_ref, sin_ref, out_ref, key_sum, value_sum
    ):
        keys = packed_ref[wide : wide + HD].astype(jnp.float32).T.astype(LOW)
        values = packed_ref[wide + HD : packed].astype(jnp.float32).T.astype(LOW)
        visible = causal_tile(tile)
        key_sum[...] = jnp.zeros_like(key_sum)
        value_sum[...] = jnp.zeros_like(value_sum)
        for step in range(SEQLEN // tile):
            here = slice(step * tile, (step + 1) * tile)
            for h in range(group):
                query = packed_ref[h * HD : (h + 1) * HD, here]
                d_head = d_heads_ref[h * HD : (h + 1) * HD, here]
                log_total = total_ref[0, h : h + 1, here]
                probs, d_probs = [], []
                for start, masked in key_tiles(step, tile):
                    span = slice(start, start + tile)
                    part = jnp.dot(keys[span], query, preferred_element_type=jnp.float32)
                    part = jnp.exp(part * score_scale - log_total)
                    if masked:
                        part = jnp.where(visible, part, 0.0)
                    probs.append(part)
                    value_sum[:, span] += dot_lanes(d_head, part.astype(LOW))
                    d_probs.append(
                        jnp.dot(values[span], d_head, preferred_element_type=jnp.float32)
                    )
                row_sum = sum(
                    jnp.sum(part * d_part, axis=0, keepdims=True)
                    for part, d_part in zip(probs, d_probs)
                )
                d_query = jnp.zeros((HD, tile), jnp.float32)
                for (start, _), part, d_part in zip(key_tiles(step, tile), probs, d_probs):
                    span = slice(start, start + tile)
                    d_scores = (part * (d_part - row_sum)).astype(LOW)
                    d_query += jnp.dot(
                        packed_ref[wide : wide + HD, span],
                        d_scores,
                        preferred_element_type=jnp.float32,
                    )
                    key_sum[:, span] += dot_lanes(query, d_scores)
                out_ref[h * HD : (h + 1) * HD, here] = rotate_rows(
                    d_query * score_scale, cos_ref[:, here], -sin_ref[:, here]
                ).astype(LOW)
        out_ref[wide : wide + HD] = rotate_rows(
            key_sum[...] * score_scale, cos_ref[...], -sin_ref[...]
        ).astype(LOW)
        out_ref[wide + HD : packed] = value_sum[...].astype(LOW)

    half = HD // 2
    return pl.pallas_call(
        kernel,
        grid=(rows // SEQLEN, kv_heads),
        in_specs=[
            pl.BlockSpec((packed, SEQLEN), lambda s, j: (j, s)),
            pl.BlockSpec((wide, SEQLEN), lambda s, j: (j, s)),
            pl.BlockSpec((1, group, SEQLEN), lambda s, j: (j, 0, s)),
            pl.BlockSpec((half, SEQLEN), lambda s, j: (0, 0)),
            pl.BlockSpec((half, SEQLEN), lambda s, j: (0, 0)),
        ],
        out_specs=pl.BlockSpec((packed, SEQLEN), lambda s, j: (j, s)),
        out_shape=jax.ShapeDtypeStruct((columns, rows), LOW),
        scratch_shapes=[
            pltpu.VMEM((HD, SEQLEN), jnp.float32),
            pltpu.VMEM((HD, SEQLEN), jnp.float32),
        ],
        cost_estimate=pl.CostEstimate(
            flops=10 * rows * SEQLEN * kv_heads * wide,
            transcendentals=rows * SEQLEN * kv_heads * group,
            bytes_accessed=6 << 20,
        ),
        name="attend_back",
    )(projected, d_heads, totals, cos_rows, sin_rows)


def project_and_norm(all_heads, weights, gathered, gain_vec):
    groups, rows, group_columns = all_heads.shape
    (first, first_offsets), (second, second_offsets) = weights
    parts, _, depth, half = first.shape
    width = 2 * half
    tile = rows // groups
    places = jnp.stack([lax.axis_index(TP), lax.axis_index(DP)])

    def kernel(
        at_ref,
        heads_ref,
        first_ref,
        second_ref,
        tokens_ref,
        gain_ref,
        hidden_ref,
        normed_ref,
        turned_ref,
        weight_ref,
        wide_ref,
    ):
        step = pl.program_id(0)

        @pl.when(step == 0)
        def _():
            for side, part_ref, offsets in (
                (0, first_ref, first_offsets),
                (half, second_ref, second_offsets),
            ):
                for part in range(parts):
                    for g in range(groups):
                        start = g * group_columns + (at_ref[1] ^ offsets[part]) * depth
                        at = pl.ds(pl.multiple_of(start, depth), depth)
                        weight_ref[at, side : side + half] = part_ref[part, g]

        for g in range(groups):
            wide_ref[:, g * group_columns : (g + 1) * group_columns] = heads_ref[g]
        hidden = tokens_ref[0].astype(jnp.float32) + jnp.dot(
            wide_ref[...], weight_ref[...], preferred_element_type=jnp.float32
        )
        row_scale = lax.rsqrt(jnp.mean(hidden * hidden, axis=-1, keepdims=True) + EPS)
        normed = hidden * row_scale * gain_ref[...].astype(jnp.float32)
        normed_ref[...] = normed.astype(LOW)
        turned_ref[...] = normed.T.astype(LOW)

        @pl.when(step == at_ref[0])
        def _():
            hidden_ref[...] = hidden

    return pl.pallas_call(
        kernel,
        grid_spec=pltpu.PrefetchScalarGridSpec(
            num_scalar_prefetch=1,
            grid=(groups,),
            in_specs=[
                pl.BlockSpec((groups, tile, group_columns), lambda i, at_ref: (0, i, 0)),
                pl.BlockSpec(first.shape, lambda i, at_ref: (0, 0, 0, 0)),
                pl.BlockSpec(second.shape, lambda i, at_ref: (0, 0, 0, 0)),
                pl.BlockSpec((1, tile, width), lambda i, at_ref: (i, 0, 0)),
                pl.BlockSpec((1, width), lambda i, at_ref: (0, 0)),
            ],
            out_specs=[
                pl.BlockSpec((tile, width), lambda i, at_ref: (0, 0)),
                pl.BlockSpec((tile, width), lambda i, at_ref: (i, 0)),
                pl.BlockSpec((width, tile), lambda i, at_ref: (0, i)),
            ],
            scratch_shapes=[
                pltpu.VMEM((groups * group_columns, width), LOW),
                pltpu.VMEM((tile, groups * group_columns), LOW),
            ],
        ),
        out_shape=[
            jax.ShapeDtypeStruct((tile, width), jnp.float32),
            jax.ShapeDtypeStruct((rows, width), LOW),
            jax.ShapeDtypeStruct((width, rows), LOW),
        ],
        cost_estimate=pl.CostEstimate(
            flops=2 * rows * width * width, transcendentals=rows, bytes_accessed=24 << 20
        ),
        name="project_and_norm",
    )(places, all_heads, first, second, gathered, gain_vec.reshape(1, -1))


def gated_up(normed, w_gate, w_up):
    rows, width = normed.shape
    columns = w_gate.shape[1]
    tile = 256

    def kernel(normed_ref, gate_w_ref, up_w_ref, active_ref, turned_ref, smooth_ref, slope_ref):
        gate = jnp.dot(normed_ref[...], gate_w_ref[...], preferred_element_type=jnp.float32)
        up = jnp.dot(normed_ref[...], up_w_ref[...], preferred_element_type=jnp.float32)
        chance = jax.nn.sigmoid(gate)
        smooth = gate * chance
        active = smooth * up
        active_ref[...] = active.astype(LOW)
        turned_ref[...] = active.T.astype(LOW)
        smooth_ref[...] = smooth.astype(LOW)
        slope_ref[...] = (up * (chance * (1.0 + gate * (1.0 - chance)))).astype(LOW)

    column_block = pl.BlockSpec((rows, tile), lambda j: (0, j))
    weight_block = pl.BlockSpec((width, tile), lambda j: (0, j))
    flat = jax.ShapeDtypeStruct((rows, columns), LOW)
    return pl.pallas_call(
        kernel,
        grid=(columns // tile,),
        in_specs=[pl.BlockSpec((rows, width), lambda j: (0, 0)), weight_block, weight_block],
        out_specs=[
            column_block,
            pl.BlockSpec((tile, rows), lambda j: (j, 0)),
            column_block,
            column_block,
        ],
        out_shape=[flat, jax.ShapeDtypeStruct((columns, rows), LOW), flat, flat],
        cost_estimate=pl.CostEstimate(
            flops=4 * rows * width * columns,
            transcendentals=rows * columns,
            bytes_accessed=36 << 20,
        ),
        name="gated_up",
    )(normed, w_gate, w_up)


def gated_back(all_cot, w_down, smooth, slope):
    rows, width = all_cot.shape
    columns = w_down.shape[0]
    tile = 256

    def kernel(cot_ref, weight_ref, smooth_ref, slope_ref, d_gate_ref, d_up_ref):
        d_active = dot_lanes(cot_ref[...], weight_ref[...])
        d_up_ref[...] = (d_active * smooth_ref[...].astype(jnp.float32)).astype(LOW)
        d_gate_ref[...] = (d_active * slope_ref[...].astype(jnp.float32)).astype(LOW)

    column_block = pl.BlockSpec((rows, tile), lambda j: (0, j))
    return pl.pallas_call(
        kernel,
        grid=(columns // tile,),
        in_specs=[
            pl.BlockSpec((rows, width), lambda j: (0, 0)),
            pl.BlockSpec((tile, width), lambda j: (j, 0)),
            column_block,
            column_block,
        ],
        out_specs=[column_block] * 2,
        out_shape=[jax.ShapeDtypeStruct((rows, columns), LOW)] * 2,
        cost_estimate=pl.CostEstimate(
            flops=2 * rows * width * columns, transcendentals=0, bytes_accessed=28 << 20
        ),
        name="gated_back",
    )(all_cot, w_down, smooth, slope)


def product(left, rights, folds):
    rows, depth = left.shape
    each = rights[0].shape[1]
    tile = 512
    row_steps, column_steps = rows // tile, each // tile
    count = len(rights)
    per = count * column_steps // folds

    def kernel(left_ref, *refs):
        out_ref = refs[count]
        for k in range(count):

            def _(k=k):
                out_ref[...] = jnp.dot(
                    left_ref[...], refs[k][...], preferred_element_type=jnp.float32
                ).astype(LOW)

            if count == 1:
                _()
            else:
                pl.when(pl.program_id(1) // column_steps == k)(_)

    def right_block(k):
        return pl.BlockSpec(
            (depth, tile), lambda i, j: (0, jnp.clip(j - k * column_steps, 0, column_steps - 1))
        )

    return pl.pallas_call(
        kernel,
        grid=(row_steps, count * column_steps),
        in_specs=[pl.BlockSpec((tile, depth), lambda i, j: (i, 0))]
        + [right_block(k) for k in range(count)],
        out_specs=pl.BlockSpec(
            (tile, tile), lambda i, j: (i + (j // per) * row_steps, j % per)
        ),
        out_shape=jax.ShapeDtypeStruct((rows * folds, count * each // folds), LOW),
        cost_estimate=pl.CostEstimate(
            flops=2 * rows * depth * count * each,
            transcendentals=0,
            bytes_accessed=2 * (rows * depth + (depth + rows) * count * each),
        ),
        name="product",
    )(left, *rights)


def pair_product(places, tile, first, first_weight, second, second_weight):
    rows, depth = first.shape
    columns = first_weight.shape[0]
    count = len(places)
    part = 512 if count == 1 else 256
    at = jnp.stack(places)

    def kernel(at_ref, first_ref, second_ref, first_w_ref, second_w_ref, *out_refs):
        for k, out_ref in enumerate(out_refs):
            here = (
                slice(None)
                if count == 1
                else pl.ds(pl.multiple_of(at_ref[k] * tile, tile), tile)
            )
            out_ref[...] = (
                dot_lanes(first_ref[here, :], first_w_ref[...])
                + dot_lanes(second_ref[here, :], second_w_ref[...])
            ).astype(LOW)

    held = (
        pl.BlockSpec((tile, depth), lambda j, at_ref: (at_ref[0], 0))
        if count == 1
        else pl.BlockSpec((rows, depth), lambda j, at_ref: (0, 0))
    )
    weight_block = pl.BlockSpec((part, depth), lambda j, at_ref: (j, 0))
    return pl.pallas_call(
        kernel,
        grid_spec=pltpu.PrefetchScalarGridSpec(
            num_scalar_prefetch=1,
            grid=(columns // part,),
            in_specs=[held, held, weight_block, weight_block],
            out_specs=[pl.BlockSpec((tile, part), lambda j, at_ref: (0, j))] * count,
        ),
        out_shape=[jax.ShapeDtypeStruct((tile, columns), LOW)] * count,
        cost_estimate=pl.CostEstimate(
            flops=4 * count * tile * depth * columns, transcendentals=0, bytes_accessed=20 << 20
        ),
        name="pair_product",
    )(at, first, second, first_weight, second_weight)


def projection_back(places, d_projected, weight_rows, gathered):
    columns, width = weight_rows.shape
    tile = gathered.shape[1]
    count = len(places)
    at = jnp.stack(places)

    def kernel(at_ref, d_ref, weight_ref, tokens_ref, *out_refs):
        step = pl.program_id(0)
        grads = d_ref[...].astype(jnp.float32).T.astype(LOW)
        made = jnp.dot(grads, weight_ref[...], preferred_element_type=jnp.float32).astype(LOW)
        values = tokens_ref[0].astype(jnp.float32)
        row_scale = lax.rsqrt(jnp.mean(values * values, axis=-1, keepdims=True) + EPS)
        added = jnp.sum(made.astype(jnp.float32) * values * row_scale, axis=0, keepdims=True)
        gain_ref = out_refs[count]
        gain_ref[...] = jnp.where(step == 0, added, gain_ref[...] + added)
        for k in range(count):

            @pl.when(step == k)
            def _():
                out_refs[k][...] = made

    return pl.pallas_call(
        kernel,
        grid_spec=pltpu.PrefetchScalarGridSpec(
            num_scalar_prefetch=1,
            grid=(count,),
            in_specs=[
                pl.BlockSpec((columns, tile), lambda i, at_ref: (0, at_ref[i])),
                pl.BlockSpec((columns, width), lambda i, at_ref: (0, 0)),
                pl.BlockSpec((1, tile, width), lambda i, at_ref: (at_ref[i], 0, 0)),
            ],
            out_specs=[pl.BlockSpec((tile, width), lambda i, at_ref: (0, 0))] * count
            + [pl.BlockSpec((1, width), lambda i, at_ref: (0, 0))],
        ),
        out_shape=[jax.ShapeDtypeStruct((tile, width), LOW)] * count
        + [jax.ShapeDtypeStruct((1, width), jnp.float32)],
        cost_estimate=pl.CostEstimate(
            flops=2 * count * tile * columns * width, transcendentals=0, bytes_accessed=8 << 20
        ),
        name="projection_back",
    )(at, d_projected, weight_rows, gathered)


def norm_back(values, gain_vec, base, blocks):
    rows, width = values.shape
    part = 64
    count = len(blocks)

    def kernel(values_ref, gain_ref, base_ref, *refs):
        wide_ref, low_ref, sum_ref = refs[count:]
        step = pl.program_id(0)
        upstream = sum(ref[...].astype(jnp.float32) for ref in refs[:count])
        held = values_ref[...].astype(jnp.float32)
        row_scale = lax.rsqrt(jnp.mean(held * held, axis=-1, keepdims=True) + EPS)
        scaled = held * row_scale
        added = jnp.sum(upstream * scaled, axis=0, keepdims=True)
        sum_ref[...] = jnp.where(step == 0, added, sum_ref[...] + added)
        weighted = upstream * gain_ref[...].astype(jnp.float32)
        inner = jnp.mean(weighted * scaled, axis=-1, keepdims=True)
        result = base_ref[...].astype(jnp.float32) + row_scale * (weighted - scaled * inner)
        wide_ref[...] = result
        low_ref[...] = result.astype(LOW)

    tile_block = pl.BlockSpec((part, width), lambda i: (i, 0))
    line = pl.BlockSpec((1, width), lambda i: (0, 0))
    return pl.pallas_call(
        kernel,
        grid=(rows // part,),
        in_specs=[tile_block, line, tile_block] + [tile_block] * count,
        out_specs=[tile_block, tile_block, line],
        out_shape=[
            jax.ShapeDtypeStruct((rows, width), jnp.float32),
            jax.ShapeDtypeStruct((rows, width), LOW),
            jax.ShapeDtypeStruct((1, width), jnp.float32),
        ],
        cost_estimate=pl.CostEstimate(
            flops=16 * rows * width, transcendentals=rows, bytes_accessed=10 << 20
        ),
        name="norm_back",
    )(values, gain_vec.reshape(1, -1), base, *blocks)


def exchange(make_blocks, axis):
    n = lax.axis_size(axis)
    me = lax.axis_index(axis)
    places = [(me + hop) % n for hop in range(1, n)] + [me]
    made = list(make_blocks(places[:1]))
    moved = []
    for hop in range(1, n):
        if hop == 2:
            made += make_blocks(places[1:])
        pairs = [(i, (i + hop) % n) for i in range(n)]
        moved.append(lax.ppermute(made[hop - 1], axis, pairs))
    return moved + made[n - 1 :]


def place_blocks(halves, axis):
    (first, first_offsets), (second, second_offsets) = halves
    some, rows, half = first[0].shape
    parts = 2 * some

    def kernel(at_ref, *refs):
        out_ref = refs[4]
        k = pl.program_id(0)
        for side, offsets in enumerate((first_offsets, second_offsets)):
            columns = slice(side * half, (side + 1) * half)
            late = functools.reduce(
                jnp.logical_or, [k == offset for offset in offsets[some:]]
            )
            early_ref, late_ref = refs[2 * side : 2 * side + 2]
            out_ref[:, columns] = jnp.where(late, late_ref[0], early_ref[0]).astype(jnp.float32)

    def entry(offsets):
        def index(k, at_ref):
            found = 0
            for at, offset in enumerate(offsets):
                found = jnp.where(k == offset, at, found)
            return (found, 0, 0)

        return pl.BlockSpec((1, rows, half), index)

    specs = []
    for offsets in (first_offsets, second_offsets):
        specs += [entry(offsets[:some]), entry(offsets[some:])]
    return pl.pallas_call(
        kernel,
        grid_spec=pltpu.PrefetchScalarGridSpec(
            num_scalar_prefetch=1,
            grid=(parts,),
            in_specs=specs,
            out_specs=pl.BlockSpec((rows, 2 * half), lambda k, at_ref: (at_ref[0] ^ k, 0)),
        ),
        out_shape=jax.ShapeDtypeStruct((parts * rows, 2 * half), jnp.float32),
        cost_estimate=pl.CostEstimate(
            flops=0, transcendentals=0, bytes_accessed=12 * parts * rows * half
        ),
        name="place_blocks",
    )(lax.axis_index(axis).reshape(1), *first, *second)


def unpack_attention(shared, q_columns, k_columns, folds):
    rows, columns = shared.shape
    block = rows // folds
    kv_heads = k_columns // HD
    wide = q_columns // kv_heads
    packed = wide + 2 * HD
    end = kv_heads * packed

    def kernel(shared_ref, query_ref, key_ref, value_ref, output_ref):
        for j in range(kv_heads):
            start = j * packed
            query_ref[:, j * wide : (j + 1) * wide] = shared_ref[
                :, start : start + wide
            ].astype(jnp.float32)
            for at, ref in ((start + wide, key_ref), (start + wide + HD, value_ref)):
                ref[:, j * HD : (j + 1) * HD] = shared_ref[:, at : at + HD].astype(jnp.float32)
        output_ref[...] = shared_ref[:, end:].astype(jnp.float32)

    narrow = pl.BlockSpec((block, k_columns), lambda p: (p, 0))
    return pl.pallas_call(
        kernel,
        grid=(folds,),
        in_specs=[pl.BlockSpec((block, columns), lambda p: (p, 0))],
        out_specs=[
            pl.BlockSpec((block, q_columns), lambda p: (p, 0)),
            narrow,
            narrow,
            pl.BlockSpec((block, columns - end), lambda p: (0, p)),
        ],
        out_shape=[
            jax.ShapeDtypeStruct((rows, q_columns), jnp.float32),
            jax.ShapeDtypeStruct((rows, k_columns), jnp.float32),
            jax.ShapeDtypeStruct((rows, k_columns), jnp.float32),
            jax.ShapeDtypeStruct((block, (columns - end) * folds), jnp.float32),
        ],
        cost_estimate=pl.CostEstimate(
            flops=0, transcendentals=0, bytes_accessed=6 * rows * columns
        ),
        name="unpack_attention",
    )(shared)


def add_all(blocks):
    return sum(block.astype(jnp.float32) for block in blocks)


def row_major(array):
    return with_layout_constraint(array, Layout(major_to_minor=tuple(range(array.ndim))))


def split_columns(array, parts):
    if parts == 1:
        return array
    rows, columns = array.shape[0], array.shape[1] // parts
    return array.reshape(rows, parts, columns).swapaxes(0, 1).reshape(parts * rows, columns)


def join_columns(array, parts):
    if parts == 1:
        return array
    rows, columns = array.shape[0] // parts, array.shape[1]
    return array.reshape(parts, rows, columns).swapaxes(0, 1).reshape(rows, parts * columns)


def block(
    tokens,
    cotangent,
    norm1_gain,
    w_query,
    w_key,
    w_value,
    w_output,
    norm2_gain,
    w_gate,
    w_up,
    w_down,
):
    n_dp = lax.axis_size(DP)
    own_rows, width = tokens.shape
    depth = w_output.shape[0] // n_dp
    q_columns, k_columns = w_query.shape[1], w_key.shape[1]
    kv_heads = k_columns // HD
    group = q_columns // k_columns
    ff_columns = w_gate.shape[1]
    ff_folds = width // w_down.shape[0]
    folds = width // w_output.shape[0]
    nothing = scatter_sum(tokens[:, :128] * 0, DP)[0, 0]
    gathered = lax.all_gather(tokens, TP, axis=0)
    own_part = lax.dynamic_slice_in_dim(w_output, lax.axis_index(DP) * depth, depth, 0)
    output_part = lax.all_gather(own_part, TP, axis=0)
    all_output = cube_gather(output_part, DP)
    cos_table, sin_table = rope_tables(SEQLEN, HD)
    cos_rows, sin_rows = cos_table.T, sin_table.T
    pieces = []
    for j in range(kv_heads):
        pieces.append(w_query[:, j * group * HD : (j + 1) * group * HD].T)
        pieces.append(w_key[:, j * HD : (j + 1) * HD].T)
        pieces.append(w_value[:, j * HD : (j + 1) * HD].T)
    weight_rows = jnp.concatenate(pieces, axis=0)
    normed1, projected = norm_project(
        gathered, norm1_gain, weight_rows, cos_rows, sin_rows, group
    )
    heads_out, heads_rows, totals = attend(projected, group)
    all_heads = lax.all_gather(heads_out, TP, axis=0)
    all_cot = gather_rows(cotangent, TP)
    hidden_state, normed2, normed2_rows = project_and_norm(
        all_heads, all_output, gathered, norm2_gain.astype(jnp.float32) + nothing.astype(jnp.float32)
    )
    activated, active_rows, smooth, slope = gated_up(normed2, w_gate, w_up)
    mlp_part = product(activated, [w_down], 1)
    half_width = width // 2

    def part_of(columns):
        return lambda places: [
            lax.dynamic_slice(mlp_part, (place * own_rows, columns), (own_rows, half_width))
            for place in places
        ]

    first_half = exchange(part_of(0), TP)
    second_half = exchange(part_of(half_width), TP)
    output = (
        hidden_state
        + jnp.concatenate([add_all(first_half), add_all(second_half)], axis=1)
    ).astype(LOW)
    d_gate, d_up = gated_back(all_cot, w_down, smooth, slope)
    grad_down = product(active_rows, [all_cot], ff_folds)
    part_down = scatter_sum(grad_down, DP)
    dn2_blocks = exchange(
        lambda places: pair_product(places, own_rows, d_gate, w_gate, d_up, w_up), TP
    )
    gate_up_grads = product(normed2_rows, [d_gate, d_up], 1)
    part_gate_up = scatter_sum(gate_up_grads, DP)
    d_state, state_low, gain_two = norm_back(hidden_state, norm2_gain, cotangent, dn2_blocks)
    d_state_low = gather_rows(state_low, TP)
    gain_two_sum = cube_sum(gain_two[0], (DP, TP))
    d_heads_rows = contract_cols(w_output, d_state_low).astype(LOW)
    d_projected = attend_back(projected, d_heads_rows, totals, cos_rows, sin_rows)
    gains = []

    def dn1_blocks_of(places):
        *made, gain = projection_back(places, d_projected, weight_rows, gathered)
        gains.append(gain)
        return made

    dn1_blocks = exchange(dn1_blocks_of, TP)
    gain_one_sum = cube_sum(sum(gains)[0], (DP, TP))
    grad_qkv = lax.dot_general(
        normed1,
        d_projected,
        (((0,), (1,)), ((), ())),
        preferred_element_type=jnp.float32,
    ).astype(LOW)
    grad_output = jnp.dot(heads_rows, d_state_low, preferred_element_type=jnp.float32).astype(LOW)
    low_attn = row_major(
        jnp.concatenate([grad_qkv, split_columns(grad_output, folds)], axis=1)
    )
    part_attn = scatter_sum(low_attn, DP)
    down_halves = cube_gather(part_down, DP, join=False)
    full_down = join_columns(place_blocks(down_halves, DP), ff_folds)
    shared_ff = row_major(gather_rows(part_gate_up, DP))
    shared_attn = row_major(gather_rows(part_attn, DP))
    _, input_grad, _ = norm_back(tokens, norm1_gain, d_state, dn1_blocks)
    full_gate = shared_ff[:, :ff_columns].astype(jnp.float32)
    full_up = shared_ff[:, ff_columns:].astype(jnp.float32)
    full_query, full_key, full_value, full_output = unpack_attention(
        shared_attn, q_columns, k_columns, folds
    )
    return (
        output,
        input_grad,
        gain_one_sum,
        full_query,
        full_key,
        full_value,
        full_output,
        gain_two_sum,
        full_gate,
        full_up,
        full_down,
    )


ROWS, COLUMNS, HIDDEN = P((DP, TP), None), P(None, TP), P(TP, None)


def solution(mesh):
    return jax.shard_map(
        block,
        mesh=mesh,
        in_specs=(ROWS, ROWS, P(), COLUMNS, COLUMNS, COLUMNS, HIDDEN, P(), COLUMNS, COLUMNS, HIDDEN),
        out_specs=(ROWS, ROWS, P(), COLUMNS, COLUMNS, COLUMNS, HIDDEN, P(), COLUMNS, COLUMNS, HIDDEN),
        check_vma=False,
    )
```

```python
import functools

import jax
import jax.numpy as jnp
from jax import lax
from jax.experimental import pallas as pl
from jax.experimental.pallas import tpu as pltpu
from jax.experimental.layout import Layout, with_layout_constraint
from jax.sharding import PartitionSpec as P


LOW = jnp.bfloat16
DP, TP = "dp", "tensor"

HD = 64
SEQLEN = 512


EPS = 1e-05
ROPE_BASE = 500000.0
MASKED = -1e30


def rope_tables(length, columns):
    half_width = columns // 2
    frequency = ROPE_BASE ** (-(jnp.arange(half_width, dtype=jnp.float32) * 2.0 / columns))
    angles = jnp.arange(length, dtype=jnp.float32)[:, None] * frequency[None, :]
    return (jnp.cos(angles), jnp.sin(angles))


def contract_cols(left_side, right_side):
    return lax.dot_general(
        left_side, right_side, (((1,), (1,)), ((), ())), preferred_element_type=jnp.float32
    )


def gather_rows(block, axis):
    return lax.all_gather(block, axis, axis=0, tiled=True)


def scatter_sum(partial, axis):
    return lax.psum_scatter(partial, axis, scatter_dimension=0, tiled=True)


def cube_gather(blocks, axis, join=True):
    n = lax.axis_size(axis)
    bits = [1 << b for b in range(n.bit_length() - 1)]
    half = blocks.shape[-1] // 2
    halves = []
    for part, order in (
        (blocks[..., :half], bits[1:] + bits[:1]),
        (blocks[..., half:], bits[:0:-1] + bits[:1]),
    ):
        held, offsets = part[None], [0]
        for bit in order:
            moved = lax.ppermute(held, axis, [(i, i ^ bit) for i in range(n)])
            offsets = offsets + [o ^ bit for o in offsets]
            if join or bit != order[-1]:
                held = jnp.concatenate([held, moved], axis=0)
        halves.append((held if join else (held, moved), tuple(offsets)))
    return halves


def cube_sum(vector, axes):
    for axis in axes:
        n = lax.axis_size(axis)
        bit = 1
        while bit < n:
            vector = vector + lax.ppermute(vector, axis, [(i, i ^ bit) for i in range(n)])
            bit *= 2
    return vector


def rotate_rows(values, cos_rows, sin_rows):
    half = HD // 2
    heads = []
    for h in range(values.shape[0] // HD):
        upper = values[h * HD : h * HD + half]
        lower = values[h * HD + half : (h + 1) * HD]
        heads.append(upper * cos_rows - lower * sin_rows)
        heads.append(lower * cos_rows + upper * sin_rows)
    return jnp.concatenate(heads, axis=0)


def dot_lanes(left_side, right_side):
    return lax.dot_general(
        left_side, right_side, (((1,), (1,)), ((), ())), preferred_element_type=jnp.float32
    )


def norm_project(gathered, gain_vec, weight_rows, cos_rows, sin_rows, group):
    blocks, tile, width = gathered.shape
    rows = blocks * tile
    columns = weight_rows.shape[0]
    packed = (group + 2) * HD

    def kernel(tokens_ref, gain_ref, weight_ref, cos_ref, sin_ref, normed_ref, out_ref):
        values = tokens_ref[0].astype(jnp.float32)
        row_scale = lax.rsqrt(jnp.mean(values * values, axis=-1, keepdims=True) + EPS)
        normed = (values * row_scale * gain_ref[...].astype(jnp.float32)).astype(LOW)
        normed_ref[...] = normed
        projected = dot_lanes(weight_ref[...], normed)
        for start in range(0, columns, packed):
            turned = start + packed - HD
            out_ref[start:turned] = rotate_rows(
                projected[start:turned], cos_ref[...], sin_ref[...]
            ).astype(LOW)
            out_ref[turned : turned + HD] = projected[turned : turned + HD].astype(LOW)

    half = HD // 2
    return pl.pallas_call(
        kernel,
        grid=(blocks,),
        in_specs=[
            pl.BlockSpec((1, tile, width), lambda i: (i, 0, 0)),
            pl.BlockSpec((1, width), lambda i: (0, 0)),
            pl.BlockSpec((columns, width), lambda i: (0, 0)),
            pl.BlockSpec((half, tile), lambda i: (0, i % (SEQLEN // tile))),
            pl.BlockSpec((half, tile), lambda i: (0, i % (SEQLEN // tile))),
        ],
        out_specs=[
            pl.BlockSpec((tile, width), lambda i: (i, 0)),
            pl.BlockSpec((columns, tile), lambda i: (0, i)),
        ],
        out_shape=[
            jax.ShapeDtypeStruct((rows, width), LOW),
            jax.ShapeDtypeStruct((columns, rows), LOW),
        ],
        cost_estimate=pl.CostEstimate(
            flops=2 * rows * width * columns, transcendentals=rows, bytes_accessed=12 << 20
        ),
        name="norm_project",
    )(gathered, gain_vec.reshape(1, -1), weight_rows, cos_rows, sin_rows)


def key_tiles(step, tile):
    return [(t * tile, t == step) for t in range(step + 1)]


def causal_tile(tile):
    key_at = lax.broadcasted_iota(jnp.int32, (tile, tile), 0)
    query_at = lax.broadcasted_iota(jnp.int32, (tile, tile), 1)
    return key_at <= query_at


def attend(projected, group):
    columns, rows = projected.shape
    packed = (group + 2) * HD
    kv_heads = columns // packed
    wide = group * HD
    tile = 256
    score_scale = HD ** (-0.5)

    def kernel(packed_ref, heads_ref, heads_t_ref, total_ref):
        keys = packed_ref[wide : wide + HD].astype(jnp.float32).T.astype(LOW)
        visible = causal_tile(tile)
        for step in range(SEQLEN // tile):
            here = slice(step * tile, (step + 1) * tile)
            for h in range(group):
                query = packed_ref[h * HD : (h + 1) * HD, here]
                parts = []
                for start, masked in key_tiles(step, tile):
                    part = jnp.dot(
                        keys[start : start + tile], query, preferred_element_type=jnp.float32
                    )
                    parts.append(jnp.where(visible, part, MASKED) if masked else part)
                top = functools.reduce(
                    jnp.maximum, [jnp.max(part, axis=0, keepdims=True) for part in parts]
                )
                parts = [jnp.exp((part - top) * score_scale) for part in parts]
                total = sum(jnp.sum(part, axis=0, keepdims=True) for part in parts)
                inverse = 1.0 / total
                mixed = sum(
                    jnp.dot(
                        packed_ref[wide + HD : packed, start : start + tile],
                        (part * inverse).astype(LOW),
                        preferred_element_type=jnp.float32,
                    )
                    for part, (start, _) in zip(parts, key_tiles(step, tile))
                )
                heads_t_ref[h * HD : (h + 1) * HD, here] = mixed.astype(LOW)
                total_ref[0, h : h + 1, here] = top * score_scale + jnp.log(total)
        heads_ref[...] = heads_t_ref[...].astype(jnp.float32).T.astype(LOW)

    return pl.pallas_call(
        kernel,
        grid=(rows // SEQLEN, kv_heads),
        in_specs=[pl.BlockSpec((packed, SEQLEN), lambda s, j: (j, s))],
        out_specs=[
            pl.BlockSpec((SEQLEN, wide), lambda s, j: (s, j)),
            pl.BlockSpec((wide, SEQLEN), lambda s, j: (j, s)),
            pl.BlockSpec((1, group, SEQLEN), lambda s, j: (j, 0, s)),
        ],
        out_shape=[
            jax.ShapeDtypeStruct((rows, kv_heads * wide), LOW),
            jax.ShapeDtypeStruct((kv_heads * wide, rows), LOW),
            jax.ShapeDtypeStruct((kv_heads, group, rows), jnp.float32),
        ],
        cost_estimate=pl.CostEstimate(
            flops=4 * rows * SEQLEN * kv_heads * wide,
            transcendentals=rows * SEQLEN * kv_heads * group,
            bytes_accessed=4 << 20,
        ),
        name="attend",
    )(projected)


def attend_back(projected, d_heads, totals, cos_rows, sin_rows):
    columns, rows = projected.shape
    kv_heads, group, _ = totals.shape
    packed = (group + 2) * HD
    wide = group * HD
    tile = 256
    score_scale = HD ** (-0.5)

    def kernel(
        packed_ref, d_heads_ref, total_ref, cos_ref, sin_ref, out_ref, key_sum, value_sum
    ):
        keys = packed_ref[wide : wide + HD].astype(jnp.float32).T.astype(LOW)
        values = packed_ref[wide + HD : packed].astype(jnp.float32).T.astype(LOW)
        visible = causal_tile(tile)
        key_sum[...] = jnp.zeros_like(key_sum)
        value_sum[...] = jnp.zeros_like(value_sum)
        for step in range(SEQLEN // tile):
            here = slice(step * tile, (step + 1) * tile)
            for h in range(group):
                query = packed_ref[h * HD : (h + 1) * HD, here]
                d_head = d_heads_ref[h * HD : (h + 1) * HD, here]
                log_total = total_ref[0, h : h + 1, here]
                probs, d_probs = [], []
                for start, masked in key_tiles(step, tile):
                    span = slice(start, start + tile)
                    part = jnp.dot(keys[span], query, preferred_element_type=jnp.float32)
                    part = jnp.exp(part * score_scale - log_total)
                    if masked:
                        part = jnp.where(visible, part, 0.0)
                    probs.append(part)
                    value_sum[:, span] += dot_lanes(d_head, part.astype(LOW))
                    d_probs.append(
                        jnp.dot(values[span], d_head, preferred_element_type=jnp.float32)
                    )
                row_sum = sum(
                    jnp.sum(part * d_part, axis=0, keepdims=True)
                    for part, d_part in zip(probs, d_probs)
                )
                d_query = jnp.zeros((HD, tile), jnp.float32)
                for (start, _), part, d_part in zip(key_tiles(step, tile), probs, d_probs):
                    span = slice(start, start + tile)
                    d_scores = (part * (d_part - row_sum)).astype(LOW)
                    d_query += jnp.dot(
                        packed_ref[wide : wide + HD, span],
                        d_scores,
                        preferred_element_type=jnp.float32,
                    )
                    key_sum[:, span] += dot_lanes(query, d_scores)
                out_ref[h * HD : (h + 1) * HD, here] = rotate_rows(
                    d_query * score_scale, cos_ref[:, here], -sin_ref[:, here]
                ).astype(LOW)
        out_ref[wide : wide + HD] = rotate_rows(
            key_sum[...] * score_scale, cos_ref[...], -sin_ref[...]
        ).astype(LOW)
        out_ref[wide + HD : packed] = value_sum[...].astype(LOW)

    half = HD // 2
    return pl.pallas_call(
        kernel,
        grid=(rows // SEQLEN, kv_heads),
        in_specs=[
            pl.BlockSpec((packed, SEQLEN), lambda s, j: (j, s)),
            pl.BlockSpec((wide, SEQLEN), lambda s, j: (j, s)),
            pl.BlockSpec((1, group, SEQLEN), lambda s, j: (j, 0, s)),
            pl.BlockSpec((half, SEQLEN), lambda s, j: (0, 0)),
            pl.BlockSpec((half, SEQLEN), lambda s, j: (0, 0)),
        ],
        out_specs=pl.BlockSpec((packed, SEQLEN), lambda s, j: (j, s)),
        out_shape=jax.ShapeDtypeStruct((columns, rows), LOW),
        scratch_shapes=[
            pltpu.VMEM((HD, SEQLEN), jnp.float32),
            pltpu.VMEM((HD, SEQLEN), jnp.float32),
        ],
        cost_estimate=pl.CostEstimate(
            flops=10 * rows * SEQLEN * kv_heads * wide,
            transcendentals=rows * SEQLEN * kv_heads * group,
            bytes_accessed=6 << 20,
        ),
        name="attend_back",
    )(projected, d_heads, totals, cos_rows, sin_rows)


def project_and_norm(all_heads, weights, gathered, gain_vec):
    groups, rows, group_columns = all_heads.shape
    (first, first_offsets), (second, second_offsets) = weights
    parts, _, depth, half = first.shape
    width = 2 * half
    tile = rows // groups
    places = jnp.stack([lax.axis_index(TP), lax.axis_index(DP)])

    def kernel(
        at_ref,
        heads_ref,
        first_ref,
        second_ref,
        tokens_ref,
        gain_ref,
        hidden_ref,
        normed_ref,
        turned_ref,
        weight_ref,
        wide_ref,
    ):
        step = pl.program_id(0)

        @pl.when(step == 0)
        def _():
            for side, part_ref, offsets in (
                (0, first_ref, first_offsets),
                (half, second_ref, second_offsets),
            ):
                for part in range(parts):
                    for g in range(groups):
                        start = g * group_columns + (at_ref[1] ^ offsets[part]) * depth
                        at = pl.ds(pl.multiple_of(start, depth), depth)
                        weight_ref[at, side : side + half] = part_ref[part, g]

        for g in range(groups):
            wide_ref[:, g * group_columns : (g + 1) * group_columns] = heads_ref[g]
        hidden = tokens_ref[0].astype(jnp.float32) + jnp.dot(
            wide_ref[...], weight_ref[...], preferred_element_type=jnp.float32
        )
        row_scale = lax.rsqrt(jnp.mean(hidden * hidden, axis=-1, keepdims=True) + EPS)
        normed = hidden * row_scale * gain_ref[...].astype(jnp.float32)
        normed_ref[...] = normed.astype(LOW)
        turned_ref[...] = normed.T.astype(LOW)

        @pl.when(step == at_ref[0])
        def _():
            hidden_ref[...] = hidden

    return pl.pallas_call(
        kernel,
        grid_spec=pltpu.PrefetchScalarGridSpec(
            num_scalar_prefetch=1,
            grid=(groups,),
            in_specs=[
                pl.BlockSpec((groups, tile, group_columns), lambda i, at_ref: (0, i, 0)),
                pl.BlockSpec(first.shape, lambda i, at_ref: (0, 0, 0, 0)),
                pl.BlockSpec(second.shape, lambda i, at_ref: (0, 0, 0, 0)),
                pl.BlockSpec((1, tile, width), lambda i, at_ref: (i, 0, 0)),
                pl.BlockSpec((1, width), lambda i, at_ref: (0, 0)),
            ],
            out_specs=[
                pl.BlockSpec((tile, width), lambda i, at_ref: (0, 0)),
                pl.BlockSpec((tile, width), lambda i, at_ref: (i, 0)),
                pl.BlockSpec((width, tile), lambda i, at_ref: (0, i)),
            ],
            scratch_shapes=[
                pltpu.VMEM((groups * group_columns, width), LOW),
                pltpu.VMEM((tile, groups * group_columns), LOW),
            ],
        ),
        out_shape=[
            jax.ShapeDtypeStruct((tile, width), jnp.float32),
            jax.ShapeDtypeStruct((rows, width), LOW),
            jax.ShapeDtypeStruct((width, rows), LOW),
        ],
        cost_estimate=pl.CostEstimate(
            flops=2 * rows * width * width, transcendentals=rows, bytes_accessed=24 << 20
        ),
        name="project_and_norm",
    )(places, all_heads, first, second, gathered, gain_vec.reshape(1, -1))


def gated_up(normed, w_gate, w_up):
    rows, width = normed.shape
    columns = w_gate.shape[1]
    tile = 256

    def kernel(normed_ref, gate_w_ref, up_w_ref, active_ref, turned_ref, smooth_ref, slope_ref):
        gate = jnp.dot(normed_ref[...], gate_w_ref[...], preferred_element_type=jnp.float32)
        up = jnp.dot(normed_ref[...], up_w_ref[...], preferred_element_type=jnp.float32)
        chance = jax.nn.sigmoid(gate)
        smooth = gate * chance
        active = smooth * up
        active_ref[...] = active.astype(LOW)
        turned_ref[...] = active.T.astype(LOW)
        smooth_ref[...] = smooth.astype(LOW)
        slope_ref[...] = (up * (chance * (1.0 + gate * (1.0 - chance)))).astype(LOW)

    column_block = pl.BlockSpec((rows, tile), lambda j: (0, j))
    weight_block = pl.BlockSpec((width, tile), lambda j: (0, j))
    flat = jax.ShapeDtypeStruct((rows, columns), LOW)
    return pl.pallas_call(
        kernel,
        grid=(columns // tile,),
        in_specs=[pl.BlockSpec((rows, width), lambda j: (0, 0)), weight_block, weight_block],
        out_specs=[
            column_block,
            pl.BlockSpec((tile, rows), lambda j: (j, 0)),
            column_block,
            column_block,
        ],
        out_shape=[flat, jax.ShapeDtypeStruct((columns, rows), LOW), flat, flat],
        cost_estimate=pl.CostEstimate(
            flops=4 * rows * width * columns,
            transcendentals=rows * columns,
            bytes_accessed=36 << 20,
        ),
        name="gated_up",
    )(normed, w_gate, w_up)


def gated_back(all_cot, w_down, smooth, slope):
    rows, width = all_cot.shape
    columns = w_down.shape[0]
    tile = 512

    def kernel(cot_ref, weight_ref, smooth_ref, slope_ref, d_gate_ref, d_up_ref):
        for start in range(0, tile, 256):
            here = slice(start, start + 256)
            d_active = dot_lanes(cot_ref[...], weight_ref[here, :])
            d_up_ref[:, here] = (d_active * smooth_ref[:, here].astype(jnp.float32)).astype(LOW)
            d_gate_ref[:, here] = (d_active * slope_ref[:, here].astype(jnp.float32)).astype(LOW)

    column_block = pl.BlockSpec((rows, tile), lambda j: (0, j))
    return pl.pallas_call(
        kernel,
        grid=(columns // tile,),
        in_specs=[
            pl.BlockSpec((rows, width), lambda j: (0, 0)),
            pl.BlockSpec((tile, width), lambda j: (j, 0)),
            column_block,
            column_block,
        ],
        out_specs=[column_block] * 2,
        out_shape=[jax.ShapeDtypeStruct((rows, columns), LOW)] * 2,
        cost_estimate=pl.CostEstimate(
            flops=2 * rows * width * columns, transcendentals=0, bytes_accessed=28 << 20
        ),
        name="gated_back",
    )(all_cot, w_down, smooth, slope)


def product(left, rights, folds):
    rows, depth = left.shape
    each = rights[0].shape[1]
    tile = 512
    column_steps = each // tile
    count = len(rights)
    per = count * column_steps // folds

    def kernel(left_ref, *refs):
        out_ref = refs[count]
        for k in range(count):

            def _(k=k):
                out_ref[...] = jnp.dot(
                    left_ref[...], refs[k][...], preferred_element_type=jnp.float32
                ).astype(LOW)

            if count == 1:
                _()
            else:
                pl.when(pl.program_id(0) // column_steps == k)(_)

    def right_block(k):
        return pl.BlockSpec(
            (depth, tile), lambda j: (0, jnp.clip(j - k * column_steps, 0, column_steps - 1))
        )

    return pl.pallas_call(
        kernel,
        grid=(count * column_steps,),
        in_specs=[pl.BlockSpec((rows, depth), lambda j: (0, 0))]
        + [right_block(k) for k in range(count)],
        out_specs=pl.BlockSpec((rows, tile), lambda j: (j // per, j % per)),
        out_shape=jax.ShapeDtypeStruct((rows * folds, count * each // folds), LOW),
        cost_estimate=pl.CostEstimate(
            flops=2 * rows * depth * count * each,
            transcendentals=0,
            bytes_accessed=2 * (rows * depth + (depth + rows) * count * each),
        ),
        name="product",
    )(left, *rights)


def pair_product(places, tile, first, first_weight, second, second_weight):
    rows, depth = first.shape
    columns = first_weight.shape[0]
    count = len(places)
    part = 512 if count == 1 else 256
    at = jnp.stack(places)

    def kernel(at_ref, first_ref, second_ref, first_w_ref, second_w_ref, *out_refs):
        for k, out_ref in enumerate(out_refs):
            here = (
                slice(None)
                if count == 1
                else pl.ds(pl.multiple_of(at_ref[k] * tile, tile), tile)
            )
            out_ref[...] = (
                dot_lanes(first_ref[here, :], first_w_ref[...])
                + dot_lanes(second_ref[here, :], second_w_ref[...])
            ).astype(LOW)

    held = (
        pl.BlockSpec((tile, depth), lambda j, at_ref: (at_ref[0], 0))
        if count == 1
        else pl.BlockSpec((rows, depth), lambda j, at_ref: (0, 0))
    )
    weight_block = pl.BlockSpec((part, depth), lambda j, at_ref: (j, 0))
    return pl.pallas_call(
        kernel,
        grid_spec=pltpu.PrefetchScalarGridSpec(
            num_scalar_prefetch=1,
            grid=(columns // part,),
            in_specs=[held, held, weight_block, weight_block],
            out_specs=[pl.BlockSpec((tile, part), lambda j, at_ref: (0, j))] * count,
        ),
        out_shape=[jax.ShapeDtypeStruct((tile, columns), LOW)] * count,
        cost_estimate=pl.CostEstimate(
            flops=4 * count * tile * depth * columns, transcendentals=0, bytes_accessed=20 << 20
        ),
        name="pair_product",
    )(at, first, second, first_weight, second_weight)


def projection_back(places, d_projected, weight_rows, gathered):
    columns, width = weight_rows.shape
    tile = gathered.shape[1]
    count = len(places)
    at = jnp.stack(places)

    def kernel(at_ref, d_ref, weight_ref, tokens_ref, *out_refs):
        step = pl.program_id(0)
        grads = d_ref[...].astype(jnp.float32).T.astype(LOW)
        made = jnp.dot(grads, weight_ref[...], preferred_element_type=jnp.float32).astype(LOW)
        values = tokens_ref[0].astype(jnp.float32)
        row_scale = lax.rsqrt(jnp.mean(values * values, axis=-1, keepdims=True) + EPS)
        added = jnp.sum(made.astype(jnp.float32) * values * row_scale, axis=0, keepdims=True)
        gain_ref = out_refs[count]
        gain_ref[...] = jnp.where(step == 0, added, gain_ref[...] + added)
        for k in range(count):

            @pl.when(step == k)
            def _():
                out_refs[k][...] = made

    return pl.pallas_call(
        kernel,
        grid_spec=pltpu.PrefetchScalarGridSpec(
            num_scalar_prefetch=1,
            grid=(count,),
            in_specs=[
                pl.BlockSpec((columns, tile), lambda i, at_ref: (0, at_ref[i])),
                pl.BlockSpec((columns, width), lambda i, at_ref: (0, 0)),
                pl.BlockSpec((1, tile, width), lambda i, at_ref: (at_ref[i], 0, 0)),
            ],
            out_specs=[pl.BlockSpec((tile, width), lambda i, at_ref: (0, 0))] * count
            + [pl.BlockSpec((1, width), lambda i, at_ref: (0, 0))],
        ),
        out_shape=[jax.ShapeDtypeStruct((tile, width), LOW)] * count
        + [jax.ShapeDtypeStruct((1, width), jnp.float32)],
        cost_estimate=pl.CostEstimate(
            flops=2 * count * tile * columns * width, transcendentals=0, bytes_accessed=8 << 20
        ),
        name="projection_back",
    )(at, d_projected, weight_rows, gathered)


def norm_back(values, gain_vec, base, blocks):
    rows, width = values.shape
    part = 64
    count = len(blocks)

    def kernel(values_ref, gain_ref, base_ref, *refs):
        wide_ref, low_ref, sum_ref = refs[count:]
        step = pl.program_id(0)
        upstream = sum(ref[...].astype(jnp.float32) for ref in refs[:count])
        held = values_ref[...].astype(jnp.float32)
        row_scale = lax.rsqrt(jnp.mean(held * held, axis=-1, keepdims=True) + EPS)
        scaled = held * row_scale
        added = jnp.sum(upstream * scaled, axis=0, keepdims=True)
        sum_ref[...] = jnp.where(step == 0, added, sum_ref[...] + added)
        weighted = upstream * gain_ref[...].astype(jnp.float32)
        inner = jnp.mean(weighted * scaled, axis=-1, keepdims=True)
        result = base_ref[...].astype(jnp.float32) + row_scale * (weighted - scaled * inner)
        wide_ref[...] = result
        low_ref[...] = result.astype(LOW)

    tile_block = pl.BlockSpec((part, width), lambda i: (i, 0))
    line = pl.BlockSpec((1, width), lambda i: (0, 0))
    return pl.pallas_call(
        kernel,
        grid=(rows // part,),
        in_specs=[tile_block, line, tile_block] + [tile_block] * count,
        out_specs=[tile_block, tile_block, line],
        out_shape=[
            jax.ShapeDtypeStruct((rows, width), jnp.float32),
            jax.ShapeDtypeStruct((rows, width), LOW),
            jax.ShapeDtypeStruct((1, width), jnp.float32),
        ],
        cost_estimate=pl.CostEstimate(
            flops=16 * rows * width, transcendentals=rows, bytes_accessed=10 << 20
        ),
        name="norm_back",
    )(values, gain_vec.reshape(1, -1), base, *blocks)


def exchange(make_blocks, axis):
    n = lax.axis_size(axis)
    me = lax.axis_index(axis)
    places = [(me + hop) % n for hop in range(1, n)] + [me]
    made = list(make_blocks(places[:1]))
    moved = []
    for hop in range(1, n):
        if hop == 2:
            made += make_blocks(places[1:])
        pairs = [(i, (i + hop) % n) for i in range(n)]
        moved.append(lax.ppermute(made[hop - 1], axis, pairs))
    return moved + made[n - 1 :]


def place_blocks(halves, axis):
    (first, first_offsets), (second, second_offsets) = halves
    some, rows, half = first[0].shape
    parts = 2 * some

    def kernel(at_ref, *refs):
        out_ref = refs[4]
        k = pl.program_id(0)
        for side, offsets in enumerate((first_offsets, second_offsets)):
            columns = slice(side * half, (side + 1) * half)
            late = functools.reduce(
                jnp.logical_or, [k == offset for offset in offsets[some:]]
            )
            early_ref, late_ref = refs[2 * side : 2 * side + 2]
            out_ref[:, columns] = jnp.where(late, late_ref[0], early_ref[0]).astype(jnp.float32)

    def entry(offsets):
        def index(k, at_ref):
            found = 0
            for at, offset in enumerate(offsets):
                found = jnp.where(k == offset, at, found)
            return (found, 0, 0)

        return pl.BlockSpec((1, rows, half), index)

    specs = []
    for offsets in (first_offsets, second_offsets):
        specs += [entry(offsets[:some]), entry(offsets[some:])]
    return pl.pallas_call(
        kernel,
        grid_spec=pltpu.PrefetchScalarGridSpec(
            num_scalar_prefetch=1,
            grid=(parts,),
            in_specs=specs,
            out_specs=pl.BlockSpec((rows, 2 * half), lambda k, at_ref: (at_ref[0] ^ k, 0)),
        ),
        out_shape=jax.ShapeDtypeStruct((parts * rows, 2 * half), jnp.float32),
        cost_estimate=pl.CostEstimate(
            flops=0, transcendentals=0, bytes_accessed=12 * parts * rows * half
        ),
        name="place_blocks",
    )(lax.axis_index(axis).reshape(1), *first, *second)


def unpack_attention(shared, q_columns, k_columns, folds):
    rows, columns = shared.shape
    block = rows // folds
    kv_heads = k_columns // HD
    wide = q_columns // kv_heads
    packed = wide + 2 * HD
    end = kv_heads * packed

    def kernel(shared_ref, query_ref, key_ref, value_ref, output_ref):
        for j in range(kv_heads):
            start = j * packed
            query_ref[:, j * wide : (j + 1) * wide] = shared_ref[
                :, start : start + wide
            ].astype(jnp.float32)
            for at, ref in ((start + wide, key_ref), (start + wide + HD, value_ref)):
                ref[:, j * HD : (j + 1) * HD] = shared_ref[:, at : at + HD].astype(jnp.float32)
        output_ref[...] = shared_ref[:, end:].astype(jnp.float32)

    narrow = pl.BlockSpec((block, k_columns), lambda p: (p, 0))
    return pl.pallas_call(
        kernel,
        grid=(folds,),
        in_specs=[pl.BlockSpec((block, columns), lambda p: (p, 0))],
        out_specs=[
            pl.BlockSpec((block, q_columns), lambda p: (p, 0)),
            narrow,
            narrow,
            pl.BlockSpec((block, columns - end), lambda p: (0, p)),
        ],
        out_shape=[
            jax.ShapeDtypeStruct((rows, q_columns), jnp.float32),
            jax.ShapeDtypeStruct((rows, k_columns), jnp.float32),
            jax.ShapeDtypeStruct((rows, k_columns), jnp.float32),
            jax.ShapeDtypeStruct((block, (columns - end) * folds), jnp.float32),
        ],
        cost_estimate=pl.CostEstimate(
            flops=0, transcendentals=0, bytes_accessed=6 * rows * columns
        ),
        name="unpack_attention",
    )(shared)


def add_all(blocks):
    return sum(block.astype(jnp.float32) for block in blocks)


def row_major(array):
    return with_layout_constraint(array, Layout(major_to_minor=tuple(range(array.ndim))))


def split_columns(array, parts):
    if parts == 1:
        return array
    rows, columns = array.shape[0], array.shape[1] // parts
    return array.reshape(rows, parts, columns).swapaxes(0, 1).reshape(parts * rows, columns)


def join_columns(array, parts):
    if parts == 1:
        return array
    rows, columns = array.shape[0] // parts, array.shape[1]
    return array.reshape(parts, rows, columns).swapaxes(0, 1).reshape(rows, parts * columns)


def block(
    tokens,
    cotangent,
    norm1_gain,
    w_query,
    w_key,
    w_value,
    w_output,
    norm2_gain,
    w_gate,
    w_up,
    w_down,
):
    n_dp = lax.axis_size(DP)
    own_rows, width = tokens.shape
    depth = w_output.shape[0] // n_dp
    q_columns, k_columns = w_query.shape[1], w_key.shape[1]
    kv_heads = k_columns // HD
    group = q_columns // k_columns
    ff_columns = w_gate.shape[1]
    ff_folds = width // w_down.shape[0]
    folds = width // w_output.shape[0]
    nothing = scatter_sum(tokens[:, :128] * 0, DP)[0, 0]
    gathered = lax.all_gather(tokens, TP, axis=0)
    own_part = lax.dynamic_slice_in_dim(w_output, lax.axis_index(DP) * depth, depth, 0)
    output_part = lax.all_gather(own_part, TP, axis=0)
    all_output = cube_gather(output_part, DP)
    cos_table, sin_table = rope_tables(SEQLEN, HD)
    cos_rows, sin_rows = cos_table.T, sin_table.T
    pieces = []
    for j in range(kv_heads):
        pieces.append(w_query[:, j * group * HD : (j + 1) * group * HD].T)
        pieces.append(w_key[:, j * HD : (j + 1) * HD].T)
        pieces.append(w_value[:, j * HD : (j + 1) * HD].T)
    weight_rows = jnp.concatenate(pieces, axis=0)
    normed1, projected = norm_project(
        gathered, norm1_gain, weight_rows, cos_rows, sin_rows, group
    )
    heads_out, heads_rows, totals = attend(projected, group)
    all_heads = lax.all_gather(heads_out, TP, axis=0)
    all_cot = gather_rows(cotangent, TP)
    hidden_state, normed2, normed2_rows = project_and_norm(
        all_heads, all_output, gathered, norm2_gain.astype(jnp.float32) + nothing.astype(jnp.float32)
    )
    activated, active_rows, smooth, slope = gated_up(normed2, w_gate, w_up)
    mlp_part = product(activated, [w_down], 1)
    half_width = width // 2

    def part_of(columns):
        return lambda places: [
            lax.dynamic_slice(mlp_part, (place * own_rows, columns), (own_rows, half_width))
            for place in places
        ]

    first_half = exchange(part_of(0), TP)
    second_half = exchange(part_of(half_width), TP)
    output = (
        hidden_state
        + jnp.concatenate([add_all(first_half), add_all(second_half)], axis=1)
    ).astype(LOW)
    d_gate, d_up = gated_back(all_cot, w_down, smooth, slope)
    grad_down = product(active_rows, [all_cot], ff_folds)
    part_down = scatter_sum(grad_down, DP)
    dn2_blocks = exchange(
        lambda places: pair_product(places, own_rows, d_gate, w_gate, d_up, w_up), TP
    )
    gate_up_grads = product(normed2_rows, [d_gate, d_up], 1)
    part_gate_up = scatter_sum(gate_up_grads, DP)
    d_state, state_low, gain_two = norm_back(hidden_state, norm2_gain, cotangent, dn2_blocks)
    d_state_low = gather_rows(state_low, TP)
    gain_two_sum = cube_sum(gain_two[0], (DP, TP))
    grad_output = jnp.dot(heads_rows, d_state_low, preferred_element_type=jnp.float32)
    output_grads = row_major(split_columns(grad_output.astype(LOW), folds))
    part_out = scatter_sum(output_grads, DP)
    d_heads_rows = contract_cols(w_output, d_state_low).astype(LOW)
    d_projected = attend_back(projected, d_heads_rows, totals, cos_rows, sin_rows)
    gains = []

    def dn1_blocks_of(places):
        *made, gain = projection_back(places, d_projected, weight_rows, gathered)
        gains.append(gain)
        return made

    dn1_blocks = exchange(dn1_blocks_of, TP)
    gain_one_sum = cube_sum(sum(gains)[0], (DP, TP))
    packed_grads = row_major(
        lax.dot_general(
            normed1,
            d_projected,
            (((0,), (1,)), ((), ())),
            preferred_element_type=jnp.float32,
        ).astype(LOW)
    )
    part_attn = scatter_sum(packed_grads, DP)
    down_halves = cube_gather(part_down, DP, join=False)
    full_down = join_columns(place_blocks(down_halves, DP), ff_folds)
    shared_ff = row_major(gather_rows(part_gate_up, DP))
    shared_attn = row_major(
        gather_rows(row_major(jnp.concatenate([part_attn, part_out], axis=1)), DP)
    )
    _, input_grad, _ = norm_back(tokens, norm1_gain, d_state, dn1_blocks)
    full_gate = shared_ff[:, :ff_columns].astype(jnp.float32)
    full_up = shared_ff[:, ff_columns:].astype(jnp.float32)
    full_query, full_key, full_value, full_output = unpack_attention(
        shared_attn, q_columns, k_columns, folds
    )
    return (
        output,
        input_grad,
        gain_one_sum,
        full_query,
        full_key,
        full_value,
        full_output,
        gain_two_sum,
        full_gate,
        full_up,
        full_down,
    )


ROWS, COLUMNS, HIDDEN = P((DP, TP), None), P(None, TP), P(TP, None)


def solution(mesh):
    return jax.shard_map(
        block,
        mesh=mesh,
        in_specs=(ROWS, ROWS, P(), COLUMNS, COLUMNS, COLUMNS, HIDDEN, P(), COLUMNS, COLUMNS, HIDDEN),
        out_specs=(ROWS, ROWS, P(), COLUMNS, COLUMNS, COLUMNS, HIDDEN, P(), COLUMNS, COLUMNS, HIDDEN),
        check_vma=False,
    )
```

```python
import functools

import jax
import jax.numpy as jnp
from jax import lax
from jax.experimental import pallas as pl
from jax.experimental.pallas import tpu as pltpu
from jax.experimental.layout import Layout, with_layout_constraint
from jax.sharding import PartitionSpec as P


LOW = jnp.bfloat16
DP, TP = "dp", "tensor"

HD = 64
SEQLEN = 512


EPS = 1e-05
ROPE_BASE = 500000.0
MASKED = -1e30


def rope_tables(length, columns):
    half_width = columns // 2
    frequency = ROPE_BASE ** (-(jnp.arange(half_width, dtype=jnp.float32) * 2.0 / columns))
    angles = jnp.arange(length, dtype=jnp.float32)[:, None] * frequency[None, :]
    return (jnp.cos(angles), jnp.sin(angles))


def contract_cols(left_side, right_side):
    return lax.dot_general(
        left_side, right_side, (((1,), (1,)), ((), ())), preferred_element_type=jnp.float32
    )


def gather_rows(block, axis):
    return lax.all_gather(block, axis, axis=0, tiled=True)


def scatter_sum(partial, axis):
    return lax.psum_scatter(partial, axis, scatter_dimension=0, tiled=True)


def cube_gather(blocks, axis, join=True):
    n = lax.axis_size(axis)
    bits = [1 << b for b in range(n.bit_length() - 1)]
    half = blocks.shape[-1] // 2
    halves = []
    for part, order in (
        (blocks[..., :half], bits[1:] + bits[:1]),
        (blocks[..., half:], bits[:0:-1] + bits[:1]),
    ):
        held, offsets = part[None], [0]
        for bit in order:
            moved = lax.ppermute(held, axis, [(i, i ^ bit) for i in range(n)])
            offsets = offsets + [o ^ bit for o in offsets]
            if join or bit != order[-1]:
                held = jnp.concatenate([held, moved], axis=0)
        halves.append((held if join else (held, moved), tuple(offsets)))
    return halves


def cube_sum(vector, axes):
    for axis in axes:
        n = lax.axis_size(axis)
        bit = 1
        while bit < n:
            vector = vector + lax.ppermute(vector, axis, [(i, i ^ bit) for i in range(n)])
            bit *= 2
    return vector


def rotate_rows(values, cos_rows, sin_rows):
    half = HD // 2
    heads = []
    for h in range(values.shape[0] // HD):
        upper = values[h * HD : h * HD + half]
        lower = values[h * HD + half : (h + 1) * HD]
        heads.append(upper * cos_rows - lower * sin_rows)
        heads.append(lower * cos_rows + upper * sin_rows)
    return jnp.concatenate(heads, axis=0)


def dot_lanes(left_side, right_side):
    return lax.dot_general(
        left_side, right_side, (((1,), (1,)), ((), ())), preferred_element_type=jnp.float32
    )


def norm_project(gathered, gain_vec, weight_rows, cos_rows, sin_rows, group):
    blocks, tile, width = gathered.shape
    rows = blocks * tile
    columns = weight_rows.shape[0]
    packed = (group + 2) * HD

    def kernel(tokens_ref, gain_ref, weight_ref, cos_ref, sin_ref, normed_ref, out_ref):
        values = tokens_ref[0].astype(jnp.float32)
        row_scale = lax.rsqrt(jnp.mean(values * values, axis=-1, keepdims=True) + EPS)
        normed = (values * row_scale * gain_ref[...].astype(jnp.float32)).astype(LOW)
        normed_ref[...] = normed
        projected = dot_lanes(weight_ref[...], normed)
        for start in range(0, columns, packed):
            turned = start + packed - HD
            out_ref[start:turned] = rotate_rows(
                projected[start:turned], cos_ref[...], sin_ref[...]
            ).astype(LOW)
            out_ref[turned : turned + HD] = projected[turned : turned + HD].astype(LOW)

    half = HD // 2
    return pl.pallas_call(
        kernel,
        grid=(blocks,),
        in_specs=[
            pl.BlockSpec((1, tile, width), lambda i: (i, 0, 0)),
            pl.BlockSpec((1, width), lambda i: (0, 0)),
            pl.BlockSpec((columns, width), lambda i: (0, 0)),
            pl.BlockSpec((half, tile), lambda i: (0, i % (SEQLEN // tile))),
            pl.BlockSpec((half, tile), lambda i: (0, i % (SEQLEN // tile))),
        ],
        out_specs=[
            pl.BlockSpec((tile, width), lambda i: (i, 0)),
            pl.BlockSpec((columns, tile), lambda i: (0, i)),
        ],
        out_shape=[
            jax.ShapeDtypeStruct((rows, width), LOW),
            jax.ShapeDtypeStruct((columns, rows), LOW),
        ],
        cost_estimate=pl.CostEstimate(
            flops=2 * rows * width * columns, transcendentals=rows, bytes_accessed=12 << 20
        ),
        name="norm_project",
    )(gathered, gain_vec.reshape(1, -1), weight_rows, cos_rows, sin_rows)


def key_tiles(step, tile):
    return [(t * tile, t == step) for t in range(step + 1)]


def causal_tile(tile):
    key_at = lax.broadcasted_iota(jnp.int32, (tile, tile), 0)
    query_at = lax.broadcasted_iota(jnp.int32, (tile, tile), 1)
    return key_at <= query_at


def attend(projected, group):
    columns, rows = projected.shape
    packed = (group + 2) * HD
    kv_heads = columns // packed
    wide = group * HD
    tile = 256
    score_scale = HD ** (-0.5)

    def kernel(packed_ref, heads_ref, heads_t_ref, total_ref):
        keys = packed_ref[wide : wide + HD].astype(jnp.float32).T.astype(LOW)
        visible = causal_tile(tile)
        for step in range(SEQLEN // tile):
            here = slice(step * tile, (step + 1) * tile)
            for h in range(group):
                query = packed_ref[h * HD : (h + 1) * HD, here]
                parts = []
                for start, masked in key_tiles(step, tile):
                    part = jnp.dot(
                        keys[start : start + tile], query, preferred_element_type=jnp.float32
                    )
                    parts.append(jnp.where(visible, part, MASKED) if masked else part)
                top = functools.reduce(
                    jnp.maximum, [jnp.max(part, axis=0, keepdims=True) for part in parts]
                )
                parts = [jnp.exp((part - top) * score_scale) for part in parts]
                total = sum(jnp.sum(part, axis=0, keepdims=True) for part in parts)
                inverse = 1.0 / total
                mixed = sum(
                    jnp.dot(
                        packed_ref[wide + HD : packed, start : start + tile],
                        (part * inverse).astype(LOW),
                        preferred_element_type=jnp.float32,
                    )
                    for part, (start, _) in zip(parts, key_tiles(step, tile))
                )
                heads_t_ref[h * HD : (h + 1) * HD, here] = mixed.astype(LOW)
                total_ref[0, h : h + 1, here] = top * score_scale + jnp.log(total)
        heads_ref[...] = heads_t_ref[...].astype(jnp.float32).T.astype(LOW)

    return pl.pallas_call(
        kernel,
        grid=(rows // SEQLEN, kv_heads),
        in_specs=[pl.BlockSpec((packed, SEQLEN), lambda s, j: (j, s))],
        out_specs=[
            pl.BlockSpec((SEQLEN, wide), lambda s, j: (s, j)),
            pl.BlockSpec((wide, SEQLEN), lambda s, j: (j, s)),
            pl.BlockSpec((1, group, SEQLEN), lambda s, j: (j, 0, s)),
        ],
        out_shape=[
            jax.ShapeDtypeStruct((rows, kv_heads * wide), LOW),
            jax.ShapeDtypeStruct((kv_heads * wide, rows), LOW),
            jax.ShapeDtypeStruct((kv_heads, group, rows), jnp.float32),
        ],
        cost_estimate=pl.CostEstimate(
            flops=4 * rows * SEQLEN * kv_heads * wide,
            transcendentals=rows * SEQLEN * kv_heads * group,
            bytes_accessed=4 << 20,
        ),
        name="attend",
    )(projected)


def attend_back(projected, d_heads, totals, cos_rows, sin_rows):
    columns, rows = projected.shape
    kv_heads, group, _ = totals.shape
    packed = (group + 2) * HD
    wide = group * HD
    tile = 256
    score_scale = HD ** (-0.5)

    def kernel(
        packed_ref, d_heads_ref, total_ref, cos_ref, sin_ref, out_ref, key_sum, value_sum
    ):
        keys = packed_ref[wide : wide + HD].astype(jnp.float32).T.astype(LOW)
        values = packed_ref[wide + HD : packed].astype(jnp.float32).T.astype(LOW)
        visible = causal_tile(tile)
        key_sum[...] = jnp.zeros_like(key_sum)
        value_sum[...] = jnp.zeros_like(value_sum)
        for step in range(SEQLEN // tile):
            here = slice(step * tile, (step + 1) * tile)
            for h in range(group):
                query = packed_ref[h * HD : (h + 1) * HD, here]
                d_head = d_heads_ref[h * HD : (h + 1) * HD, here]
                log_total = total_ref[0, h : h + 1, here]
                probs, d_probs = [], []
                for start, masked in key_tiles(step, tile):
                    span = slice(start, start + tile)
                    part = jnp.dot(keys[span], query, preferred_element_type=jnp.float32)
                    part = jnp.exp(part * score_scale - log_total)
                    if masked:
                        part = jnp.where(visible, part, 0.0)
                    probs.append(part)
                    value_sum[:, span] += dot_lanes(d_head, part.astype(LOW))
                    d_probs.append(
                        jnp.dot(values[span], d_head, preferred_element_type=jnp.float32)
                    )
                row_sum = sum(
                    jnp.sum(part * d_part, axis=0, keepdims=True)
                    for part, d_part in zip(probs, d_probs)
                )
                d_query = jnp.zeros((HD, tile), jnp.float32)
                for (start, _), part, d_part in zip(key_tiles(step, tile), probs, d_probs):
                    span = slice(start, start + tile)
                    d_scores = (part * (d_part - row_sum)).astype(LOW)
                    d_query += jnp.dot(
                        packed_ref[wide : wide + HD, span],
                        d_scores,
                        preferred_element_type=jnp.float32,
                    )
                    key_sum[:, span] += dot_lanes(query, d_scores)
                out_ref[h * HD : (h + 1) * HD, here] = rotate_rows(
                    d_query * score_scale, cos_ref[:, here], -sin_ref[:, here]
                ).astype(LOW)
        out_ref[wide : wide + HD] = rotate_rows(
            key_sum[...] * score_scale, cos_ref[...], -sin_ref[...]
        ).astype(LOW)
        out_ref[wide + HD : packed] = value_sum[...].astype(LOW)

    half = HD // 2
    return pl.pallas_call(
        kernel,
        grid=(rows // SEQLEN, kv_heads),
        in_specs=[
            pl.BlockSpec((packed, SEQLEN), lambda s, j: (j, s)),
            pl.BlockSpec((wide, SEQLEN), lambda s, j: (j, s)),
            pl.BlockSpec((1, group, SEQLEN), lambda s, j: (j, 0, s)),
            pl.BlockSpec((half, SEQLEN), lambda s, j: (0, 0)),
            pl.BlockSpec((half, SEQLEN), lambda s, j: (0, 0)),
        ],
        out_specs=pl.BlockSpec((packed, SEQLEN), lambda s, j: (j, s)),
        out_shape=jax.ShapeDtypeStruct((columns, rows), LOW),
        scratch_shapes=[
            pltpu.VMEM((HD, SEQLEN), jnp.float32),
            pltpu.VMEM((HD, SEQLEN), jnp.float32),
        ],
        cost_estimate=pl.CostEstimate(
            flops=10 * rows * SEQLEN * kv_heads * wide,
            transcendentals=rows * SEQLEN * kv_heads * group,
            bytes_accessed=6 << 20,
        ),
        name="attend_back",
    )(projected, d_heads, totals, cos_rows, sin_rows)


def project_and_norm(all_heads, weights, gathered, gain_vec):
    groups, rows, group_columns = all_heads.shape
    (first, first_offsets), (second, second_offsets) = weights
    parts, _, depth, half = first.shape
    width = 2 * half
    tile = rows // groups
    places = jnp.stack([lax.axis_index(TP), lax.axis_index(DP)])

    def kernel(
        at_ref,
        heads_ref,
        first_ref,
        second_ref,
        tokens_ref,
        gain_ref,
        hidden_ref,
        normed_ref,
        turned_ref,
        weight_ref,
        wide_ref,
    ):
        step = pl.program_id(0)

        @pl.when(step == 0)
        def _():
            for side, part_ref, offsets in (
                (0, first_ref, first_offsets),
                (half, second_ref, second_offsets),
            ):
                for part in range(parts):
                    for g in range(groups):
                        start = g * group_columns + (at_ref[1] ^ offsets[part]) * depth
                        at = pl.ds(pl.multiple_of(start, depth), depth)
                        weight_ref[at, side : side + half] = part_ref[part, g]

        for g in range(groups):
            wide_ref[:, g * group_columns : (g + 1) * group_columns] = heads_ref[g]
        hidden = tokens_ref[0].astype(jnp.float32) + jnp.dot(
            wide_ref[...], weight_ref[...], preferred_element_type=jnp.float32
        )
        row_scale = lax.rsqrt(jnp.mean(hidden * hidden, axis=-1, keepdims=True) + EPS)
        normed = hidden * row_scale * gain_ref[...].astype(jnp.float32)
        normed_ref[...] = normed.astype(LOW)
        turned_ref[...] = normed.T.astype(LOW)

        @pl.when(step == at_ref[0])
        def _():
            hidden_ref[...] = hidden

    return pl.pallas_call(
        kernel,
        grid_spec=pltpu.PrefetchScalarGridSpec(
            num_scalar_prefetch=1,
            grid=(groups,),
            in_specs=[
                pl.BlockSpec((groups, tile, group_columns), lambda i, at_ref: (0, i, 0)),
                pl.BlockSpec(first.shape, lambda i, at_ref: (0, 0, 0, 0)),
                pl.BlockSpec(second.shape, lambda i, at_ref: (0, 0, 0, 0)),
                pl.BlockSpec((1, tile, width), lambda i, at_ref: (i, 0, 0)),
                pl.BlockSpec((1, width), lambda i, at_ref: (0, 0)),
            ],
            out_specs=[
                pl.BlockSpec((tile, width), lambda i, at_ref: (0, 0)),
                pl.BlockSpec((tile, width), lambda i, at_ref: (i, 0)),
                pl.BlockSpec((width, tile), lambda i, at_ref: (0, i)),
            ],
            scratch_shapes=[
                pltpu.VMEM((groups * group_columns, width), LOW),
                pltpu.VMEM((tile, groups * group_columns), LOW),
            ],
        ),
        out_shape=[
            jax.ShapeDtypeStruct((tile, width), jnp.float32),
            jax.ShapeDtypeStruct((rows, width), LOW),
            jax.ShapeDtypeStruct((width, rows), LOW),
        ],
        cost_estimate=pl.CostEstimate(
            flops=2 * rows * width * width, transcendentals=rows, bytes_accessed=24 << 20
        ),
        name="project_and_norm",
    )(places, all_heads, first, second, gathered, gain_vec.reshape(1, -1))


def gated_up(normed, w_gate, w_up):
    rows, width = normed.shape
    columns = w_gate.shape[1]
    tile = 256

    def kernel(normed_ref, gate_w_ref, up_w_ref, active_ref, turned_ref, smooth_ref, slope_ref):
        gate = jnp.dot(normed_ref[...], gate_w_ref[...], preferred_element_type=jnp.float32)
        up = jnp.dot(normed_ref[...], up_w_ref[...], preferred_element_type=jnp.float32)
        chance = jax.nn.sigmoid(gate)
        smooth = gate * chance
        active = smooth * up
        active_ref[...] = active.astype(LOW)
        turned_ref[...] = active.T.astype(LOW)
        smooth_ref[...] = smooth.astype(LOW)
        slope_ref[...] = (up * (chance * (1.0 + gate * (1.0 - chance)))).astype(LOW)

    column_block = pl.BlockSpec((rows, tile), lambda j: (0, j))
    weight_block = pl.BlockSpec((width, tile), lambda j: (0, j))
    flat = jax.ShapeDtypeStruct((rows, columns), LOW)
    return pl.pallas_call(
        kernel,
        grid=(columns // tile,),
        in_specs=[pl.BlockSpec((rows, width), lambda j: (0, 0)), weight_block, weight_block],
        out_specs=[
            column_block,
            pl.BlockSpec((tile, rows), lambda j: (j, 0)),
            column_block,
            column_block,
        ],
        out_shape=[flat, jax.ShapeDtypeStruct((columns, rows), LOW), flat, flat],
        cost_estimate=pl.CostEstimate(
            flops=4 * rows * width * columns,
            transcendentals=rows * columns,
            bytes_accessed=36 << 20,
        ),
        name="gated_up",
    )(normed, w_gate, w_up)


def gated_back(all_cot, w_down, smooth, slope):
    rows, width = all_cot.shape
    columns = w_down.shape[0]
    tile = 512

    def kernel(cot_ref, weight_ref, smooth_ref, slope_ref, d_gate_ref, d_up_ref):
        for start in range(0, tile, 256):
            here = slice(start, start + 256)
            d_active = dot_lanes(cot_ref[...], weight_ref[here, :])
            d_up_ref[:, here] = (d_active * smooth_ref[:, here].astype(jnp.float32)).astype(LOW)
            d_gate_ref[:, here] = (d_active * slope_ref[:, here].astype(jnp.float32)).astype(LOW)

    column_block = pl.BlockSpec((rows, tile), lambda j: (0, j))
    return pl.pallas_call(
        kernel,
        grid=(columns // tile,),
        in_specs=[
            pl.BlockSpec((rows, width), lambda j: (0, 0)),
            pl.BlockSpec((tile, width), lambda j: (j, 0)),
            column_block,
            column_block,
        ],
        out_specs=[column_block] * 2,
        out_shape=[jax.ShapeDtypeStruct((rows, columns), LOW)] * 2,
        cost_estimate=pl.CostEstimate(
            flops=2 * rows * width * columns, transcendentals=0, bytes_accessed=28 << 20
        ),
        name="gated_back",
    )(all_cot, w_down, smooth, slope)


def product(left, rights, folds):
    rows, depth = left.shape
    each = rights[0].shape[1]
    tile = 512
    column_steps = each // tile
    count = len(rights)
    per = count * column_steps // folds

    def kernel(left_ref, *refs):
        out_ref = refs[count]
        for k in range(count):

            def _(k=k):
                out_ref[...] = jnp.dot(
                    left_ref[...], refs[k][...], preferred_element_type=jnp.float32
                ).astype(LOW)

            if count == 1:
                _()
            else:
                pl.when(pl.program_id(0) // column_steps == k)(_)

    def right_block(k):
        return pl.BlockSpec(
            (depth, tile), lambda j: (0, jnp.clip(j - k * column_steps, 0, column_steps - 1))
        )

    return pl.pallas_call(
        kernel,
        grid=(count * column_steps,),
        in_specs=[pl.BlockSpec((rows, depth), lambda j: (0, 0))]
        + [right_block(k) for k in range(count)],
        out_specs=pl.BlockSpec((rows, tile), lambda j: (j // per, j % per)),
        out_shape=jax.ShapeDtypeStruct((rows * folds, count * each // folds), LOW),
        cost_estimate=pl.CostEstimate(
            flops=2 * rows * depth * count * each,
            transcendentals=0,
            bytes_accessed=2 * (rows * depth + (depth + rows) * count * each),
        ),
        name="product",
    )(left, *rights)


def pair_product(places, tile, first, first_weight, second, second_weight):
    rows, depth = first.shape
    columns = first_weight.shape[0]
    count = len(places)
    part = 512 if count == 1 else 256
    at = jnp.stack(places)

    def kernel(at_ref, first_ref, second_ref, first_w_ref, second_w_ref, *out_refs):
        for k, out_ref in enumerate(out_refs):
            here = (
                slice(None)
                if count == 1
                else pl.ds(pl.multiple_of(at_ref[k] * tile, tile), tile)
            )
            out_ref[...] = (
                dot_lanes(first_ref[here, :], first_w_ref[...])
                + dot_lanes(second_ref[here, :], second_w_ref[...])
            ).astype(LOW)

    held = (
        pl.BlockSpec((tile, depth), lambda j, at_ref: (at_ref[0], 0))
        if count == 1
        else pl.BlockSpec((rows, depth), lambda j, at_ref: (0, 0))
    )
    weight_block = pl.BlockSpec((part, depth), lambda j, at_ref: (j, 0))
    return pl.pallas_call(
        kernel,
        grid_spec=pltpu.PrefetchScalarGridSpec(
            num_scalar_prefetch=1,
            grid=(columns // part,),
            in_specs=[held, held, weight_block, weight_block],
            out_specs=[pl.BlockSpec((tile, part), lambda j, at_ref: (0, j))] * count,
        ),
        out_shape=[jax.ShapeDtypeStruct((tile, columns), LOW)] * count,
        cost_estimate=pl.CostEstimate(
            flops=4 * count * tile * depth * columns, transcendentals=0, bytes_accessed=20 << 20
        ),
        name="pair_product",
    )(at, first, second, first_weight, second_weight)


def projection_back(places, d_projected, weight_rows, gathered):
    columns, width = weight_rows.shape
    tile = gathered.shape[1]
    count = len(places)
    at = jnp.stack(places)

    def kernel(at_ref, d_ref, weight_ref, tokens_ref, *out_refs):
        step = pl.program_id(0)
        grads = d_ref[...].astype(jnp.float32).T.astype(LOW)
        made = jnp.dot(grads, weight_ref[...], preferred_element_type=jnp.float32).astype(LOW)
        values = tokens_ref[0].astype(jnp.float32)
        row_scale = lax.rsqrt(jnp.mean(values * values, axis=-1, keepdims=True) + EPS)
        added = jnp.sum(made.astype(jnp.float32) * values * row_scale, axis=0, keepdims=True)
        gain_ref = out_refs[count]
        gain_ref[...] = jnp.where(step == 0, added, gain_ref[...] + added)
        for k in range(count):

            @pl.when(step == k)
            def _():
                out_refs[k][...] = made

    return pl.pallas_call(
        kernel,
        grid_spec=pltpu.PrefetchScalarGridSpec(
            num_scalar_prefetch=1,
            grid=(count,),
            in_specs=[
                pl.BlockSpec((columns, tile), lambda i, at_ref: (0, at_ref[i])),
                pl.BlockSpec((columns, width), lambda i, at_ref: (0, 0)),
                pl.BlockSpec((1, tile, width), lambda i, at_ref: (at_ref[i], 0, 0)),
            ],
            out_specs=[pl.BlockSpec((tile, width), lambda i, at_ref: (0, 0))] * count
            + [pl.BlockSpec((1, width), lambda i, at_ref: (0, 0))],
        ),
        out_shape=[jax.ShapeDtypeStruct((tile, width), LOW)] * count
        + [jax.ShapeDtypeStruct((1, width), jnp.float32)],
        cost_estimate=pl.CostEstimate(
            flops=2 * count * tile * columns * width, transcendentals=0, bytes_accessed=8 << 20
        ),
        name="projection_back",
    )(at, d_projected, weight_rows, gathered)


def norm_back(values, gain_vec, base, blocks):
    rows, width = values.shape
    part = 64
    count = len(blocks)

    def kernel(values_ref, gain_ref, base_ref, *refs):
        wide_ref, low_ref, sum_ref = refs[count:]
        step = pl.program_id(0)
        upstream = sum(ref[...].astype(jnp.float32) for ref in refs[:count])
        held = values_ref[...].astype(jnp.float32)
        row_scale = lax.rsqrt(jnp.mean(held * held, axis=-1, keepdims=True) + EPS)
        scaled = held * row_scale
        added = jnp.sum(upstream * scaled, axis=0, keepdims=True)
        sum_ref[...] = jnp.where(step == 0, added, sum_ref[...] + added)
        weighted = upstream * gain_ref[...].astype(jnp.float32)
        inner = jnp.mean(weighted * scaled, axis=-1, keepdims=True)
        result = base_ref[...].astype(jnp.float32) + row_scale * (weighted - scaled * inner)
        wide_ref[...] = result
        low_ref[...] = result.astype(LOW)

    tile_block = pl.BlockSpec((part, width), lambda i: (i, 0))
    line = pl.BlockSpec((1, width), lambda i: (0, 0))
    return pl.pallas_call(
        kernel,
        grid=(rows // part,),
        in_specs=[tile_block, line, tile_block] + [tile_block] * count,
        out_specs=[tile_block, tile_block, line],
        out_shape=[
            jax.ShapeDtypeStruct((rows, width), jnp.float32),
            jax.ShapeDtypeStruct((rows, width), LOW),
            jax.ShapeDtypeStruct((1, width), jnp.float32),
        ],
        cost_estimate=pl.CostEstimate(
            flops=16 * rows * width, transcendentals=rows, bytes_accessed=10 << 20
        ),
        name="norm_back",
    )(values, gain_vec.reshape(1, -1), base, *blocks)


def exchange(make_blocks, axis):
    n = lax.axis_size(axis)
    me = lax.axis_index(axis)
    places = [(me + hop) % n for hop in range(1, n)] + [me]
    made = list(make_blocks(places[:1]))
    moved = []
    for hop in range(1, n):
        if hop == 2:
            made += make_blocks(places[1:])
        pairs = [(i, (i + hop) % n) for i in range(n)]
        moved.append(lax.ppermute(made[hop - 1], axis, pairs))
    return moved + made[n - 1 :]


def place_blocks(halves, axis):
    (first, first_offsets), (second, second_offsets) = halves
    some, rows, half = first[0].shape
    parts = 2 * some

    def kernel(at_ref, *refs):
        out_ref = refs[4]
        k = pl.program_id(0)
        for side, offsets in enumerate((first_offsets, second_offsets)):
            columns = slice(side * half, (side + 1) * half)
            late = functools.reduce(
                jnp.logical_or, [k == offset for offset in offsets[some:]]
            )
            early_ref, late_ref = refs[2 * side : 2 * side + 2]
            out_ref[:, columns] = jnp.where(late, late_ref[0], early_ref[0]).astype(jnp.float32)

    def entry(offsets):
        def index(k, at_ref):
            found = 0
            for at, offset in enumerate(offsets):
                found = jnp.where(k == offset, at, found)
            return (found, 0, 0)

        return pl.BlockSpec((1, rows, half), index)

    specs = []
    for offsets in (first_offsets, second_offsets):
        specs += [entry(offsets[:some]), entry(offsets[some:])]
    return pl.pallas_call(
        kernel,
        grid_spec=pltpu.PrefetchScalarGridSpec(
            num_scalar_prefetch=1,
            grid=(parts,),
            in_specs=specs,
            out_specs=pl.BlockSpec((rows, 2 * half), lambda k, at_ref: (at_ref[0] ^ k, 0)),
        ),
        out_shape=jax.ShapeDtypeStruct((parts * rows, 2 * half), jnp.float32),
        cost_estimate=pl.CostEstimate(
            flops=0, transcendentals=0, bytes_accessed=12 * parts * rows * half
        ),
        name="place_blocks",
    )(lax.axis_index(axis).reshape(1), *first, *second)


def unpack_attention(shared, q_columns, k_columns, folds):
    rows, columns = shared.shape
    block = rows // folds
    kv_heads = k_columns // HD
    wide = q_columns // kv_heads
    packed = wide + 2 * HD
    end = kv_heads * packed

    def kernel(shared_ref, query_ref, key_ref, value_ref, output_ref):
        for j in range(kv_heads):
            start = j * packed
            query_ref[:, j * wide : (j + 1) * wide] = shared_ref[
                :, start : start + wide
            ].astype(jnp.float32)
            for at, ref in ((start + wide, key_ref), (start + wide + HD, value_ref)):
                ref[:, j * HD : (j + 1) * HD] = shared_ref[:, at : at + HD].astype(jnp.float32)
        output_ref[...] = shared_ref[:, end:].astype(jnp.float32)

    narrow = pl.BlockSpec((block, k_columns), lambda p: (p, 0))
    return pl.pallas_call(
        kernel,
        grid=(folds,),
        in_specs=[pl.BlockSpec((block, columns), lambda p: (p, 0))],
        out_specs=[
            pl.BlockSpec((block, q_columns), lambda p: (p, 0)),
            narrow,
            narrow,
            pl.BlockSpec((block, columns - end), lambda p: (0, p)),
        ],
        out_shape=[
            jax.ShapeDtypeStruct((rows, q_columns), jnp.float32),
            jax.ShapeDtypeStruct((rows, k_columns), jnp.float32),
            jax.ShapeDtypeStruct((rows, k_columns), jnp.float32),
            jax.ShapeDtypeStruct((block, (columns - end) * folds), jnp.float32),
        ],
        cost_estimate=pl.CostEstimate(
            flops=0, transcendentals=0, bytes_accessed=6 * rows * columns
        ),
        name="unpack_attention",
    )(shared)


def add_all(blocks):
    return sum(block.astype(jnp.float32) for block in blocks)


def row_major(array):
    return with_layout_constraint(array, Layout(major_to_minor=tuple(range(array.ndim))))


def split_columns(array, parts):
    if parts == 1:
        return array
    rows, columns = array.shape[0], array.shape[1] // parts
    return array.reshape(rows, parts, columns).swapaxes(0, 1).reshape(parts * rows, columns)


def join_columns(array, parts):
    if parts == 1:
        return array
    rows, columns = array.shape[0] // parts, array.shape[1]
    return array.reshape(parts, rows, columns).swapaxes(0, 1).reshape(rows, parts * columns)


def block(
    tokens,
    cotangent,
    norm1_gain,
    w_query,
    w_key,
    w_value,
    w_output,
    norm2_gain,
    w_gate,
    w_up,
    w_down,
):
    n_dp = lax.axis_size(DP)
    own_rows, width = tokens.shape
    depth = w_output.shape[0] // n_dp
    q_columns, k_columns = w_query.shape[1], w_key.shape[1]
    kv_heads = k_columns // HD
    group = q_columns // k_columns
    ff_columns = w_gate.shape[1]
    ff_folds = width // w_down.shape[0]
    folds = width // w_output.shape[0]
    nothing = scatter_sum(tokens[:, :128] * 0, DP)[0, 0]
    gathered = lax.all_gather(tokens, TP, axis=0)
    own_part = lax.dynamic_slice_in_dim(w_output, lax.axis_index(DP) * depth, depth, 0)
    output_part = lax.all_gather(own_part, TP, axis=0)
    all_output = cube_gather(output_part, DP)
    cos_table, sin_table = rope_tables(SEQLEN, HD)
    cos_rows, sin_rows = cos_table.T, sin_table.T
    pieces = []
    for j in range(kv_heads):
        pieces.append(w_query[:, j * group * HD : (j + 1) * group * HD].T)
        pieces.append(w_key[:, j * HD : (j + 1) * HD].T)
        pieces.append(w_value[:, j * HD : (j + 1) * HD].T)
    weight_rows = jnp.concatenate(pieces, axis=0)
    normed1, projected = norm_project(
        gathered, norm1_gain, weight_rows, cos_rows, sin_rows, group
    )
    heads_out, heads_rows, totals = attend(projected, group)
    all_heads = lax.all_gather(heads_out, TP, axis=0)
    all_cot = gather_rows(cotangent, TP)
    hidden_state, normed2, normed2_rows = project_and_norm(
        all_heads, all_output, gathered, norm2_gain.astype(jnp.float32) + nothing.astype(jnp.float32)
    )
    activated, active_rows, smooth, slope = gated_up(normed2, w_gate, w_up)
    mlp_part = product(activated, [w_down], 1)
    half_width = width // 2

    def part_of(columns):
        return lambda places: [
            lax.dynamic_slice(mlp_part, (place * own_rows, columns), (own_rows, half_width))
            for place in places
        ]

    first_half = exchange(part_of(0), TP)
    second_half = exchange(part_of(half_width), TP)
    output = (
        hidden_state
        + jnp.concatenate([add_all(first_half), add_all(second_half)], axis=1)
    ).astype(LOW)
    d_gate, d_up = gated_back(all_cot, w_down, smooth, slope)
    grad_down = product(active_rows, [all_cot], ff_folds)
    part_down = scatter_sum(grad_down, DP)
    dn2_blocks = exchange(
        lambda places: pair_product(places, own_rows, d_gate, w_gate, d_up, w_up), TP
    )
    gate_up_grads = product(normed2_rows, [d_gate, d_up], 1)
    part_gate_up = scatter_sum(gate_up_grads, DP)
    d_state, state_low, gain_two = norm_back(hidden_state, norm2_gain, cotangent, dn2_blocks)
    d_state_low = gather_rows(state_low, TP)
    gain_two_sum = cube_sum(gain_two[0], (DP, TP))
    d_heads_rows = contract_cols(w_output, d_state_low).astype(LOW)
    d_projected = attend_back(projected, d_heads_rows, totals, cos_rows, sin_rows)
    gains = []

    def dn1_blocks_of(places):
        *made, gain = projection_back(places, d_projected, weight_rows, gathered)
        gains.append(gain)
        return made

    dn1_blocks = exchange(dn1_blocks_of, TP)
    gain_one_sum = cube_sum(sum(gains)[0], (DP, TP))
    grad_qkv = lax.dot_general(
        normed1,
        d_projected,
        (((0,), (1,)), ((), ())),
        preferred_element_type=jnp.float32,
    ).astype(LOW)
    grad_output = jnp.dot(heads_rows, d_state_low, preferred_element_type=jnp.float32).astype(LOW)
    low_attn = row_major(
        jnp.concatenate([grad_qkv, split_columns(grad_output, folds)], axis=1)
    )
    part_attn = scatter_sum(low_attn, DP)
    down_halves = cube_gather(part_down, DP, join=False)
    full_down = join_columns(place_blocks(down_halves, DP), ff_folds)
    shared_ff = row_major(gather_rows(part_gate_up, DP))
    shared_attn = row_major(gather_rows(part_attn, DP))
    _, input_grad, _ = norm_back(tokens, norm1_gain, d_state, dn1_blocks)
    full_gate = shared_ff[:, :ff_columns].astype(jnp.float32)
    full_up = shared_ff[:, ff_columns:].astype(jnp.float32)
    full_query, full_key, full_value, full_output = unpack_attention(
        shared_attn, q_columns, k_columns, folds
    )
    return (
        output,
        input_grad,
        gain_one_sum,
        full_query,
        full_key,
        full_value,
        full_output,
        gain_two_sum,
        full_gate,
        full_up,
        full_down,
    )


ROWS, COLUMNS, HIDDEN = P((DP, TP), None), P(None, TP), P(TP, None)


def solution(mesh):
    return jax.shard_map(
        block,
        mesh=mesh,
        in_specs=(ROWS, ROWS, P(), COLUMNS, COLUMNS, COLUMNS, HIDDEN, P(), COLUMNS, COLUMNS, HIDDEN),
        out_specs=(ROWS, ROWS, P(), COLUMNS, COLUMNS, COLUMNS, HIDDEN, P(), COLUMNS, COLUMNS, HIDDEN),
        check_vma=False,
    )
```

```python
import functools

import jax
import jax.numpy as jnp
from jax import lax
from jax.experimental import pallas as pl
from jax.experimental.pallas import tpu as pltpu
from jax.experimental.layout import Layout, with_layout_constraint
from jax.sharding import PartitionSpec as P


LOW = jnp.bfloat16
DP, TP = "dp", "tensor"

HD = 64
SEQLEN = 512


EPS = 1e-05
ROPE_BASE = 500000.0
MASKED = -1e30


def rope_tables(length, columns):
    half_width = columns // 2
    frequency = ROPE_BASE ** (-(jnp.arange(half_width, dtype=jnp.float32) * 2.0 / columns))
    angles = jnp.arange(length, dtype=jnp.float32)[:, None] * frequency[None, :]
    return (jnp.cos(angles), jnp.sin(angles))


def contract_cols(left_side, right_side):
    return lax.dot_general(
        left_side, right_side, (((1,), (1,)), ((), ())), preferred_element_type=jnp.float32
    )


def gather_rows(block, axis):
    return lax.all_gather(block, axis, axis=0, tiled=True)


def scatter_sum(partial, axis):
    return lax.psum_scatter(partial, axis, scatter_dimension=0, tiled=True)


def cube_gather(blocks, axis, join=True):
    n = lax.axis_size(axis)
    bits = [1 << b for b in range(n.bit_length() - 1)]
    half = blocks.shape[-1] // 2
    halves = []
    for part, order in (
        (blocks[..., :half], bits[1:] + bits[:1]),
        (blocks[..., half:], bits[:0:-1] + bits[:1]),
    ):
        held, offsets = part[None], [0]
        for bit in order:
            moved = lax.ppermute(held, axis, [(i, i ^ bit) for i in range(n)])
            offsets = offsets + [o ^ bit for o in offsets]
            if join or bit != order[-1]:
                held = jnp.concatenate([held, moved], axis=0)
        halves.append((held if join else (held, moved), tuple(offsets)))
    return halves


def cube_sum(vector, axes):
    for axis in axes:
        n = lax.axis_size(axis)
        bit = 1
        while bit < n:
            vector = vector + lax.ppermute(vector, axis, [(i, i ^ bit) for i in range(n)])
            bit *= 2
    return vector


def rotate_rows(values, cos_rows, sin_rows):
    half = HD // 2
    heads = []
    for h in range(values.shape[0] // HD):
        upper = values[h * HD : h * HD + half]
        lower = values[h * HD + half : (h + 1) * HD]
        heads.append(upper * cos_rows - lower * sin_rows)
        heads.append(lower * cos_rows + upper * sin_rows)
    return jnp.concatenate(heads, axis=0)


def dot_lanes(left_side, right_side):
    return lax.dot_general(
        left_side, right_side, (((1,), (1,)), ((), ())), preferred_element_type=jnp.float32
    )


def norm_project(gathered, gain_vec, weight_rows, cos_rows, sin_rows, group):
    blocks, tile, width = gathered.shape
    rows = blocks * tile
    columns = weight_rows.shape[0]
    packed = (group + 2) * HD

    def kernel(tokens_ref, gain_ref, weight_ref, cos_ref, sin_ref, normed_ref, out_ref):
        values = tokens_ref[0].astype(jnp.float32)
        row_scale = lax.rsqrt(jnp.mean(values * values, axis=-1, keepdims=True) + EPS)
        normed = (values * row_scale * gain_ref[...].astype(jnp.float32)).astype(LOW)
        normed_ref[...] = normed
        projected = dot_lanes(weight_ref[...], normed)
        for start in range(0, columns, packed):
            turned = start + packed - HD
            out_ref[start:turned] = rotate_rows(
                projected[start:turned], cos_ref[...], sin_ref[...]
            ).astype(LOW)
            out_ref[turned : turned + HD] = projected[turned : turned + HD].astype(LOW)

    half = HD // 2
    return pl.pallas_call(
        kernel,
        grid=(blocks,),
        in_specs=[
            pl.BlockSpec((1, tile, width), lambda i: (i, 0, 0)),
            pl.BlockSpec((1, width), lambda i: (0, 0)),
            pl.BlockSpec((columns, width), lambda i: (0, 0)),
            pl.BlockSpec((half, tile), lambda i: (0, i % (SEQLEN // tile))),
            pl.BlockSpec((half, tile), lambda i: (0, i % (SEQLEN // tile))),
        ],
        out_specs=[
            pl.BlockSpec((tile, width), lambda i: (i, 0)),
            pl.BlockSpec((columns, tile), lambda i: (0, i)),
        ],
        out_shape=[
            jax.ShapeDtypeStruct((rows, width), LOW),
            jax.ShapeDtypeStruct((columns, rows), LOW),
        ],
        cost_estimate=pl.CostEstimate(
            flops=2 * rows * width * columns, transcendentals=rows, bytes_accessed=12 << 20
        ),
        name="norm_project",
    )(gathered, gain_vec.reshape(1, -1), weight_rows, cos_rows, sin_rows)


def key_tiles(step, tile):
    return [(t * tile, t == step) for t in range(step + 1)]


def causal_tile(tile):
    key_at = lax.broadcasted_iota(jnp.int32, (tile, tile), 0)
    query_at = lax.broadcasted_iota(jnp.int32, (tile, tile), 1)
    return key_at <= query_at


def attend(projected, group):
    columns, rows = projected.shape
    packed = (group + 2) * HD
    kv_heads = columns // packed
    wide = group * HD
    tile = 256
    score_scale = HD ** (-0.5)

    def kernel(packed_ref, heads_ref, heads_t_ref, total_ref):
        keys = packed_ref[wide : wide + HD].astype(jnp.float32).T.astype(LOW)
        visible = causal_tile(tile)
        for step in range(SEQLEN // tile):
            here = slice(step * tile, (step + 1) * tile)
            for h in range(group):
                query = packed_ref[h * HD : (h + 1) * HD, here]
                parts = []
                for start, masked in key_tiles(step, tile):
                    part = jnp.dot(
                        keys[start : start + tile], query, preferred_element_type=jnp.float32
                    )
                    parts.append(jnp.where(visible, part, MASKED) if masked else part)
                top = functools.reduce(
                    jnp.maximum, [jnp.max(part, axis=0, keepdims=True) for part in parts]
                )
                parts = [jnp.exp((part - top) * score_scale) for part in parts]
                total = sum(jnp.sum(part, axis=0, keepdims=True) for part in parts)
                inverse = 1.0 / total
                mixed = sum(
                    jnp.dot(
                        packed_ref[wide + HD : packed, start : start + tile],
                        (part * inverse).astype(LOW),
                        preferred_element_type=jnp.float32,
                    )
                    for part, (start, _) in zip(parts, key_tiles(step, tile))
                )
                heads_t_ref[h * HD : (h + 1) * HD, here] = mixed.astype(LOW)
                total_ref[0, h : h + 1, here] = top * score_scale + jnp.log(total)
        heads_ref[...] = heads_t_ref[...].astype(jnp.float32).T.astype(LOW)

    return pl.pallas_call(
        kernel,
        grid=(rows // SEQLEN, kv_heads),
        in_specs=[pl.BlockSpec((packed, SEQLEN), lambda s, j: (j, s))],
        out_specs=[
            pl.BlockSpec((SEQLEN, wide), lambda s, j: (s, j)),
            pl.BlockSpec((wide, SEQLEN), lambda s, j: (j, s)),
            pl.BlockSpec((1, group, SEQLEN), lambda s, j: (j, 0, s)),
        ],
        out_shape=[
            jax.ShapeDtypeStruct((rows, kv_heads * wide), LOW),
            jax.ShapeDtypeStruct((kv_heads * wide, rows), LOW),
            jax.ShapeDtypeStruct((kv_heads, group, rows), jnp.float32),
        ],
        cost_estimate=pl.CostEstimate(
            flops=4 * rows * SEQLEN * kv_heads * wide,
            transcendentals=rows * SEQLEN * kv_heads * group,
            bytes_accessed=4 << 20,
        ),
        name="attend",
    )(projected)


def attend_back(projected, d_heads, totals, cos_rows, sin_rows):
    columns, rows = projected.shape
    kv_heads, group, _ = totals.shape
    packed = (group + 2) * HD
    wide = group * HD
    tile = 256
    score_scale = HD ** (-0.5)

    def kernel(
        packed_ref, d_heads_ref, total_ref, cos_ref, sin_ref, out_ref, key_sum, value_sum
    ):
        keys = packed_ref[wide : wide + HD].astype(jnp.float32).T.astype(LOW)
        values = packed_ref[wide + HD : packed].astype(jnp.float32).T.astype(LOW)
        visible = causal_tile(tile)
        key_sum[...] = jnp.zeros_like(key_sum)
        value_sum[...] = jnp.zeros_like(value_sum)
        for step in range(SEQLEN // tile):
            here = slice(step * tile, (step + 1) * tile)
            for h in range(group):
                query = packed_ref[h * HD : (h + 1) * HD, here]
                d_head = d_heads_ref[h * HD : (h + 1) * HD, here]
                log_total = total_ref[0, h : h + 1, here]
                probs, d_probs = [], []
                for start, masked in key_tiles(step, tile):
                    span = slice(start, start + tile)
                    part = jnp.dot(keys[span], query, preferred_element_type=jnp.float32)
                    part = jnp.exp(part * score_scale - log_total)
                    if masked:
                        part = jnp.where(visible, part, 0.0)
                    probs.append(part)
                    value_sum[:, span] += dot_lanes(d_head, part.astype(LOW))
                    d_probs.append(
                        jnp.dot(values[span], d_head, preferred_element_type=jnp.float32)
                    )
                row_sum = sum(
                    jnp.sum(part * d_part, axis=0, keepdims=True)
                    for part, d_part in zip(probs, d_probs)
                )
                d_query = jnp.zeros((HD, tile), jnp.float32)
                for (start, _), part, d_part in zip(key_tiles(step, tile), probs, d_probs):
                    span = slice(start, start + tile)
                    d_scores = (part * (d_part - row_sum)).astype(LOW)
                    d_query += jnp.dot(
                        packed_ref[wide : wide + HD, span],
                        d_scores,
                        preferred_element_type=jnp.float32,
                    )
                    key_sum[:, span] += dot_lanes(query, d_scores)
                out_ref[h * HD : (h + 1) * HD, here] = rotate_rows(
                    d_query * score_scale, cos_ref[:, here], -sin_ref[:, here]
                ).astype(LOW)
        out_ref[wide : wide + HD] = rotate_rows(
            key_sum[...] * score_scale, cos_ref[...], -sin_ref[...]
        ).astype(LOW)
        out_ref[wide + HD : packed] = value_sum[...].astype(LOW)

    half = HD // 2
    return pl.pallas_call(
        kernel,
        grid=(rows // SEQLEN, kv_heads),
        in_specs=[
            pl.BlockSpec((packed, SEQLEN), lambda s, j: (j, s)),
            pl.BlockSpec((wide, SEQLEN), lambda s, j: (j, s)),
            pl.BlockSpec((1, group, SEQLEN), lambda s, j: (j, 0, s)),
            pl.BlockSpec((half, SEQLEN), lambda s, j: (0, 0)),
            pl.BlockSpec((half, SEQLEN), lambda s, j: (0, 0)),
        ],
        out_specs=pl.BlockSpec((packed, SEQLEN), lambda s, j: (j, s)),
        out_shape=jax.ShapeDtypeStruct((columns, rows), LOW),
        scratch_shapes=[
            pltpu.VMEM((HD, SEQLEN), jnp.float32),
            pltpu.VMEM((HD, SEQLEN), jnp.float32),
        ],
        cost_estimate=pl.CostEstimate(
            flops=10 * rows * SEQLEN * kv_heads * wide,
            transcendentals=rows * SEQLEN * kv_heads * group,
            bytes_accessed=6 << 20,
        ),
        name="attend_back",
    )(projected, d_heads, totals, cos_rows, sin_rows)


def project_and_norm(all_heads, weights, gathered, gain_vec):
    groups, rows, group_columns = all_heads.shape
    (first, first_offsets), (second, second_offsets) = weights
    parts, _, depth, half = first.shape
    width = 2 * half
    tile = rows // groups
    places = jnp.stack([lax.axis_index(TP), lax.axis_index(DP)])

    def kernel(
        at_ref,
        heads_ref,
        first_ref,
        second_ref,
        tokens_ref,
        gain_ref,
        hidden_ref,
        normed_ref,
        turned_ref,
        weight_ref,
        wide_ref,
    ):
        step = pl.program_id(0)

        @pl.when(step == 0)
        def _():
            for side, part_ref, offsets in (
                (0, first_ref, first_offsets),
                (half, second_ref, second_offsets),
            ):


                @pl.loop(0, groups)
                def _(g, side=side, part_ref=part_ref, offsets=offsets):
                    for part in range(parts):
                        start = g * group_columns + (at_ref[1] ^ offsets[part]) * depth
                        at = pl.ds(pl.multiple_of(start, depth), depth)
                        weight_ref[at, side : side + half] = part_ref[part, g]

        for g in range(groups):
            wide_ref[:, g * group_columns : (g + 1) * group_columns] = heads_ref[g]
        hidden = tokens_ref[0].astype(jnp.float32) + jnp.dot(
            wide_ref[...], weight_ref[...], preferred_element_type=jnp.float32
        )
        row_scale = lax.rsqrt(jnp.mean(hidden * hidden, axis=-1, keepdims=True) + EPS)
        normed = hidden * row_scale * gain_ref[...].astype(jnp.float32)
        normed_ref[...] = normed.astype(LOW)
        turned_ref[...] = normed.T.astype(LOW)

        @pl.when(step == at_ref[0])
        def _():
            hidden_ref[...] = hidden

    return pl.pallas_call(
        kernel,
        grid_spec=pltpu.PrefetchScalarGridSpec(
            num_scalar_prefetch=1,
            grid=(groups,),
            in_specs=[
                pl.BlockSpec((groups, tile, group_columns), lambda i, at_ref: (0, i, 0)),
                pl.BlockSpec(first.shape, lambda i, at_ref: (0, 0, 0, 0)),
                pl.BlockSpec(second.shape, lambda i, at_ref: (0, 0, 0, 0)),
                pl.BlockSpec((1, tile, width), lambda i, at_ref: (i, 0, 0)),
                pl.BlockSpec((1, width), lambda i, at_ref: (0, 0)),
            ],
            out_specs=[
                pl.BlockSpec((tile, width), lambda i, at_ref: (0, 0)),
                pl.BlockSpec((tile, width), lambda i, at_ref: (i, 0)),
                pl.BlockSpec((width, tile), lambda i, at_ref: (0, i)),
            ],
            scratch_shapes=[
                pltpu.VMEM((groups * group_columns, width), LOW),
                pltpu.VMEM((tile, groups * group_columns), LOW),
            ],
        ),
        out_shape=[
            jax.ShapeDtypeStruct((tile, width), jnp.float32),
            jax.ShapeDtypeStruct((rows, width), LOW),
            jax.ShapeDtypeStruct((width, rows), LOW),
        ],
        cost_estimate=pl.CostEstimate(
            flops=2 * rows * width * width, transcendentals=rows, bytes_accessed=24 << 20
        ),
        name="project_and_norm",
    )(places, all_heads, first, second, gathered, gain_vec.reshape(1, -1))


def gated_up(normed, w_gate, w_up):
    rows, width = normed.shape
    columns = w_gate.shape[1]
    tile = 256

    def kernel(normed_ref, gate_w_ref, up_w_ref, active_ref, turned_ref, smooth_ref, slope_ref):
        gate = jnp.dot(normed_ref[...], gate_w_ref[...], preferred_element_type=jnp.float32)
        up = jnp.dot(normed_ref[...], up_w_ref[...], preferred_element_type=jnp.float32)
        chance = jax.nn.sigmoid(gate)
        smooth = gate * chance
        active = smooth * up
        active_ref[...] = active.astype(LOW)
        turned_ref[...] = active.T.astype(LOW)
        smooth_ref[...] = smooth.astype(LOW)
        slope_ref[...] = (up * (chance * (1.0 + gate * (1.0 - chance)))).astype(LOW)

    column_block = pl.BlockSpec((rows, tile), lambda j: (0, j))
    weight_block = pl.BlockSpec((width, tile), lambda j: (0, j))
    flat = jax.ShapeDtypeStruct((rows, columns), LOW)
    return pl.pallas_call(
        kernel,
        grid=(columns // tile,),
        in_specs=[pl.BlockSpec((rows, width), lambda j: (0, 0)), weight_block, weight_block],
        out_specs=[
            column_block,
            pl.BlockSpec((tile, rows), lambda j: (j, 0)),
            column_block,
            column_block,
        ],
        out_shape=[flat, jax.ShapeDtypeStruct((columns, rows), LOW), flat, flat],
        cost_estimate=pl.CostEstimate(
            flops=4 * rows * width * columns,
            transcendentals=rows * columns,
            bytes_accessed=36 << 20,
        ),
        name="gated_up",
    )(normed, w_gate, w_up)


def gated_back(all_cot, w_down, smooth, slope):
    rows, width = all_cot.shape
    columns = w_down.shape[0]
    tile = 512

    def kernel(cot_ref, weight_ref, smooth_ref, slope_ref, out_ref):
        for start in range(0, tile, 256):
            here = slice(start, start + 256)
            d_active = dot_lanes(cot_ref[...], weight_ref[here, :])
            out_ref[0, :, here] = (d_active * slope_ref[:, here].astype(jnp.float32)).astype(LOW)
            out_ref[1, :, here] = (d_active * smooth_ref[:, here].astype(jnp.float32)).astype(LOW)

    column_block = pl.BlockSpec((rows, tile), lambda j: (0, j))
    return pl.pallas_call(
        kernel,
        grid=(columns // tile,),
        in_specs=[
            pl.BlockSpec((rows, width), lambda j: (0, 0)),
            pl.BlockSpec((tile, width), lambda j: (j, 0)),
            column_block,
            column_block,
        ],
        out_specs=pl.BlockSpec((2, rows, tile), lambda j: (0, 0, j)),
        out_shape=jax.ShapeDtypeStruct((2, rows, columns), LOW),
        cost_estimate=pl.CostEstimate(
            flops=2 * rows * width * columns, transcendentals=0, bytes_accessed=28 << 20
        ),
        name="gated_back",
    )(all_cot, w_down, smooth, slope)


def product(left, right, folds):
    rows, depth = left.shape
    right = right.reshape(-1, depth, right.shape[-1])
    count, _, each = right.shape
    tile = 512
    steps = each // tile
    per = count * steps // folds

    def kernel(left_ref, right_ref, out_ref):
        out_ref[...] = jnp.dot(
            left_ref[...], right_ref[0], preferred_element_type=jnp.float32
        ).astype(LOW)

    return pl.pallas_call(
        kernel,
        grid=(count * steps,),
        in_specs=[
            pl.BlockSpec((rows, depth), lambda j: (0, 0)),
            pl.BlockSpec((1, depth, tile), lambda j: (j // steps, 0, j % steps)),
        ],
        out_specs=pl.BlockSpec((rows, tile), lambda j: (j // per, j % per)),
        out_shape=jax.ShapeDtypeStruct((rows * folds, count * each // folds), LOW),
        cost_estimate=pl.CostEstimate(
            flops=2 * rows * depth * count * each,
            transcendentals=0,
            bytes_accessed=2 * (rows * depth + (depth + rows) * count * each),
        ),
        name="product",
    )(left, right)


def pair_product(places, tile, pair, first_weight, second_weight):
    _, rows, depth = pair.shape
    columns = first_weight.shape[0]
    count = len(places)
    part = 512 if count == 1 else 256
    at = jnp.stack(places)

    def kernel(at_ref, pair_ref, first_w_ref, second_w_ref, *out_refs):
        for k, out_ref in enumerate(out_refs):
            here = (
                slice(None)
                if count == 1
                else pl.ds(pl.multiple_of(at_ref[k] * tile, tile), tile)
            )
            out_ref[...] = (
                dot_lanes(pair_ref[0, here, :], first_w_ref[...])
                + dot_lanes(pair_ref[1, here, :], second_w_ref[...])
            ).astype(LOW)

    held = (
        pl.BlockSpec((2, tile, depth), lambda j, at_ref: (0, at_ref[0], 0))
        if count == 1
        else pl.BlockSpec((2, rows, depth), lambda j, at_ref: (0, 0, 0))
    )
    weight_block = pl.BlockSpec((part, depth), lambda j, at_ref: (j, 0))
    return pl.pallas_call(
        kernel,
        grid_spec=pltpu.PrefetchScalarGridSpec(
            num_scalar_prefetch=1,
            grid=(columns // part,),
            in_specs=[held, weight_block, weight_block],
            out_specs=[pl.BlockSpec((tile, part), lambda j, at_ref: (0, j))] * count,
        ),
        out_shape=[jax.ShapeDtypeStruct((tile, columns), LOW)] * count,
        cost_estimate=pl.CostEstimate(
            flops=4 * count * tile * depth * columns, transcendentals=0, bytes_accessed=20 << 20
        ),
        name="pair_product",
    )(at, pair, first_weight, second_weight)


def projection_back(places, d_projected, weight_rows, gathered):
    columns, width = weight_rows.shape
    tile = gathered.shape[1]
    count = len(places)
    at = jnp.stack(places)

    def kernel(at_ref, d_ref, weight_ref, tokens_ref, *out_refs):
        step = pl.program_id(0)
        grads = d_ref[...].astype(jnp.float32).T.astype(LOW)
        made = jnp.dot(grads, weight_ref[...], preferred_element_type=jnp.float32).astype(LOW)
        values = tokens_ref[0].astype(jnp.float32)
        row_scale = lax.rsqrt(jnp.mean(values * values, axis=-1, keepdims=True) + EPS)
        added = jnp.sum(made.astype(jnp.float32) * values * row_scale, axis=0, keepdims=True)
        gain_ref = out_refs[count]
        gain_ref[...] = jnp.where(step == 0, added, gain_ref[...] + added)
        for k in range(count):

            @pl.when(step == k)
            def _():
                out_refs[k][...] = made

    return pl.pallas_call(
        kernel,
        grid_spec=pltpu.PrefetchScalarGridSpec(
            num_scalar_prefetch=1,
            grid=(count,),
            in_specs=[
                pl.BlockSpec((columns, tile), lambda i, at_ref: (0, at_ref[i])),
                pl.BlockSpec((columns, width), lambda i, at_ref: (0, 0)),
                pl.BlockSpec((1, tile, width), lambda i, at_ref: (at_ref[i], 0, 0)),
            ],
            out_specs=[pl.BlockSpec((tile, width), lambda i, at_ref: (0, 0))] * count
            + [pl.BlockSpec((1, width), lambda i, at_ref: (0, 0))],
        ),
        out_shape=[jax.ShapeDtypeStruct((tile, width), LOW)] * count
        + [jax.ShapeDtypeStruct((1, width), jnp.float32)],
        cost_estimate=pl.CostEstimate(
            flops=2 * count * tile * columns * width, transcendentals=0, bytes_accessed=8 << 20
        ),
        name="projection_back",
    )(at, d_projected, weight_rows, gathered)


def norm_back(values, gain_vec, base, blocks):
    rows, width = values.shape
    part = 64
    count = len(blocks)

    def kernel(values_ref, gain_ref, base_ref, *refs):
        wide_ref, low_ref, sum_ref = refs[count:]
        step = pl.program_id(0)
        upstream = sum(ref[...].astype(jnp.float32) for ref in refs[:count])
        held = values_ref[...].astype(jnp.float32)
        row_scale = lax.rsqrt(jnp.mean(held * held, axis=-1, keepdims=True) + EPS)
        scaled = held * row_scale
        added = jnp.sum(upstream * scaled, axis=0, keepdims=True)
        sum_ref[...] = jnp.where(step == 0, added, sum_ref[...] + added)
        weighted = upstream * gain_ref[...].astype(jnp.float32)
        inner = jnp.mean(weighted * scaled, axis=-1, keepdims=True)
        result = base_ref[...].astype(jnp.float32) + row_scale * (weighted - scaled * inner)
        wide_ref[...] = result
        low_ref[...] = result.astype(LOW)

    tile_block = pl.BlockSpec((part, width), lambda i: (i, 0))
    line = pl.BlockSpec((1, width), lambda i: (0, 0))
    return pl.pallas_call(
        kernel,
        grid=(rows // part,),
        in_specs=[tile_block, line, tile_block] + [tile_block] * count,
        out_specs=[tile_block, tile_block, line],
        out_shape=[
            jax.ShapeDtypeStruct((rows, width), jnp.float32),
            jax.ShapeDtypeStruct((rows, width), LOW),
            jax.ShapeDtypeStruct((1, width), jnp.float32),
        ],
        cost_estimate=pl.CostEstimate(
            flops=16 * rows * width, transcendentals=rows, bytes_accessed=10 << 20
        ),
        name="norm_back",
    )(values, gain_vec.reshape(1, -1), base, *blocks)


def exchange(make_blocks, axis):
    n = lax.axis_size(axis)
    me = lax.axis_index(axis)
    places = [(me + hop) % n for hop in range(1, n)] + [me]
    made = list(make_blocks(places[:1]))
    moved = []
    for hop in range(1, n):
        if hop == 2:
            made += make_blocks(places[1:])
        pairs = [(i, (i + hop) % n) for i in range(n)]
        moved.append(lax.ppermute(made[hop - 1], axis, pairs))
    return moved + made[n - 1 :]


def place_blocks(halves, axis):
    (first, first_offsets), (second, second_offsets) = halves
    some, rows, half = first[0].shape
    parts = 2 * some

    def kernel(at_ref, *refs):
        out_ref = refs[4]
        k = pl.program_id(0)
        for side, offsets in enumerate((first_offsets, second_offsets)):
            columns = slice(side * half, (side + 1) * half)
            late = functools.reduce(
                jnp.logical_or, [k == offset for offset in offsets[some:]]
            )
            early_ref, late_ref = refs[2 * side : 2 * side + 2]
            out_ref[:, columns] = jnp.where(late, late_ref[0], early_ref[0]).astype(jnp.float32)

    def entry(offsets):
        def index(k, at_ref):
            found = 0
            for at, offset in enumerate(offsets):
                found = jnp.where(k == offset, at, found)
            return (found, 0, 0)

        return pl.BlockSpec((1, rows, half), index)

    specs = []
    for offsets in (first_offsets, second_offsets):
        specs += [entry(offsets[:some]), entry(offsets[some:])]
    return pl.pallas_call(
        kernel,
        grid_spec=pltpu.PrefetchScalarGridSpec(
            num_scalar_prefetch=1,
            grid=(parts,),
            in_specs=specs,
            out_specs=pl.BlockSpec((rows, 2 * half), lambda k, at_ref: (at_ref[0] ^ k, 0)),
        ),
        out_shape=jax.ShapeDtypeStruct((parts * rows, 2 * half), jnp.float32),
        cost_estimate=pl.CostEstimate(
            flops=0, transcendentals=0, bytes_accessed=12 * parts * rows * half
        ),
        name="place_blocks",
    )(lax.axis_index(axis).reshape(1), *first, *second)


def unpack_attention(shared, q_columns, k_columns, folds):
    rows, columns = shared.shape
    block = rows // folds
    kv_heads = k_columns // HD
    wide = q_columns // kv_heads
    packed = wide + 2 * HD
    end = kv_heads * packed

    def kernel(shared_ref, query_ref, key_ref, value_ref, output_ref):
        for j in range(kv_heads):
            start = j * packed
            query_ref[:, j * wide : (j + 1) * wide] = shared_ref[
                :, start : start + wide
            ].astype(jnp.float32)
            for at, ref in ((start + wide, key_ref), (start + wide + HD, value_ref)):
                ref[:, j * HD : (j + 1) * HD] = shared_ref[:, at : at + HD].astype(jnp.float32)
        output_ref[...] = shared_ref[:, end:].astype(jnp.float32)

    narrow = pl.BlockSpec((block, k_columns), lambda p: (p, 0))
    return pl.pallas_call(
        kernel,
        grid=(folds,),
        in_specs=[pl.BlockSpec((block, columns), lambda p: (p, 0))],
        out_specs=[
            pl.BlockSpec((block, q_columns), lambda p: (p, 0)),
            narrow,
            narrow,
            pl.BlockSpec((block, columns - end), lambda p: (0, p)),
        ],
        out_shape=[
            jax.ShapeDtypeStruct((rows, q_columns), jnp.float32),
            jax.ShapeDtypeStruct((rows, k_columns), jnp.float32),
            jax.ShapeDtypeStruct((rows, k_columns), jnp.float32),
            jax.ShapeDtypeStruct((block, (columns - end) * folds), jnp.float32),
        ],
        cost_estimate=pl.CostEstimate(
            flops=0, transcendentals=0, bytes_accessed=6 * rows * columns
        ),
        name="unpack_attention",
    )(shared)


def row_major(array):
    return with_layout_constraint(array, Layout(major_to_minor=tuple(range(array.ndim))))


def join_columns(array, parts):
    if parts == 1:
        return array
    rows, columns = array.shape[0] // parts, array.shape[1]
    return array.reshape(parts, rows, columns).swapaxes(0, 1).reshape(rows, parts * columns)


def block(
    tokens,
    cotangent,
    norm1_gain,
    w_query,
    w_key,
    w_value,
    w_output,
    norm2_gain,
    w_gate,
    w_up,
    w_down,
):
    n_dp = lax.axis_size(DP)
    own_rows, width = tokens.shape
    depth = w_output.shape[0] // n_dp
    q_columns, k_columns = w_query.shape[1], w_key.shape[1]
    kv_heads = k_columns // HD
    group = q_columns // k_columns
    ff_columns = w_gate.shape[1]
    ff_folds = width // w_down.shape[0]
    folds = width // w_output.shape[0]
    nothing = scatter_sum(tokens[:, :128] * 0, DP)[0, 0]
    gathered = lax.all_gather(tokens, TP, axis=0)
    own_part = lax.dynamic_slice_in_dim(w_output, lax.axis_index(DP) * depth, depth, 0)
    output_part = lax.all_gather(own_part, TP, axis=0)
    all_output = cube_gather(output_part, DP)
    cos_table, sin_table = rope_tables(SEQLEN, HD)
    cos_rows, sin_rows = cos_table.T, sin_table.T
    pieces = []
    for j in range(kv_heads):
        pieces.append(w_query[:, j * group * HD : (j + 1) * group * HD].T)
        pieces.append(w_key[:, j * HD : (j + 1) * HD].T)
        pieces.append(w_value[:, j * HD : (j + 1) * HD].T)
    weight_rows = jnp.concatenate(pieces, axis=0)
    normed1, projected = norm_project(
        gathered, norm1_gain, weight_rows, cos_rows, sin_rows, group
    )
    heads_out, heads_rows, totals = attend(projected, group)
    all_heads = lax.all_gather(heads_out, TP, axis=0)
    all_cot = gather_rows(cotangent, TP)
    hidden_state, normed2, normed2_rows = project_and_norm(
        all_heads, all_output, gathered, norm2_gain.astype(jnp.float32) + nothing.astype(jnp.float32)
    )
    activated, active_rows, smooth, slope = gated_up(normed2, w_gate, w_up)
    mlp_part = product(activated, w_down, 1)
    n_tensor = lax.axis_size(TP)
    me = lax.axis_index(TP)

    def part_of(place):
        return lax.dynamic_slice_in_dim(mlp_part, place * own_rows, own_rows, 0)

    output = hidden_state + part_of(me).astype(jnp.float32)
    for hop in list(range(1, n_tensor, 2)) + list(range(2, n_tensor, 2)):
        pairs = [(i, (i + hop) % n_tensor) for i in range(n_tensor)]
        moved = lax.ppermute(part_of((me + hop) % n_tensor), TP, pairs)
        output = output + moved.astype(jnp.float32)
    output = output.astype(LOW)
    d_pair = gated_back(all_cot, w_down, smooth, slope)
    grad_down = product(active_rows, all_cot, ff_folds)
    part_down = scatter_sum(grad_down, DP)
    dn2_blocks = exchange(lambda places: pair_product(places, own_rows, d_pair, w_gate, w_up), TP)
    gate_up_grads = product(normed2_rows, d_pair, 1)
    part_gate_up = scatter_sum(gate_up_grads, DP)
    d_state, state_low, gain_two = norm_back(hidden_state, norm2_gain, cotangent, dn2_blocks)
    d_state_low = gather_rows(state_low, TP)
    d_heads_rows = contract_cols(w_output, d_state_low).astype(LOW)
    d_projected = attend_back(projected, d_heads_rows, totals, cos_rows, sin_rows)
    gains = []

    def dn1_blocks_of(places):
        *made, gain = projection_back(places, d_projected, weight_rows, gathered)
        gains.append(gain)
        return made

    dn1_blocks = exchange(dn1_blocks_of, TP)
    gain_sums = cube_sum(jnp.concatenate([sum(gains), gain_two], axis=1)[0], (DP, TP))
    gain_one_sum, gain_two_sum = gain_sums[:width], gain_sums[width:]
    grad_qkv = lax.dot_general(
        normed1,
        d_projected,
        (((0,), (1,)), ((), ())),
        preferred_element_type=jnp.float32,
    ).astype(LOW)
    output_grads = product(heads_rows, d_state_low, folds)
    low_attn = row_major(
        jnp.concatenate([grad_qkv, output_grads], axis=1)
    )
    part_attn = scatter_sum(low_attn, DP)
    down_halves = cube_gather(part_down, DP, join=False)
    full_down = join_columns(place_blocks(down_halves, DP), ff_folds)
    shared_ff = row_major(gather_rows(part_gate_up, DP))
    shared_attn = row_major(gather_rows(part_attn, DP))
    _, input_grad, _ = norm_back(tokens, norm1_gain, d_state, dn1_blocks)
    full_gate = shared_ff[:, :ff_columns].astype(jnp.float32)
    full_up = shared_ff[:, ff_columns:].astype(jnp.float32)
    full_query, full_key, full_value, full_output = unpack_attention(
        shared_attn, q_columns, k_columns, folds
    )
    return (
        output,
        input_grad,
        gain_one_sum,
        full_query,
        full_key,
        full_value,
        full_output,
        gain_two_sum,
        full_gate,
        full_up,
        full_down,
    )


ROWS, COLUMNS, HIDDEN = P((DP, TP), None), P(None, TP), P(TP, None)


def solution(mesh):
    return jax.shard_map(
        block,
        mesh=mesh,
        in_specs=(ROWS, ROWS, P(), COLUMNS, COLUMNS, COLUMNS, HIDDEN, P(), COLUMNS, COLUMNS, HIDDEN),
        out_specs=(ROWS, ROWS, P(), COLUMNS, COLUMNS, COLUMNS, HIDDEN, P(), COLUMNS, COLUMNS, HIDDEN),
        check_vma=False,
    )
```

```python
import functools

import jax
import jax.numpy as jnp
from jax import lax
from jax.experimental import pallas as pl
from jax.experimental.pallas import tpu as pltpu
from jax.experimental.layout import Layout, with_layout_constraint
from jax.sharding import PartitionSpec as P


LOW = jnp.bfloat16
DP, TP = "dp", "tensor"

HD = 64
SEQLEN = 512


EPS = 1e-05
ROPE_BASE = 500000.0
MASKED = -1e30


def rope_tables(length, columns):
    half_width = columns // 2
    frequency = ROPE_BASE ** (-(jnp.arange(half_width, dtype=jnp.float32) * 2.0 / columns))
    angles = jnp.arange(length, dtype=jnp.float32)[:, None] * frequency[None, :]
    return (jnp.cos(angles), jnp.sin(angles))


def contract_cols(left_side, right_side):
    return lax.dot_general(
        left_side, right_side, (((1,), (1,)), ((), ())), preferred_element_type=jnp.float32
    )


def gather_rows(block, axis):
    return lax.all_gather(block, axis, axis=0, tiled=True)


def scatter_sum(partial, axis):
    return lax.psum_scatter(partial, axis, scatter_dimension=0, tiled=True)


def cube_gather(blocks, axis, join=True):
    n = lax.axis_size(axis)
    bits = [1 << b for b in range(n.bit_length() - 1)]
    half = blocks.shape[-1] // 2
    halves = []
    for part, order in (
        (blocks[..., :half], bits[1:] + bits[:1]),
        (blocks[..., half:], bits[:0:-1] + bits[:1]),
    ):
        held, offsets = part[None], [0]
        for bit in order:
            moved = lax.ppermute(held, axis, [(i, i ^ bit) for i in range(n)])
            if join or bit != order[-1]:
                held = jnp.concatenate([held, moved], axis=0)
            offsets = offsets + [o ^ bit for o in offsets]
        halves.append((held if join else (held, moved), tuple(offsets)))
    return halves


def cube_sum(vector, axes):
    for axis in axes:
        n = lax.axis_size(axis)
        bit = 1
        while bit < n:
            vector = vector + lax.ppermute(vector, axis, [(i, i ^ bit) for i in range(n)])
            bit *= 2
    return vector


def rotate_rows(values, cos_rows, sin_rows):
    half = HD // 2
    heads = []
    for h in range(values.shape[0] // HD):
        upper = values[h * HD : h * HD + half]
        lower = values[h * HD + half : (h + 1) * HD]
        heads.append(upper * cos_rows - lower * sin_rows)
        heads.append(lower * cos_rows + upper * sin_rows)
    return jnp.concatenate(heads, axis=0)


def dot_lanes(left_side, right_side):
    return lax.dot_general(
        left_side, right_side, (((1,), (1,)), ((), ())), preferred_element_type=jnp.float32
    )


def norm_project(gathered, gain_vec, weight_rows, cos_rows, sin_rows, group):
    blocks, tile, width = gathered.shape
    rows = blocks * tile
    columns = weight_rows.shape[0]
    packed = (group + 2) * HD

    def kernel(tokens_ref, gain_ref, weight_ref, cos_ref, sin_ref, normed_ref, out_ref):
        values = tokens_ref[0].astype(jnp.float32)
        row_scale = lax.rsqrt(jnp.mean(values * values, axis=-1, keepdims=True) + EPS)
        normed = (values * row_scale * gain_ref[...].astype(jnp.float32)).astype(LOW)
        normed_ref[...] = normed
        projected = dot_lanes(weight_ref[...], normed)
        for start in range(0, columns, packed):
            turned = start + packed - HD
            out_ref[start:turned] = rotate_rows(
                projected[start:turned], cos_ref[...], sin_ref[...]
            ).astype(LOW)
            out_ref[turned : turned + HD] = projected[turned : turned + HD].astype(LOW)

    half = HD // 2
    return pl.pallas_call(
        kernel,
        grid=(blocks,),
        in_specs=[
            pl.BlockSpec((1, tile, width), lambda i: (i, 0, 0)),
            pl.BlockSpec((1, width), lambda i: (0, 0)),
            pl.BlockSpec((columns, width), lambda i: (0, 0)),
            pl.BlockSpec((half, tile), lambda i: (0, i % (SEQLEN // tile))),
            pl.BlockSpec((half, tile), lambda i: (0, i % (SEQLEN // tile))),
        ],
        out_specs=[
            pl.BlockSpec((tile, width), lambda i: (i, 0)),
            pl.BlockSpec((columns, tile), lambda i: (0, i)),
        ],
        out_shape=[
            jax.ShapeDtypeStruct((rows, width), LOW),
            jax.ShapeDtypeStruct((columns, rows), LOW),
        ],
        cost_estimate=pl.CostEstimate(
            flops=2 * rows * width * columns, transcendentals=rows, bytes_accessed=12 << 20
        ),
        name="norm_project",
    )(gathered, gain_vec.reshape(1, -1), weight_rows, cos_rows, sin_rows)


def key_tiles(step, tile):
    return [(t * tile, t == step) for t in range(step + 1)]


def causal_tile(tile):
    key_at = lax.broadcasted_iota(jnp.int32, (tile, tile), 0)
    query_at = lax.broadcasted_iota(jnp.int32, (tile, tile), 1)
    return key_at <= query_at


def attend(projected, group):
    columns, rows = projected.shape
    packed = (group + 2) * HD
    kv_heads = columns // packed
    wide = group * HD
    tile = 256
    score_scale = HD ** (-0.5)

    def kernel(packed_ref, heads_ref, heads_t_ref, total_ref):
        keys = packed_ref[wide : wide + HD].astype(jnp.float32).T.astype(LOW)
        visible = causal_tile(tile)
        for step in range(SEQLEN // tile):
            here = slice(step * tile, (step + 1) * tile)
            for h in range(group):
                query = packed_ref[h * HD : (h + 1) * HD, here]
                parts = []
                for start, masked in key_tiles(step, tile):
                    part = jnp.dot(
                        keys[start : start + tile], query, preferred_element_type=jnp.float32
                    )
                    parts.append(jnp.where(visible, part, MASKED) if masked else part)
                top = functools.reduce(
                    jnp.maximum, [jnp.max(part, axis=0, keepdims=True) for part in parts]
                )
                parts = [jnp.exp((part - top) * score_scale) for part in parts]
                total = sum(jnp.sum(part, axis=0, keepdims=True) for part in parts)
                inverse = 1.0 / total
                mixed = sum(
                    jnp.dot(
                        packed_ref[wide + HD : packed, start : start + tile],
                        (part * inverse).astype(LOW),
                        preferred_element_type=jnp.float32,
                    )
                    for part, (start, _) in zip(parts, key_tiles(step, tile))
                )
                heads_t_ref[h * HD : (h + 1) * HD, here] = mixed.astype(LOW)
                total_ref[0, h : h + 1, here] = top * score_scale + jnp.log(total)
        heads_ref[...] = heads_t_ref[...].astype(jnp.float32).T.astype(LOW)

    return pl.pallas_call(
        kernel,
        grid=(rows // SEQLEN, kv_heads),
        in_specs=[pl.BlockSpec((packed, SEQLEN), lambda s, j: (j, s))],
        out_specs=[
            pl.BlockSpec((SEQLEN, wide), lambda s, j: (s, j)),
            pl.BlockSpec((wide, SEQLEN), lambda s, j: (j, s)),
            pl.BlockSpec((1, group, SEQLEN), lambda s, j: (j, 0, s)),
        ],
        out_shape=[
            jax.ShapeDtypeStruct((rows, kv_heads * wide), LOW),
            jax.ShapeDtypeStruct((kv_heads * wide, rows), LOW),
            jax.ShapeDtypeStruct((kv_heads, group, rows), jnp.float32),
        ],
        cost_estimate=pl.CostEstimate(
            flops=4 * rows * SEQLEN * kv_heads * wide,
            transcendentals=rows * SEQLEN * kv_heads * group,
            bytes_accessed=4 << 20,
        ),
        name="attend",
    )(projected)


def attend_back(projected, d_heads, totals, cos_rows, sin_rows):
    columns, rows = projected.shape
    kv_heads, group, _ = totals.shape
    packed = (group + 2) * HD
    wide = group * HD
    tile = 256
    score_scale = HD ** (-0.5)

    def kernel(
        packed_ref, d_heads_ref, total_ref, cos_ref, sin_ref, out_ref, key_sum, value_sum
    ):
        keys = packed_ref[wide : wide + HD].astype(jnp.float32).T.astype(LOW)
        values = packed_ref[wide + HD : packed].astype(jnp.float32).T.astype(LOW)
        visible = causal_tile(tile)
        key_sum[...] = jnp.zeros_like(key_sum)
        value_sum[...] = jnp.zeros_like(value_sum)
        for step in range(SEQLEN // tile):
            here = slice(step * tile, (step + 1) * tile)
            for h in range(group):
                query = packed_ref[h * HD : (h + 1) * HD, here]
                d_head = d_heads_ref[h * HD : (h + 1) * HD, here]
                log_total = total_ref[0, h : h + 1, here]
                probs, d_probs = [], []
                for start, masked in key_tiles(step, tile):
                    span = slice(start, start + tile)
                    part = jnp.dot(keys[span], query, preferred_element_type=jnp.float32)
                    part = jnp.exp(part * score_scale - log_total)
                    if masked:
                        part = jnp.where(visible, part, 0.0)
                    probs.append(part)
                    value_sum[:, span] += dot_lanes(d_head, part.astype(LOW))
                    d_probs.append(
                        jnp.dot(values[span], d_head, preferred_element_type=jnp.float32)
                    )
                row_sum = sum(
                    jnp.sum(part * d_part, axis=0, keepdims=True)
                    for part, d_part in zip(probs, d_probs)
                )
                d_query = jnp.zeros((HD, tile), jnp.float32)
                for (start, _), part, d_part in zip(key_tiles(step, tile), probs, d_probs):
                    span = slice(start, start + tile)
                    d_scores = (part * (d_part - row_sum)).astype(LOW)
                    d_query += jnp.dot(
                        packed_ref[wide : wide + HD, span],
                        d_scores,
                        preferred_element_type=jnp.float32,
                    )
                    key_sum[:, span] += dot_lanes(query, d_scores)
                out_ref[h * HD : (h + 1) * HD, here] = rotate_rows(
                    d_query * score_scale, cos_ref[:, here], -sin_ref[:, here]
                ).astype(LOW)
        out_ref[wide : wide + HD] = rotate_rows(
            key_sum[...] * score_scale, cos_ref[...], -sin_ref[...]
        ).astype(LOW)
        out_ref[wide + HD : packed] = value_sum[...].astype(LOW)

    half = HD // 2
    return pl.pallas_call(
        kernel,
        grid=(rows // SEQLEN, kv_heads),
        in_specs=[
            pl.BlockSpec((packed, SEQLEN), lambda s, j: (j, s)),
            pl.BlockSpec((wide, SEQLEN), lambda s, j: (j, s)),
            pl.BlockSpec((1, group, SEQLEN), lambda s, j: (j, 0, s)),
            pl.BlockSpec((half, SEQLEN), lambda s, j: (0, 0)),
            pl.BlockSpec((half, SEQLEN), lambda s, j: (0, 0)),
        ],
        out_specs=pl.BlockSpec((packed, SEQLEN), lambda s, j: (j, s)),
        out_shape=jax.ShapeDtypeStruct((columns, rows), LOW),
        scratch_shapes=[
            pltpu.VMEM((HD, SEQLEN), jnp.float32),
            pltpu.VMEM((HD, SEQLEN), jnp.float32),
        ],
        cost_estimate=pl.CostEstimate(
            flops=10 * rows * SEQLEN * kv_heads * wide,
            transcendentals=rows * SEQLEN * kv_heads * group,
            bytes_accessed=6 << 20,
        ),
        name="attend_back",
    )(projected, d_heads, totals, cos_rows, sin_rows)


def project_and_norm(all_heads, weights, gathered, gain_vec):
    groups, rows, group_columns = all_heads.shape
    (first, first_offsets), (second, second_offsets) = weights
    parts, _, depth, half = first.shape
    width = 2 * half
    tile = rows // groups
    places = jnp.stack([lax.axis_index(TP), lax.axis_index(DP)])

    def kernel(
        at_ref,
        heads_ref,
        first_ref,
        second_ref,
        tokens_ref,
        gain_ref,
        hidden_ref,
        normed_ref,
        turned_ref,
        weight_ref,
        wide_ref,
    ):
        step = pl.program_id(0)

        @pl.when(step == 0)
        def _():
            for side, part_ref, offsets in (
                (0, first_ref, first_offsets),
                (half, second_ref, second_offsets),
            ):
                for part in range(parts):
                    for g in range(groups):
                        start = g * group_columns + (at_ref[1] ^ offsets[part]) * depth
                        at = pl.ds(pl.multiple_of(start, depth), depth)
                        weight_ref[at, side : side + half] = part_ref[part, g]

        for g in range(groups):
            wide_ref[:, g * group_columns : (g + 1) * group_columns] = heads_ref[g]
        hidden = tokens_ref[0].astype(jnp.float32) + jnp.dot(
            wide_ref[...], weight_ref[...], preferred_element_type=jnp.float32
        )
        row_scale = lax.rsqrt(jnp.mean(hidden * hidden, axis=-1, keepdims=True) + EPS)
        normed = hidden * row_scale * gain_ref[...].astype(jnp.float32)
        normed_ref[...] = normed.astype(LOW)
        turned_ref[...] = normed.T.astype(LOW)

        @pl.when(step == at_ref[0])
        def _():
            hidden_ref[...] = hidden

    return pl.pallas_call(
        kernel,
        grid_spec=pltpu.PrefetchScalarGridSpec(
            num_scalar_prefetch=1,
            grid=(groups,),
            in_specs=[
                pl.BlockSpec((groups, tile, group_columns), lambda i, at_ref: (0, i, 0)),
                pl.BlockSpec(first.shape, lambda i, at_ref: (0, 0, 0, 0)),
                pl.BlockSpec(second.shape, lambda i, at_ref: (0, 0, 0, 0)),
                pl.BlockSpec((1, tile, width), lambda i, at_ref: (i, 0, 0)),
                pl.BlockSpec((1, width), lambda i, at_ref: (0, 0)),
            ],
            out_specs=[
                pl.BlockSpec((tile, width), lambda i, at_ref: (0, 0)),
                pl.BlockSpec((tile, width), lambda i, at_ref: (i, 0)),
                pl.BlockSpec((width, tile), lambda i, at_ref: (0, i)),
            ],
            scratch_shapes=[
                pltpu.VMEM((groups * group_columns, width), LOW),
                pltpu.VMEM((tile, groups * group_columns), LOW),
            ],
        ),
        out_shape=[
            jax.ShapeDtypeStruct((tile, width), jnp.float32),
            jax.ShapeDtypeStruct((rows, width), LOW),
            jax.ShapeDtypeStruct((width, rows), LOW),
        ],
        cost_estimate=pl.CostEstimate(
            flops=2 * rows * width * width, transcendentals=rows, bytes_accessed=24 << 20
        ),
        name="project_and_norm",
    )(places, all_heads, first, second, gathered, gain_vec.reshape(1, -1))


def gated_up(normed, w_gate, w_up):
    rows, width = normed.shape
    columns = w_gate.shape[1]
    tile = 256

    def kernel(normed_ref, gate_w_ref, up_w_ref, active_ref, turned_ref, smooth_ref, slope_ref):
        gate = jnp.dot(normed_ref[...], gate_w_ref[...], preferred_element_type=jnp.float32)
        up = jnp.dot(normed_ref[...], up_w_ref[...], preferred_element_type=jnp.float32)
        chance = jax.nn.sigmoid(gate)
        smooth = gate * chance
        active = smooth * up
        active_ref[...] = active.astype(LOW)
        turned_ref[...] = active.T.astype(LOW)
        smooth_ref[...] = smooth.astype(LOW)
        slope_ref[...] = (up * (chance * (1.0 + gate * (1.0 - chance)))).astype(LOW)

    column_block = pl.BlockSpec((rows, tile), lambda j: (0, j))
    weight_block = pl.BlockSpec((width, tile), lambda j: (0, j))
    flat = jax.ShapeDtypeStruct((rows, columns), LOW)
    return pl.pallas_call(
        kernel,
        grid=(columns // tile,),
        in_specs=[pl.BlockSpec((rows, width), lambda j: (0, 0)), weight_block, weight_block],
        out_specs=[
            column_block,
            pl.BlockSpec((tile, rows), lambda j: (j, 0)),
            column_block,
            column_block,
        ],
        out_shape=[flat, jax.ShapeDtypeStruct((columns, rows), LOW), flat, flat],
        cost_estimate=pl.CostEstimate(
            flops=4 * rows * width * columns,
            transcendentals=rows * columns,
            bytes_accessed=36 << 20,
        ),
        name="gated_up",
    )(normed, w_gate, w_up)


def gated_back(all_cot, w_down, smooth, slope):
    rows, width = all_cot.shape
    columns = w_down.shape[0]
    tile = 512

    def kernel(cot_ref, weight_ref, smooth_ref, slope_ref, d_gate_ref, d_up_ref):
        for start in range(0, tile, 256):
            here = slice(start, start + 256)
            d_active = dot_lanes(cot_ref[...], weight_ref[here, :])
            d_up_ref[:, here] = (d_active * smooth_ref[:, here].astype(jnp.float32)).astype(LOW)
            d_gate_ref[:, here] = (d_active * slope_ref[:, here].astype(jnp.float32)).astype(LOW)

    column_block = pl.BlockSpec((rows, tile), lambda j: (0, j))
    return pl.pallas_call(
        kernel,
        grid=(columns // tile,),
        in_specs=[
            pl.BlockSpec((rows, width), lambda j: (0, 0)),
            pl.BlockSpec((tile, width), lambda j: (j, 0)),
            column_block,
            column_block,
        ],
        out_specs=[column_block] * 2,
        out_shape=[jax.ShapeDtypeStruct((rows, columns), LOW)] * 2,
        cost_estimate=pl.CostEstimate(
            flops=2 * rows * width * columns, transcendentals=0, bytes_accessed=28 << 20
        ),
        name="gated_back",
    )(all_cot, w_down, smooth, slope)


def product(left, rights, folds):
    rows, depth = left.shape
    each = rights[0].shape[1]
    tile = 512
    column_steps = each // tile
    count = len(rights)
    per = count * column_steps // folds

    def kernel(left_ref, *refs):
        out_ref = refs[count]
        for k in range(count):

            def _(k=k):
                out_ref[...] = jnp.dot(
                    left_ref[...], refs[k][...], preferred_element_type=jnp.float32
                ).astype(LOW)

            if count == 1:
                _()
            else:
                pl.when(pl.program_id(0) // column_steps == k)(_)

    def right_block(k):
        return pl.BlockSpec(
            (depth, tile), lambda j: (0, jnp.clip(j - k * column_steps, 0, column_steps - 1))
        )

    return pl.pallas_call(
        kernel,
        grid=(count * column_steps,),
        in_specs=[pl.BlockSpec((rows, depth), lambda j: (0, 0))]
        + [right_block(k) for k in range(count)],
        out_specs=pl.BlockSpec((rows, tile), lambda j: (j // per, j % per)),
        out_shape=jax.ShapeDtypeStruct((rows * folds, count * each // folds), LOW),
        cost_estimate=pl.CostEstimate(
            flops=2 * rows * depth * count * each,
            transcendentals=0,
            bytes_accessed=2 * (rows * depth + (depth + rows) * count * each),
        ),
        name="product",
    )(left, *rights)


def pair_product(places, tile, first, first_weight, second, second_weight):
    rows, depth = first.shape
    columns = first_weight.shape[0]
    count = len(places)
    part = 512 if count == 1 else 256
    at = jnp.stack(places)

    def kernel(at_ref, first_ref, second_ref, first_w_ref, second_w_ref, *out_refs):
        for k, out_ref in enumerate(out_refs):
            here = (
                slice(None)
                if count == 1
                else pl.ds(pl.multiple_of(at_ref[k] * tile, tile), tile)
            )
            out_ref[...] = (
                dot_lanes(first_ref[here, :], first_w_ref[...])
                + dot_lanes(second_ref[here, :], second_w_ref[...])
            ).astype(LOW)

    held = (
        pl.BlockSpec((tile, depth), lambda j, at_ref: (at_ref[0], 0))
        if count == 1
        else pl.BlockSpec((rows, depth), lambda j, at_ref: (0, 0))
    )
    weight_block = pl.BlockSpec((part, depth), lambda j, at_ref: (j, 0))
    return pl.pallas_call(
        kernel,
        grid_spec=pltpu.PrefetchScalarGridSpec(
            num_scalar_prefetch=1,
            grid=(columns // part,),
            in_specs=[held, held, weight_block, weight_block],
            out_specs=[pl.BlockSpec((tile, part), lambda j, at_ref: (0, j))] * count,
        ),
        out_shape=[jax.ShapeDtypeStruct((tile, columns), LOW)] * count,
        cost_estimate=pl.CostEstimate(
            flops=4 * count * tile * depth * columns, transcendentals=0, bytes_accessed=20 << 20
        ),
        name="pair_product",
    )(at, first, second, first_weight, second_weight)


def projection_back(places, d_projected, weight_rows, gathered):
    columns, width = weight_rows.shape
    tile = gathered.shape[1]
    count = len(places)
    at = jnp.stack(places)

    def kernel(at_ref, d_ref, weight_ref, tokens_ref, *out_refs):
        step = pl.program_id(0)
        grads = d_ref[...].astype(jnp.float32).T.astype(LOW)
        made = jnp.dot(grads, weight_ref[...], preferred_element_type=jnp.float32).astype(LOW)
        values = tokens_ref[0].astype(jnp.float32)
        row_scale = lax.rsqrt(jnp.mean(values * values, axis=-1, keepdims=True) + EPS)
        added = jnp.sum(made.astype(jnp.float32) * values * row_scale, axis=0, keepdims=True)
        gain_ref = out_refs[count]
        gain_ref[...] = jnp.where(step == 0, added, gain_ref[...] + added)
        for k in range(count):

            @pl.when(step == k)
            def _():
                out_refs[k][...] = made

    return pl.pallas_call(
        kernel,
        grid_spec=pltpu.PrefetchScalarGridSpec(
            num_scalar_prefetch=1,
            grid=(count,),
            in_specs=[
                pl.BlockSpec((columns, tile), lambda i, at_ref: (0, at_ref[i])),
                pl.BlockSpec((columns, width), lambda i, at_ref: (0, 0)),
                pl.BlockSpec((1, tile, width), lambda i, at_ref: (at_ref[i], 0, 0)),
            ],
            out_specs=[pl.BlockSpec((tile, width), lambda i, at_ref: (0, 0))] * count
            + [pl.BlockSpec((1, width), lambda i, at_ref: (0, 0))],
        ),
        out_shape=[jax.ShapeDtypeStruct((tile, width), LOW)] * count
        + [jax.ShapeDtypeStruct((1, width), jnp.float32)],
        cost_estimate=pl.CostEstimate(
            flops=2 * count * tile * columns * width, transcendentals=0, bytes_accessed=8 << 20
        ),
        name="projection_back",
    )(at, d_projected, weight_rows, gathered)


def norm_back(values, gain_vec, base, blocks):
    rows, width = values.shape
    part = 64
    count = len(blocks)

    def kernel(values_ref, gain_ref, base_ref, *refs):
        wide_ref, low_ref, sum_ref = refs[count:]
        step = pl.program_id(0)
        upstream = sum(ref[...].astype(jnp.float32) for ref in refs[:count])
        held = values_ref[...].astype(jnp.float32)
        row_scale = lax.rsqrt(jnp.mean(held * held, axis=-1, keepdims=True) + EPS)
        scaled = held * row_scale
        added = jnp.sum(upstream * scaled, axis=0, keepdims=True)
        sum_ref[...] = jnp.where(step == 0, added, sum_ref[...] + added)
        weighted = upstream * gain_ref[...].astype(jnp.float32)
        inner = jnp.mean(weighted * scaled, axis=-1, keepdims=True)
        result = base_ref[...].astype(jnp.float32) + row_scale * (weighted - scaled * inner)
        wide_ref[...] = result
        low_ref[...] = result.astype(LOW)

    tile_block = pl.BlockSpec((part, width), lambda i: (i, 0))
    line = pl.BlockSpec((1, width), lambda i: (0, 0))
    return pl.pallas_call(
        kernel,
        grid=(rows // part,),
        in_specs=[tile_block, line, tile_block] + [tile_block] * count,
        out_specs=[tile_block, tile_block, line],
        out_shape=[
            jax.ShapeDtypeStruct((rows, width), jnp.float32),
            jax.ShapeDtypeStruct((rows, width), LOW),
            jax.ShapeDtypeStruct((1, width), jnp.float32),
        ],
        cost_estimate=pl.CostEstimate(
            flops=16 * rows * width, transcendentals=rows, bytes_accessed=10 << 20
        ),
        name="norm_back",
    )(values, gain_vec.reshape(1, -1), base, *blocks)


def exchange(make_blocks, axis):
    n = lax.axis_size(axis)
    me = lax.axis_index(axis)
    places = [(me + hop) % n for hop in range(1, n)] + [me]
    made = list(make_blocks(places[:1]))
    moved = []
    for hop in range(1, n):
        if hop == 2:
            made += make_blocks(places[1:])
        pairs = [(i, (i + hop) % n) for i in range(n)]
        moved.append(lax.ppermute(made[hop - 1], axis, pairs))
    return moved + made[n - 1 :]


def place_blocks(halves, axis):
    (first, first_offsets), (second, second_offsets) = halves
    some, rows, half = first[0].shape
    parts = 2 * some

    def kernel(at_ref, *refs):
        out_ref = refs[4]
        k = pl.program_id(0)
        for side, offsets in enumerate((first_offsets, second_offsets)):
            columns = slice(side * half, (side + 1) * half)
            late = functools.reduce(
                jnp.logical_or, [k == offset for offset in offsets[some:]]
            )
            early_ref, late_ref = refs[2 * side : 2 * side + 2]
            out_ref[:, columns] = jnp.where(late, late_ref[0], early_ref[0]).astype(jnp.float32)

    def entry(offsets):
        def index(k, at_ref):
            found = 0
            for at, offset in enumerate(offsets):
                found = jnp.where(k == offset, at, found)
            return (found, 0, 0)

        return pl.BlockSpec((1, rows, half), index)

    specs = []
    for offsets in (first_offsets, second_offsets):
        specs += [entry(offsets[:some]), entry(offsets[some:])]
    return pl.pallas_call(
        kernel,
        grid_spec=pltpu.PrefetchScalarGridSpec(
            num_scalar_prefetch=1,
            grid=(parts,),
            in_specs=specs,
            out_specs=pl.BlockSpec((rows, 2 * half), lambda k, at_ref: (at_ref[0] ^ k, 0)),
        ),
        out_shape=jax.ShapeDtypeStruct((parts * rows, 2 * half), jnp.float32),
        cost_estimate=pl.CostEstimate(
            flops=0, transcendentals=0, bytes_accessed=12 * parts * rows * half
        ),
        name="place_blocks",
    )(lax.axis_index(axis).reshape(1), *first, *second)


def unpack_attention(shared, q_columns, k_columns, folds):
    rows, columns = shared.shape
    block = rows // folds
    kv_heads = k_columns // HD
    wide = q_columns // kv_heads
    packed = wide + 2 * HD
    end = kv_heads * packed

    def kernel(shared_ref, query_ref, key_ref, value_ref, output_ref):
        for j in range(kv_heads):
            start = j * packed
            query_ref[:, j * wide : (j + 1) * wide] = shared_ref[
                :, start : start + wide
            ].astype(jnp.float32)
            for at, ref in ((start + wide, key_ref), (start + wide + HD, value_ref)):
                ref[:, j * HD : (j + 1) * HD] = shared_ref[:, at : at + HD].astype(jnp.float32)
        output_ref[...] = shared_ref[:, end:].astype(jnp.float32)

    narrow = pl.BlockSpec((block, k_columns), lambda p: (p, 0))
    return pl.pallas_call(
        kernel,
        grid=(folds,),
        in_specs=[pl.BlockSpec((block, columns), lambda p: (p, 0))],
        out_specs=[
            pl.BlockSpec((block, q_columns), lambda p: (p, 0)),
            narrow,
            narrow,
            pl.BlockSpec((block, columns - end), lambda p: (0, p)),
        ],
        out_shape=[
            jax.ShapeDtypeStruct((rows, q_columns), jnp.float32),
            jax.ShapeDtypeStruct((rows, k_columns), jnp.float32),
            jax.ShapeDtypeStruct((rows, k_columns), jnp.float32),
            jax.ShapeDtypeStruct((block, (columns - end) * folds), jnp.float32),
        ],
        cost_estimate=pl.CostEstimate(
            flops=0, transcendentals=0, bytes_accessed=6 * rows * columns
        ),
        name="unpack_attention",
    )(shared)


def add_all(blocks):
    return sum(block.astype(jnp.float32) for block in blocks)


def row_major(array):
    return with_layout_constraint(array, Layout(major_to_minor=tuple(range(array.ndim))))


def split_columns(array, parts):
    if parts == 1:
        return array
    rows, columns = array.shape[0], array.shape[1] // parts
    return array.reshape(rows, parts, columns).swapaxes(0, 1).reshape(parts * rows, columns)


def join_columns(array, parts):
    if parts == 1:
        return array
    rows, columns = array.shape[0] // parts, array.shape[1]
    return array.reshape(parts, rows, columns).swapaxes(0, 1).reshape(rows, parts * columns)


def block(
    tokens,
    cotangent,
    norm1_gain,
    w_query,
    w_key,
    w_value,
    w_output,
    norm2_gain,
    w_gate,
    w_up,
    w_down,
):
    n_dp = lax.axis_size(DP)
    own_rows, width = tokens.shape
    depth = w_output.shape[0] // n_dp
    q_columns, k_columns = w_query.shape[1], w_key.shape[1]
    kv_heads = k_columns // HD
    group = q_columns // k_columns
    ff_columns = w_gate.shape[1]
    ff_folds = width // w_down.shape[0]
    folds = width // w_output.shape[0]
    nothing = scatter_sum(tokens[:, :128] * 0, DP)[0, 0]
    gathered = lax.all_gather(tokens, TP, axis=0)
    own_part = lax.dynamic_slice_in_dim(w_output, lax.axis_index(DP) * depth, depth, 0)
    output_part = lax.all_gather(own_part, TP, axis=0)
    all_output = cube_gather(output_part, DP)
    cos_table, sin_table = rope_tables(SEQLEN, HD)
    cos_rows, sin_rows = cos_table.T, sin_table.T
    pieces = []
    for j in range(kv_heads):
        pieces.append(w_query[:, j * group * HD : (j + 1) * group * HD].T)
        pieces.append(w_key[:, j * HD : (j + 1) * HD].T)
        pieces.append(w_value[:, j * HD : (j + 1) * HD].T)
    weight_rows = jnp.concatenate(pieces, axis=0)
    normed1, projected = norm_project(
        gathered, norm1_gain, weight_rows, cos_rows, sin_rows, group
    )
    heads_out, heads_rows, totals = attend(projected, group)
    all_heads = lax.all_gather(heads_out, TP, axis=0)
    all_cot = gather_rows(cotangent, TP)
    hidden_state, normed2, normed2_rows = project_and_norm(
        all_heads, all_output, gathered, norm2_gain.astype(jnp.float32) + nothing.astype(jnp.float32)
    )
    activated, active_rows, smooth, slope = gated_up(normed2, w_gate, w_up)
    mlp_part = product(activated, [w_down], 1)
    half_width = width // 2

    def part_of(columns):
        return lambda places: [
            lax.dynamic_slice(mlp_part, (place * own_rows, columns), (own_rows, half_width))
            for place in places
        ]

    first_half = exchange(part_of(0), TP)
    second_half = exchange(part_of(half_width), TP)
    output = (
        hidden_state
        + jnp.concatenate([add_all(first_half), add_all(second_half)], axis=1)
    ).astype(LOW)
    d_gate, d_up = gated_back(all_cot, w_down, smooth, slope)
    grad_down = product(active_rows, [all_cot], ff_folds)
    part_down = scatter_sum(grad_down, DP)
    dn2_blocks = exchange(
        lambda places: pair_product(places, own_rows, d_gate, w_gate, d_up, w_up), TP
    )
    gate_up_grads = product(normed2_rows, [d_gate, d_up], 1)
    part_gate_up = scatter_sum(gate_up_grads, DP)
    d_state, state_low, gain_two = norm_back(hidden_state, norm2_gain, cotangent, dn2_blocks)
    d_state_low = gather_rows(state_low, TP)
    d_heads_rows = contract_cols(w_output, d_state_low).astype(LOW)
    d_projected = attend_back(projected, d_heads_rows, totals, cos_rows, sin_rows)
    gains = []

    def dn1_blocks_of(places):
        *made, gain = projection_back(places, d_projected, weight_rows, gathered)
        gains.append(gain)
        return made

    dn1_blocks = exchange(dn1_blocks_of, TP)
    gain_sums = cube_sum(jnp.concatenate([sum(gains), gain_two], axis=1)[0], (DP, TP))
    gain_one_sum, gain_two_sum = gain_sums[:width], gain_sums[width:]
    grad_qkv = lax.dot_general(
        normed1,
        d_projected,
        (((0,), (1,)), ((), ())),
        preferred_element_type=jnp.float32,
    ).astype(LOW)
    grad_output = jnp.dot(heads_rows, d_state_low, preferred_element_type=jnp.float32).astype(LOW)
    low_attn = row_major(
        jnp.concatenate([grad_qkv, split_columns(grad_output, folds)], axis=1)
    )
    part_attn = scatter_sum(low_attn, DP)
    down_halves = cube_gather(part_down, DP, join=False)
    full_down = join_columns(place_blocks(down_halves, DP), ff_folds)
    up_halves = cube_gather(part_gate_up[:, ff_columns:], DP, join=False)
    full_up = place_blocks(up_halves, DP)
    shared_gate = row_major(gather_rows(part_gate_up[:, :ff_columns], DP))
    shared_attn = row_major(gather_rows(part_attn, DP))
    _, input_grad, _ = norm_back(tokens, norm1_gain, d_state, dn1_blocks)
    full_gate = shared_gate.astype(jnp.float32)
    full_query, full_key, full_value, full_output = unpack_attention(
        shared_attn, q_columns, k_columns, folds
    )
    return (
        output,
        input_grad,
        gain_one_sum,
        full_query,
        full_key,
        full_value,
        full_output,
        gain_two_sum,
        full_gate,
        full_up,
        full_down,
    )


ROWS, COLUMNS, HIDDEN = P((DP, TP), None), P(None, TP), P(TP, None)


def solution(mesh):
    return jax.shard_map(
        block,
        mesh=mesh,
        in_specs=(ROWS, ROWS, P(), COLUMNS, COLUMNS, COLUMNS, HIDDEN, P(), COLUMNS, COLUMNS, HIDDEN),
        out_specs=(ROWS, ROWS, P(), COLUMNS, COLUMNS, COLUMNS, HIDDEN, P(), COLUMNS, COLUMNS, HIDDEN),
        check_vma=False,
    )
```
